128 devices in a mesh: dp: 8 (over z, core), expert: 16 (over x, y).
Axes of the slice: x: 4, y: 4, z: 4, core: 2. Of those that a mesh axis runs over, the one named last changes fastest.
Arguments:
- tokens: bfloat16 [4096, 2048], P(('dp', 'expert')), may hold values from -6 to 6
- norm_gain: float32 [2, 2048], replicated, may hold values from 0.5 to 1.5
- routes: int32 [2, 4096, 8], P(None, ('dp', 'expert')), may hold values from 0 to 127, all different within a row; in each aligned block of 32 rows (0 to 31, 32 to 63, ..., all dimensions but the last counted through in order) at most 3 rows name the same one
- gates: float32 [2, 4096, 8], P(None, ('dp', 'expert')), may hold values from 0.03 to 0.3
- placement: int32 [2, 128], replicated, may hold values from 0 to 127, each once within a row
- w_in: bfloat16 [2, 128, 2048, 1536], P(None, ('dp', 'expert')), may hold values from -0.125 to 0.125
- in_scale: float32 [2, 128, 16, 12], P(None, ('dp', 'expert')), may hold values from 0.5 to 2
- w_out: bfloat16 [2, 128, 768, 2048], P(None, ('dp', 'expert')), may hold values from -0.21875 to 0.21875
- out_scale: float32 [2, 128, 6, 16], P(None, ('dp', 'expert')), may hold values from 0.5 to 2
Outputs:
- stream: bfloat16 [4096, 2048], P(('dp', 'expert'))
The draws below stay inside these ranges and needn't reach their ends.
Inputs may be any that keep to these rules, and one draw needn't show every extreme that they name: `routes`: each token names 8 different experts in each layer; among the tokens of one device in one layer no expert is named more than 3 times, a bound that some block reaches. `placement`: each layer's row is a permutation of the experts; device position p is p's index along dp+expert, dp slowest.
All inputs are finite; a program needn't handle non-finite values.
Results may differ from the reference program's by a relative error of at most 0.009.
Values may be sent and summed in bfloat16 or wider, within the bound.
No kernel may reach another device: no remote copies, remote signals or barrier semaphores. Data moves between devices by JAX's collectives and lax.ppermute only.
A program may use at most 128 MiB of HBM per device.

```python
import math
import jax
import jax.numpy as jnp
import numpy as np
from jax import lax

D = 2048
FF = 768
TOP = 8
QBLK = 128
LAYERS = 2
TOK_DEV = 32
EXPERTS = 128
TOKENS = 4096
CAP = 3


def levels(stream_key, shape, shards, smallest, largest):
    def one(axis_at, shards_of):
        draws = jax.random.uniform(jax.random.fold_in(jax.random.fold_in(stream_key, 6), axis_at), (shards_of,), jnp.float32, smallest / len(shards), largest / len(shards))
        return jnp.repeat(jnp.exp(draws), shape[axis_at] // shards_of).reshape((-1,) + (1,) * (len(shape) - axis_at - 1))

    gain = one(*shards[0])
    for cut in shards[1:]:
        gain = gain * one(*cut)
    return gain


def shared_out(rng, own, number, rows, count, top, most, lean):
    order = jax.random.permutation(rng, count)
    crowded, common = load_shares(count, rows * top, most, lean, True), load_shares(count, rows * top, most, lean, False)
    places = jnp.arange(count)

    def named(tallies, rotation):
        used = int((tallies > 0).sum())
        fixed = max(1, used // 4)
        shifted = fixed + (places - fixed + rotation * (used - fixed)) % max(1, count - fixed)
        return jnp.zeros((count,), jnp.int32).at[order[jnp.where(places < fixed, places, shifted)]].set(jnp.asarray(tallies, jnp.int32))

    tallies = jnp.where(number % 4 == 0, named(crowded, number // 4), named(common, number - number // 4 - 1))
    mixed = jax.random.permutation(jax.random.fold_in(own, 3), count)
    donor, taker = mixed[0:count // 2 * 2:2], mixed[1:count // 2 * 2:2]
    room = jnp.minimum(tallies[donor] - 1, most - tallies[taker]) // 2
    room = jnp.where((donor == order[0]) | (taker == order[0]) | (tallies[taker] == 0), 0, jnp.maximum(room, 0))
    shifted = jax.random.randint(jax.random.fold_in(own, 4), (count // 2,), 0, 1 << 20) % (room + 1)
    tallies = tallies.at[donor].add(-shifted).at[taker].add(shifted)
    labels = jnp.searchsorted(jnp.cumsum(tallies), jnp.arange(rows * top), side="right").astype(jnp.int32)
    table = labels.reshape(top, rows).T
    table = table[jax.random.permutation(jax.random.fold_in(own, 1), rows)]
    rotation = jax.random.randint(jax.random.fold_in(own, 2), (rows, 1), 0, top)
    return jnp.take_along_axis(table, (jnp.arange(top)[None, :] + rotation) % top, axis=1)


def load_shares(number_of, total, most, skew, full):
    weights = [(1 << 20) // math.isqrt(standing ** skew) + 1 for standing in range(1, number_of + 1)]
    largest = most if full else min(most, max(-(-total // number_of), total * weights[0] // sum(weights)))
    least = 1 if total - largest >= number_of - 1 else 0
    holding, rest = [largest] + [least] * (number_of - 1), total - largest - least * (number_of - 1)
    while rest > 0:
        movable = [i for i in range(1, number_of) if holding[i] < largest] or [i for i in range(1, number_of) if holding[i] < most]
        pool, remaining = sum([weights[i] for i in movable]), rest
        for i in movable:
            extra = min(most - holding[i], max(1, remaining * weights[i] // pool), rest)
            holding[i] = holding[i] + extra
            rest = rest - extra
    return np.array(holding)


def scatter_about(stream_key, shape, deviation, reach, split=(), kind=jnp.bfloat16):
    level = levels(stream_key, shape, split, -0.22, 0.18) if split else 1.0
    entries = jax.random.normal(stream_key, shape, jnp.float32) * deviation * level
    return jnp.minimum(jnp.maximum(entries, -reach), reach).astype(kind)


def setup_inputs(seed: int = 0) -> dict:
    arg_keys = jax.random.split(jax.random.key(seed), 10)
    tokens = scatter_about(arg_keys[0], (TOKENS, D), 1.0, 6.0, ((0, 128),))
    norm_gain = jnp.clip(jax.random.uniform(arg_keys[1], (LAYERS, D), jnp.float32, 0.5, 1.5), 0.5, 1.5)
    routes_keys = jax.random.split(jax.random.fold_in(arg_keys[2], 1), LAYERS * TOKENS // TOK_DEV)
    routes_turns = jax.random.permutation(jax.random.fold_in(arg_keys[2], 3), LAYERS * TOKENS // TOK_DEV)
    routes = jax.vmap(lambda own, number: shared_out(jax.random.fold_in(arg_keys[2], 2), own, number, TOK_DEV, EXPERTS, TOP, CAP, 2))(routes_keys, routes_turns).reshape((LAYERS, TOKENS, TOP))
    gates = jnp.clip(jnp.exp(math.log(0.3) - 2.3025852 * jax.random.uniform(arg_keys[3], (LAYERS, TOKENS, TOP), jnp.float32) ** levels(arg_keys[3], (LAYERS, TOKENS, TOP), ((1, 128),), -0.2, 0.2)), 0.03, 0.3)
    placement = jax.vmap(lambda own: jax.random.permutation(own, EXPERTS))(jax.random.split(arg_keys[4], LAYERS)).reshape((LAYERS, EXPERTS)).astype(jnp.int32)
    w_in = scatter_about(arg_keys[5], (LAYERS, EXPERTS, D, 2 * FF), D ** -0.5, 0.125, ((1, 128),))
    in_scale = jnp.clip(jnp.exp(math.log(2.0) - 1.3862944 * jax.random.uniform(arg_keys[6], (LAYERS, EXPERTS, D // QBLK, 2 * FF // QBLK), jnp.float32) ** levels(arg_keys[6], (LAYERS, EXPERTS, D // QBLK, 2 * FF // QBLK), ((1, 128),), -0.2, 0.2)), 0.5, 2.0)
    w_out = scatter_about(arg_keys[7], (LAYERS, EXPERTS, FF, D), FF ** -0.5, 0.21875, ((1, 128),))
    out_scale = jnp.clip(jnp.exp(math.log(2.0) - 1.3862944 * jax.random.uniform(arg_keys[8], (LAYERS, EXPERTS, FF // QBLK, D // QBLK), jnp.float32) ** levels(arg_keys[8], (LAYERS, EXPERTS, FF // QBLK, D // QBLK), ((1, 128),), -0.2, 0.2)), 0.5, 2.0)
    return {"tokens": tokens, "norm_gain": norm_gain, "routes": routes, "gates": gates, "placement": placement, "w_in": w_in, "in_scale": in_scale, "w_out": w_out, "out_scale": out_scale}


epsilon = 1e-06

def dequantize(quantized, scales, block_size):
    height, breadth = quantized.shape
    blocks = quantized.astype(jnp.float32).reshape(height // block_size, block_size, breadth // block_size, block_size)
    return (blocks * scales[:, None, :, None]).reshape(height, breadth).astype(jnp.bfloat16)

def reference(tokens, norm_gain, routes, gates, placement, w_in, in_scale, w_out, out_scale):
    stream = tokens
    assigned = TOK_DEV * TOP
    expert_ids = jnp.arange(EXPERTS, dtype=jnp.int32)
    for layer_index in range(LAYERS):
        stream_f = stream.astype(jnp.float32)
        normed = (stream_f * lax.rsqrt(lax.optimization_barrier(jnp.mean(stream_f * stream_f, axis=-1, keepdims=True)) + epsilon) * norm_gain[layer_index]).astype(jnp.bfloat16)
        holder = jnp.argsort(placement[layer_index]).astype(jnp.int32)
        chosen = routes[layer_index].reshape(EXPERTS, assigned).astype(jnp.int32)
        onehot = (chosen[:, :, None] == expert_ids[None, None, :]).astype(jnp.int32)
        ranks = lax.optimization_barrier(jnp.sum((jnp.cumsum(onehot, axis=1) - 1) * onehot, axis=2)).astype(jnp.int32)
        source = jnp.arange(EXPERTS, dtype=jnp.int32)[:, None]
        slot_rows = (source * CAP + ranks).reshape(-1).astype(jnp.int32)
        token_of = (source * TOK_DEV + jnp.arange(assigned, dtype=jnp.int32)[None, :] // TOP).reshape(-1).astype(jnp.int32)
        flat_expert = chosen.reshape(-1)
        table = jnp.full((EXPERTS, EXPERTS * CAP), TOKENS, jnp.int32).at[flat_expert, slot_rows].set(token_of)
        weight_table = jnp.zeros((EXPERTS, EXPERTS * CAP), jnp.float32).at[flat_expert, slot_rows].set(gates[layer_index].reshape(-1))
        padded = jnp.concatenate([normed, jnp.zeros((1, D), jnp.bfloat16)], axis=0)

        def expert_step(total, expert):
            holder_row = holder[expert]
            in_weight = dequantize(w_in[layer_index, holder_row], in_scale[layer_index, holder_row], QBLK)
            out_weight = dequantize(w_out[layer_index, holder_row], out_scale[layer_index, holder_row], QBLK)
            picked = table[expert]
            token_rows = padded[picked]
            gate_up = jnp.dot(token_rows, in_weight, preferred_element_type=jnp.float32)
            hidden = (jax.nn.silu(gate_up[:, :FF]) * gate_up[:, FF:]).astype(jnp.bfloat16)
            answer = jnp.dot(hidden, out_weight, preferred_element_type=jnp.float32).astype(jnp.bfloat16)
            total = total.at[picked].add(weight_table[expert][:, None] * answer.astype(jnp.float32))
            return (total, None)
        total, _ = lax.scan(expert_step, jnp.zeros((TOKENS + 1, D), jnp.float32), expert_ids)
        stream = (stream_f + total[:TOKENS]).astype(jnp.bfloat16)
    return stream
```

```python
import functools

import jax
import jax.numpy as jnp
from jax import lax
from jax.experimental import pallas as pl
from jax.experimental.pallas import tpu as pltpu
from jax.sharding import PartitionSpec as P

AXES = ("dp", "expert")
QBLK = 128
CAP = 3
PIECES = 8
GROUP = 32
EPS = 1e-06
MIB = 1 << 20


def fold_matrix():
    row = lax.broadcasted_iota(jnp.int32, (GROUP * PIECES, GROUP * PIECES), 0)
    col = lax.broadcasted_iota(jnp.int32, (GROUP * PIECES, GROUP * PIECES), 1)
    return jnp.where(col == (row & (PIECES - 1)) * GROUP + (row >> 3), 1.0, 0.0).astype(jnp.bfloat16)


def unfold_matrix():
    row = lax.broadcasted_iota(jnp.int32, (GROUP * PIECES, GROUP * PIECES), 0)
    col = lax.broadcasted_iota(jnp.int32, (GROUP * PIECES, GROUP * PIECES), 1)
    return jnp.where(col == (row & (GROUP - 1)) * PIECES + (row >> 5), 1.0, 0.0).astype(jnp.bfloat16)


def unfold_rows(slab_ref, rows_ref):
    piece = slab_ref.shape[1]
    span = GROUP * PIECES
    unfold = unfold_matrix()
    for b in range(slab_ref.shape[0] // span):
        block = jnp.dot(
            unfold, slab_ref[b * span : (b + 1) * span, :], preferred_element_type=jnp.float32
        ).astype(jnp.bfloat16)
        for p in range(PIECES):
            rows_ref[b * GROUP : (b + 1) * GROUP, p * piece : (p + 1) * piece] = block[
                p * GROUP : (p + 1) * GROUP
            ]


def fold_rows(stack_ref, slab_ref):
    span = GROUP * PIECES
    fold = fold_matrix()
    for b in range(slab_ref.shape[0] // span):
        slab_ref[b * span : (b + 1) * span, :] = jnp.dot(
            fold, stack_ref[b * span : (b + 1) * span, :], preferred_element_type=jnp.float32
        ).astype(jnp.bfloat16)


def stack_piece(stack_ref, values, p):
    span = GROUP * PIECES
    for b in range(values.shape[0] // GROUP):
        stack_ref[b * span + p * GROUP : b * span + (p + 1) * GROUP, :] = values[
            b * GROUP : (b + 1) * GROUP
        ]


def slot_tables(routes_t, place_row, gates_t):
    tokens = routes_t.shape[1]
    devices = place_row.shape[1]
    slots = devices * CAP
    home = lax.broadcasted_iota(jnp.int32, (devices, slots), 0)
    slot = lax.broadcasted_iota(jnp.int32, (devices, slots), 1)
    low = home * CAP
    widen = jnp.where((slot >= low) & (slot < low + CAP), 1.0, 0.0).astype(jnp.bfloat16)
    place = jnp.dot(
        jnp.broadcast_to(place_row.astype(jnp.float32), (8, devices)).astype(jnp.bfloat16),
        widen,
        preferred_element_type=jnp.float32,
    )[:1]
    rank_of = jnp.dot(
        jnp.broadcast_to(
            lax.broadcasted_iota(jnp.int32, (1, devices), 1).astype(jnp.float32), (8, devices)
        ).astype(jnp.bfloat16),
        widen,
        preferred_element_type=jnp.float32,
    )[:1]
    order = lax.broadcasted_iota(jnp.int32, (1, slots), 1).astype(jnp.float32) - rank_of * CAP
    chosen = jnp.transpose(routes_t.astype(jnp.float32))
    gate = None if gates_t is None else jnp.transpose(gates_t)
    taken = jnp.zeros((tokens, slots), jnp.float32)
    weight = jnp.zeros((tokens, slots), jnp.float32)
    for k in range(chosen.shape[1]):
        same = chosen[:, k : k + 1] == place
        taken = jnp.where(same, 1.0, taken)
        if gate is not None:
            weight = jnp.where(same, gate[:, k : k + 1], weight)
    later = lax.broadcasted_iota(jnp.int32, (tokens, tokens), 0)
    earlier = lax.broadcasted_iota(jnp.int32, (tokens, tokens), 1)
    before = jnp.where(earlier < later, 1.0, 0.0).astype(jnp.bfloat16)
    ranks = jnp.dot(before, taken.astype(jnp.bfloat16), preferred_element_type=jnp.float32)
    mine = ranks == order
    return jnp.where(mine, taken, 0.0), jnp.where(mine, weight, 0.0)


def normalise(stream_f, gain):
    scale = lax.rsqrt(jnp.mean(stream_f * stream_f, axis=-1, keepdims=True) + EPS)
    return (stream_f * scale * gain).astype(jnp.bfloat16)


def send_rows(select, normed, stack_ref, slab_ref):
    piece = slab_ref.shape[1]
    pick = jnp.transpose(select).astype(jnp.bfloat16)
    for p in range(PIECES):
        rows = jnp.dot(
            pick, normed[:, p * piece : (p + 1) * piece], preferred_element_type=jnp.float32
        ).astype(jnp.bfloat16)
        stack_piece(stack_ref, rows, p)
    fold_rows(stack_ref, slab_ref)


def mix(weight, slab_ref, rows_ref):
    unfold_rows(slab_ref, rows_ref)
    high = weight.astype(jnp.bfloat16)
    low = (weight - high.astype(jnp.float32)).astype(jnp.bfloat16)
    both = jnp.dot(
        jnp.concatenate([high, low], axis=0), rows_ref[...], preferred_element_type=jnp.float32
    )
    tokens = weight.shape[0]
    return both[:tokens] + both[tokens:]


def first_kernel(tokens_ref, gain_ref, routes_ref, place_ref, slab_ref, stack_ref):
    select, _ = slot_tables(routes_ref[0], place_ref[0:1, :], None)
    normed = normalise(tokens_ref[...].astype(jnp.float32), gain_ref[0:1, :])
    send_rows(select, normed, stack_ref, slab_ref)


def middle_kernel(
    layer, slab_in, stream_ref, gain_ref, routes_ref, gates_ref, place_ref,
    slab_ref, out_ref, rows_ref, stack_ref,
):
    _, weight = slot_tables(routes_ref[layer], place_ref[layer : layer + 1, :], gates_ref[layer])
    select, _ = slot_tables(routes_ref[layer + 1], place_ref[layer + 1 : layer + 2, :], None)
    mixed = mix(weight, slab_in, rows_ref)
    stream = (stream_ref[...].astype(jnp.float32) + mixed).astype(jnp.bfloat16)
    out_ref[...] = stream
    normed = normalise(stream.astype(jnp.float32), gain_ref[layer + 1 : layer + 2, :])
    send_rows(select, normed, stack_ref, slab_ref)


def last_kernel(
    layer, slab_in, stream_ref, routes_ref, gates_ref, place_ref, out_ref, rows_ref
):
    _, weight = slot_tables(routes_ref[layer], place_ref[layer : layer + 1, :], gates_ref[layer])
    mixed = mix(weight, slab_in, rows_ref)
    out_ref[...] = (stream_ref[...].astype(jnp.float32) + mixed).astype(jnp.bfloat16)


def dequant_kernel(scale_ref, w_ref, out_ref):
    layer, step = pl.program_id(0), pl.program_id(1)
    rows, cols = out_ref.shape[1], out_ref.shape[2]
    per_step = rows // QBLK
    for i in range(per_step):
        for j in range(cols // QBLK):
            scale = scale_ref[layer, step * per_step + i, j]
            at = (slice(i * QBLK, (i + 1) * QBLK), slice(j * QBLK, (j + 1) * QBLK))
            out_ref[(0,) + at] = (w_ref[(0, 0) + at].astype(jnp.float32) * scale).astype(
                jnp.bfloat16
            )


def dequant(weights, scales):
    layers, _, height, width = weights.shape
    block = 256
    return pl.pallas_call(
        dequant_kernel,
        grid=(layers, height // block),
        in_specs=[
            pl.BlockSpec(memory_space=pltpu.SMEM),
            pl.BlockSpec((1, 1, block, width), lambda l, i: (l, 0, i, 0)),
        ],
        out_specs=pl.BlockSpec((1, block, width), lambda l, i: (l, i, 0)),
        out_shape=jax.ShapeDtypeStruct((layers, height, width), jnp.bfloat16),
        cost_estimate=pl.CostEstimate(
            flops=weights.size, bytes_accessed=4 * weights.size, transcendentals=0
        ),
        name="dequant",
    )(scales[:, 0], weights)


def expert_kernel(
    layer, slab_in, win_hbm, wout_hbm, slab_ref, x_ref, win, wout, hid, stack_ref, sems
):
    width, gated = win.shape
    ff = gated // 2
    chunk = 256
    loads = []
    for n in range(ff // chunk):
        for half in range(2):
            cols = pl.ds(half * ff + n * chunk, chunk)
            loads.append(
                pltpu.make_async_copy(
                    win_hbm.at[layer, :, cols], win.at[:, cols], sems.at[len(loads)]
                )
            )
    for m in range(PIECES):
        cols = pl.ds(m * chunk, chunk)
        loads.append(
            pltpu.make_async_copy(
                wout_hbm.at[layer, :, cols], wout.at[:, cols], sems.at[len(loads)]
            )
        )
    for load in loads:
        load.start()
    unfold_rows(slab_in, x_ref)
    at = 0
    for n in range(ff // chunk):
        loads[at].wait()
        gate = jnp.dot(
            x_ref[...], win[:, n * chunk : (n + 1) * chunk], preferred_element_type=jnp.float32
        )
        loads[at + 1].wait()
        up = jnp.dot(
            x_ref[...],
            win[:, ff + n * chunk : ff + (n + 1) * chunk],
            preferred_element_type=jnp.float32,
        )
        at += 2
        hid[:, n * chunk : (n + 1) * chunk] = (gate / (1.0 + jnp.exp(-gate)) * up).astype(
            jnp.bfloat16
        )
    for m in range(PIECES):
        loads[at].wait()
        at += 1
        answer = jnp.dot(
            hid[...], wout[:, m * chunk : (m + 1) * chunk], preferred_element_type=jnp.float32
        ).astype(jnp.bfloat16)
        stack_piece(stack_ref, answer, m)
    fold_rows(stack_ref, slab_ref)


VM = pl.BlockSpec(memory_space=pltpu.VMEM)


def expert(layer, slab, in_weight, out_weight):
    rows, piece = slab.shape
    slots = rows // PIECES
    _, width, gated = in_weight.shape
    ff = gated // 2
    return pl.pallas_call(
        functools.partial(expert_kernel, layer),
        in_specs=[VM, pl.BlockSpec(memory_space=pl.ANY), pl.BlockSpec(memory_space=pl.ANY)],
        out_specs=VM,
        out_shape=jax.ShapeDtypeStruct(slab.shape, jnp.bfloat16),
        scratch_shapes=[
            pltpu.VMEM((slots, width), jnp.bfloat16),
            pltpu.VMEM((width, gated), jnp.bfloat16),
            pltpu.VMEM((ff, width), jnp.bfloat16),
            pltpu.VMEM((slots, ff), jnp.bfloat16),
            pltpu.VMEM(slab.shape, jnp.bfloat16),
            pltpu.SemaphoreType.DMA((2 * (ff // 256) + PIECES,)),
        ],
        compiler_params=pltpu.CompilerParams(vmem_limit_bytes=40 * MIB),
        cost_estimate=pl.CostEstimate(
            flops=6 * slots * width * ff,
            bytes_accessed=6 * width * ff + 4 * slots * width,
            transcendentals=slots * ff,
        ),
        name="expert",
    )(slab, in_weight, out_weight)


def exchange(slab, devices):
    split = slab.reshape(devices, slab.shape[0] // devices, slab.shape[1])
    moved = lax.all_to_all(split, AXES, split_axis=0, concat_axis=0, tiled=True)
    return moved.reshape(slab.shape)


def shards(tokens, norm_gain, routes, gates, placement, w_in, in_scale, w_out, out_scale):
    count, width = tokens.shape
    layers, devices = placement.shape
    slots = devices * CAP
    piece = width // PIECES
    routes_t = jnp.swapaxes(routes, 1, 2)
    gates_t = jnp.swapaxes(gates, 1, 2)
    slab_type = jax.ShapeDtypeStruct((slots * PIECES, piece), jnp.bfloat16)
    stream_type = jax.ShapeDtypeStruct((count, width), jnp.bfloat16)
    rows = pltpu.VMEM((slots, width), jnp.bfloat16)
    stack = pltpu.VMEM((slots * PIECES, piece), jnp.bfloat16)
    params = pltpu.CompilerParams(vmem_limit_bytes=24 * MIB)

    slab = pl.pallas_call(
        first_kernel,
        in_specs=[VM] * 4,
        out_specs=VM,
        out_shape=slab_type,
        scratch_shapes=[stack],
        compiler_params=params,
        name="first",
    )(tokens, norm_gain, routes_t, placement)
    in_weight = dequant(w_in, in_scale)
    out_weight = dequant(w_out, out_scale)
    stream = tokens
    for layer in range(layers):
        answers = expert(layer, exchange(slab, devices), in_weight, out_weight)
        back = exchange(answers, devices)
        if layer + 1 < layers:
            slab, stream = pl.pallas_call(
                functools.partial(middle_kernel, layer),
                in_specs=[VM] * 6,
                out_specs=(VM, VM),
                out_shape=(slab_type, stream_type),
                scratch_shapes=[rows, stack],
                compiler_params=params,
                name="middle",
            )(back, stream, norm_gain, routes_t, gates_t, placement)
        else:
            stream = pl.pallas_call(
                functools.partial(last_kernel, layer),
                in_specs=[VM] * 5,
                out_specs=VM,
                out_shape=stream_type,
                scratch_shapes=[rows],
                compiler_params=params,
                name="last",
            )(back, stream, routes_t, gates_t, placement)
    return stream


def solution(mesh):
    return jax.shard_map(
        shards,
        mesh=mesh,
        in_specs=(
            P(AXES, None),
            P(),
            P(None, AXES, None),
            P(None, AXES, None),
            P(),
            P(None, AXES, None, None),
            P(None, AXES, None, None),
            P(None, AXES, None, None),
            P(None, AXES, None, None),
        ),
        out_specs=P(AXES, None),
        check_vma=False,
    )
```

```python
import functools

import jax
import jax.numpy as jnp
from jax import lax
from jax.experimental import pallas as pl
from jax.experimental.pallas import tpu as pltpu
from jax.sharding import PartitionSpec as P

AXES = ("dp", "expert")
QBLK = 128
CAP = 3
PIECES = 8
GROUP = 32
EPS = 1e-06
MIB = 1 << 20


def fold_matrix():
    row = lax.broadcasted_iota(jnp.int32, (GROUP * PIECES, GROUP * PIECES), 0)
    col = lax.broadcasted_iota(jnp.int32, (GROUP * PIECES, GROUP * PIECES), 1)
    return jnp.where(col == (row & (PIECES - 1)) * GROUP + (row >> 3), 1.0, 0.0).astype(jnp.bfloat16)


def unfold_matrix():
    row = lax.broadcasted_iota(jnp.int32, (GROUP * PIECES, GROUP * PIECES), 0)
    col = lax.broadcasted_iota(jnp.int32, (GROUP * PIECES, GROUP * PIECES), 1)
    return jnp.where(col == (row & (GROUP - 1)) * PIECES + (row >> 5), 1.0, 0.0).astype(jnp.bfloat16)


def unfold_rows(slab_ref, rows_ref):
    piece = slab_ref.shape[1]
    span = GROUP * PIECES
    unfold = unfold_matrix()
    for b in range(slab_ref.shape[0] // span):
        block = jnp.dot(
            unfold, slab_ref[b * span : (b + 1) * span, :], preferred_element_type=jnp.float32
        ).astype(jnp.bfloat16)
        for p in range(PIECES):
            rows_ref[b * GROUP : (b + 1) * GROUP, p * piece : (p + 1) * piece] = block[
                p * GROUP : (p + 1) * GROUP
            ]


def fold_rows(stack_ref, slab_ref):
    span = GROUP * PIECES
    fold = fold_matrix()
    for b in range(slab_ref.shape[0] // span):
        slab_ref[b * span : (b + 1) * span, :] = jnp.dot(
            fold, stack_ref[b * span : (b + 1) * span, :], preferred_element_type=jnp.float32
        ).astype(jnp.bfloat16)


def stack_piece(stack_ref, values, p):
    span = GROUP * PIECES
    for b in range(values.shape[0] // GROUP):
        stack_ref[b * span + p * GROUP : b * span + (p + 1) * GROUP, :] = values[
            b * GROUP : (b + 1) * GROUP
        ]


def slot_tables(routes_t, place_row, gates_t):
    tokens = routes_t.shape[1]
    devices = place_row.shape[1]
    slots = devices * CAP
    home = lax.broadcasted_iota(jnp.int32, (devices, slots), 0)
    slot = lax.broadcasted_iota(jnp.int32, (devices, slots), 1)
    low = home * CAP
    widen = jnp.where((slot >= low) & (slot < low + CAP), 1.0, 0.0).astype(jnp.bfloat16)
    place = jnp.dot(
        jnp.broadcast_to(place_row.astype(jnp.float32), (8, devices)).astype(jnp.bfloat16),
        widen,
        preferred_element_type=jnp.float32,
    )[:1]
    rank_of = jnp.dot(
        jnp.broadcast_to(
            lax.broadcasted_iota(jnp.int32, (1, devices), 1).astype(jnp.float32), (8, devices)
        ).astype(jnp.bfloat16),
        widen,
        preferred_element_type=jnp.float32,
    )[:1]
    order = lax.broadcasted_iota(jnp.int32, (1, slots), 1).astype(jnp.float32) - rank_of * CAP
    chosen = jnp.transpose(routes_t.astype(jnp.float32))
    gate = None if gates_t is None else jnp.transpose(gates_t)
    taken = jnp.zeros((tokens, slots), jnp.float32)
    weight = jnp.zeros((tokens, slots), jnp.float32)
    for k in range(chosen.shape[1]):
        same = chosen[:, k : k + 1] == place
        taken = jnp.where(same, 1.0, taken)
        if gate is not None:
            weight = jnp.where(same, gate[:, k : k + 1], weight)
    later = lax.broadcasted_iota(jnp.int32, (tokens, tokens), 0)
    earlier = lax.broadcasted_iota(jnp.int32, (tokens, tokens), 1)
    before = jnp.where(earlier < later, 1.0, 0.0).astype(jnp.bfloat16)
    ranks = jnp.dot(before, taken.astype(jnp.bfloat16), preferred_element_type=jnp.float32)
    mine = ranks == order
    return jnp.where(mine, taken, 0.0), jnp.where(mine, weight, 0.0)


def normalise(stream_f, gain):
    scale = lax.rsqrt(jnp.mean(stream_f * stream_f, axis=-1, keepdims=True) + EPS)
    return (stream_f * scale * gain).astype(jnp.bfloat16)


def send_rows(pick, normed, stack_ref, slab_ref):
    piece = slab_ref.shape[1]
    for p in range(PIECES):
        rows = jnp.dot(
            pick, normed[:, p * piece : (p + 1) * piece], preferred_element_type=jnp.float32
        ).astype(jnp.bfloat16)
        stack_piece(stack_ref, rows, p)
    fold_rows(stack_ref, slab_ref)


def mix(weight, slab_ref, rows_ref):
    unfold_rows(slab_ref, rows_ref)
    both = jnp.dot(weight, rows_ref[...], preferred_element_type=jnp.float32)
    tokens = weight.shape[0] // 2
    return both[:tokens] + both[tokens:]


def first_kernel(
    tokens_hbm, gain_hbm, routes_hbm, place_hbm, slab_ref,
    tokens_ref, gain_ref, routes_ref, place_ref, stack_ref, sems,
):
    loads = [
        pltpu.make_async_copy(src, dst, sems.at[i])
        for i, (src, dst) in enumerate(
            (
                (routes_hbm, routes_ref),
                (place_hbm, place_ref),
                (tokens_hbm, tokens_ref),
                (gain_hbm, gain_ref),
            )
        )
    ]
    for load in loads:
        load.start()
    loads[0].wait()
    loads[1].wait()
    select, _ = slot_tables(routes_ref[0], place_ref[0:1, :], None)
    pick = jnp.transpose(select).astype(jnp.bfloat16)
    loads[2].wait()
    loads[3].wait()
    normed = normalise(tokens_ref[...].astype(jnp.float32), gain_ref[0:1, :])
    send_rows(pick, normed, stack_ref, slab_ref)


def middle_kernel(
    layer, slab_in, stream_ref, gain_ref, weight_ref, pick_ref,
    slab_ref, out_ref, rows_ref, stack_ref,
):
    mixed = mix(weight_ref[...], slab_in, rows_ref)
    stream = (stream_ref[...].astype(jnp.float32) + mixed).astype(jnp.bfloat16)
    out_ref[...] = stream
    normed = normalise(stream.astype(jnp.float32), gain_ref[layer + 1 : layer + 2, :])
    send_rows(pick_ref[...], normed, stack_ref, slab_ref)


def last_kernel(slab_in, stream_ref, weight_ref, out_ref, rows_ref):
    mixed = mix(weight_ref[...], slab_in, rows_ref)
    out_ref[...] = (stream_ref[...].astype(jnp.float32) + mixed).astype(jnp.bfloat16)


def prepare_kernel(
    layer, in_scale, out_scale, w_in, w_out, routes_ref, gates_ref, place_ref,
    win_hbm, wout_hbm, weight_ref, *rest,
):
    pick_ref = rest[0] if len(rest) > 5 else None
    win, wout, load_sems, in_sems, out_sems = rest[-5:]
    rows = 2 * QBLK
    chunk = win_hbm.shape[2]
    loads = []
    for src, buf, scale, dst, sems in (
        (w_in, win, in_scale, win_hbm, in_sems),
        (w_out, wout, out_scale, wout_hbm, out_sems),
    ):
        for r in range(buf.shape[0] // rows):
            span = pl.ds(r * rows, rows)
            load = pltpu.make_async_copy(
                src.at[layer, 0, span, :], buf.at[span, :], load_sems.at[len(loads)]
            )
            load.start()
            loads.append((load, buf, scale, dst, sems, r))
    _, weight = slot_tables(routes_ref[layer], place_ref[layer : layer + 1, :], gates_ref[layer])
    high = weight.astype(jnp.bfloat16)
    low = (weight - high.astype(jnp.float32)).astype(jnp.bfloat16)
    weight_ref[...] = jnp.concatenate([high, low], axis=0)
    if pick_ref is not None:
        select, _ = slot_tables(
            routes_ref[layer + 1], place_ref[layer + 1 : layer + 2, :], None
        )
        pick_ref[...] = jnp.transpose(select).astype(jnp.bfloat16)
    stores = []
    for load, buf, scale, dst, sems, r in loads:
        load.wait()
        for i in range(rows // QBLK):
            for j in range(buf.shape[1] // QBLK):
                at = (
                    slice(r * rows + i * QBLK, r * rows + (i + 1) * QBLK),
                    slice(j * QBLK, (j + 1) * QBLK),
                )
                factor = scale[layer, r * (rows // QBLK) + i, j]
                buf[at] = (buf[at].astype(jnp.float32) * factor).astype(jnp.bfloat16)
        for c in range(dst.shape[0]):
            store = pltpu.make_async_copy(
                buf.at[pl.ds(r * rows, rows), pl.ds(c * chunk, chunk)],
                dst.at[c, pl.ds(r * rows, rows), :],
                sems.at[r, c],
            )
            store.start()
            stores.append(store)
    for store in stores:
        store.wait()


def expert_steps(slab_in, slab_ref, x_ref, hid, stack_ref, in_chunk, out_chunk, chunks):
    unfold_rows(slab_in, x_ref)
    chunk = slab_ref.shape[1]
    for n in range(chunks):
        gate = jnp.dot(x_ref[...], in_chunk(n), preferred_element_type=jnp.float32)
        up = jnp.dot(x_ref[...], in_chunk(chunks + n), preferred_element_type=jnp.float32)
        hid[:, n * chunk : (n + 1) * chunk] = (gate / (1.0 + jnp.exp(-gate)) * up).astype(
            jnp.bfloat16
        )
    for m in range(PIECES):
        answer = jnp.dot(hid[...], out_chunk(m), preferred_element_type=jnp.float32).astype(
            jnp.bfloat16
        )
        stack_piece(stack_ref, answer, m)
    fold_rows(stack_ref, slab_ref)


def expert_kernel(slab_in, win, wout, slab_ref, x_ref, hid, stack_ref):
    expert_steps(
        slab_in, slab_ref, x_ref, hid, stack_ref,
        lambda c: win[c], lambda c: wout[c], win.shape[0] // 2,
    )


def streamed_kernel(
    slab_in, win_hbm, wout_hbm, slab_ref, x_ref, hid, stack_ref, win, wout, in_sems, out_sems
):
    chunks = win.shape[0] // 2

    def in_load(c):
        return pltpu.make_async_copy(win_hbm.at[c], win.at[c], in_sems.at[c])

    def out_load(c):
        return pltpu.make_async_copy(wout_hbm.at[c], wout.at[c], out_sems.at[c])

    for n in range(chunks):
        in_load(n).start()
        in_load(chunks + n).start()
    for m in range(wout.shape[0]):
        out_load(m).start()

    def in_chunk(c):
        in_load(c).wait()
        return win[c]

    def out_chunk(c):
        out_load(c).wait()
        return wout[c]

    expert_steps(slab_in, slab_ref, x_ref, hid, stack_ref, in_chunk, out_chunk, chunks)


VM = pl.BlockSpec(memory_space=pltpu.VMEM)
SM = pl.BlockSpec(memory_space=pltpu.SMEM)
HB = pl.BlockSpec(memory_space=pltpu.HBM)


def prepare(layer, layers, weights, tables, slots, chunk):
    w_in, in_scale, w_out, out_scale = weights
    routes_t, gates_t, place = tables
    tokens = routes_t.shape[2]
    width, gated = w_in.shape[2:]
    ff = w_out.shape[2]
    outs = [
        pltpu.HBM((gated // chunk, width, chunk), jnp.bfloat16),
        pltpu.HBM((width // chunk, ff, chunk), jnp.bfloat16),
        jax.ShapeDtypeStruct((2 * tokens, slots), jnp.bfloat16),
    ]
    if layer + 1 < layers:
        outs.append(jax.ShapeDtypeStruct((slots, tokens), jnp.bfloat16))
    rows = 2 * QBLK
    size = width * gated + ff * width
    return pl.pallas_call(
        functools.partial(prepare_kernel, layer),
        in_specs=[SM, SM, HB, HB, VM, VM, VM],
        out_specs=[HB, HB] + [VM] * (len(outs) - 2),
        out_shape=outs,
        scratch_shapes=[
            pltpu.VMEM((width, gated), jnp.bfloat16),
            pltpu.VMEM((ff, width), jnp.bfloat16),
            pltpu.SemaphoreType.DMA(((width + ff) // rows,)),
            pltpu.SemaphoreType.DMA((width // rows, gated // chunk)),
            pltpu.SemaphoreType.DMA((ff // rows, width // chunk)),
        ],
        compiler_params=pltpu.CompilerParams(vmem_limit_bytes=24 * MIB),
        cost_estimate=pl.CostEstimate(flops=size, bytes_accessed=4 * size, transcendentals=0),
        name="prepare",
    )(in_scale[:, 0], out_scale[:, 0], w_in, w_out, routes_t, gates_t, place)


def expert(slab, win, wout, streamed):
    rows, piece = slab.shape
    slots = rows // PIECES
    width = win.shape[1]
    ff = wout.shape[1]
    scratch = [
        pltpu.VMEM((slots, width), jnp.bfloat16),
        pltpu.VMEM((slots, ff), jnp.bfloat16),
        pltpu.VMEM(slab.shape, jnp.bfloat16),
    ]
    if streamed:
        win, wout = hbm(win), hbm(wout)
        scratch += [
            pltpu.VMEM(win.shape, jnp.bfloat16),
            pltpu.VMEM(wout.shape, jnp.bfloat16),
            pltpu.SemaphoreType.DMA((win.shape[0],)),
            pltpu.SemaphoreType.DMA((wout.shape[0],)),
        ]
    return pl.pallas_call(
        streamed_kernel if streamed else expert_kernel,
        in_specs=[VM, HB, HB] if streamed else [VM] * 3,
        out_specs=VM,
        out_shape=jax.ShapeDtypeStruct(slab.shape, jnp.bfloat16),
        scratch_shapes=scratch,
        compiler_params=pltpu.CompilerParams(vmem_limit_bytes=(28 if streamed else 20) * MIB),
        cost_estimate=pl.CostEstimate(
            flops=6 * slots * width * ff,
            bytes_accessed=6 * width * ff + 4 * slots * width,
            transcendentals=slots * ff,
        ),
        name="expert",
    )(slab, win, wout)


def hbm(array):
    return pltpu.with_memory_space_constraint(array, pltpu.HBM)


def exchange(slab, devices):
    split = slab.reshape(devices, slab.shape[0] // devices, slab.shape[1])
    moved = lax.all_to_all(split, AXES, split_axis=0, concat_axis=0, tiled=True)
    return moved.reshape(slab.shape)


def shards(tokens, norm_gain, routes, gates, placement, w_in, in_scale, w_out, out_scale):
    count, width = tokens.shape
    layers, devices = placement.shape
    slots = devices * CAP
    piece = width // PIECES
    routes_t = jnp.swapaxes(routes, 1, 2)
    gates_t = jnp.swapaxes(gates, 1, 2)
    slab_type = jax.ShapeDtypeStruct((slots * PIECES, piece), jnp.bfloat16)
    stream_type = jax.ShapeDtypeStruct((count, width), jnp.bfloat16)
    rows = pltpu.VMEM((slots, width), jnp.bfloat16)
    stack = pltpu.VMEM((slots * PIECES, piece), jnp.bfloat16)
    params = pltpu.CompilerParams(vmem_limit_bytes=24 * MIB)

    small = (
        pltpu.VMEM((count, width), jnp.bfloat16),
        pltpu.VMEM(norm_gain.shape, jnp.float32),
        pltpu.VMEM(routes_t.shape, jnp.int32),
        pltpu.VMEM(placement.shape, jnp.int32),
    )
    slab = pl.pallas_call(
        first_kernel,
        in_specs=[HB] * 4,
        out_specs=VM,
        out_shape=slab_type,
        scratch_shapes=[*small, stack, pltpu.SemaphoreType.DMA((4,))],
        compiler_params=params,
        name="first",
    )(*[hbm(a) for a in (tokens, norm_gain, routes_t, placement)])
    weights = (hbm(w_in), in_scale, hbm(w_out), out_scale)
    stream = tokens
    prepared = [
        prepare(layer, layers, weights, (routes_t, gates_t, placement), slots, piece)
        for layer in range(layers)
    ]
    for layer in range(layers):
        win, wout, weight = prepared[layer][:3]
        arrived = exchange(slab, devices)
        if layer == 0:
            arrived, prepared = lax.optimization_barrier((arrived, prepared))
            win, wout, weight = prepared[0][:3]
        answers = expert(arrived, win, wout, layer == 0)
        back = exchange(answers, devices)
        if layer + 1 < layers:
            slab, stream = pl.pallas_call(
                functools.partial(middle_kernel, layer),
                in_specs=[VM] * 5,
                out_specs=(VM, VM),
                out_shape=(slab_type, stream_type),
                scratch_shapes=[rows, stack],
                compiler_params=params,
                name="middle",
            )(back, stream, norm_gain, weight, prepared[layer][3])
        else:
            stream = pl.pallas_call(
                last_kernel,
                in_specs=[VM] * 3,
                out_specs=VM,
                out_shape=stream_type,
                scratch_shapes=[rows],
                compiler_params=params,
                name="last",
            )(back, stream, weight)
    return stream


def solution(mesh):
    return jax.shard_map(
        shards,
        mesh=mesh,
        in_specs=(
            P(AXES, None),
            P(),
            P(None, AXES, None),
            P(None, AXES, None),
            P(),
            P(None, AXES, None, None),
            P(None, AXES, None, None),
            P(None, AXES, None, None),
            P(None, AXES, None, None),
        ),
        out_specs=P(AXES, None),
        check_vma=False,
    )
```

```python
import functools

import jax
import jax.numpy as jnp
from jax import lax
from jax.experimental import pallas as pl
from jax.experimental.pallas import tpu as pltpu
from jax.sharding import PartitionSpec as P

AXES = ("dp", "expert")
QBLK = 128
CAP = 3
PIECES = 8
GROUP = 32
EPS = 1e-06
MIB = 1 << 20


def fold_matrix():
    row = lax.broadcasted_iota(jnp.int32, (GROUP * PIECES, GROUP * PIECES), 0)
    col = lax.broadcasted_iota(jnp.int32, (GROUP * PIECES, GROUP * PIECES), 1)
    return jnp.where(col == (row & (PIECES - 1)) * GROUP + (row >> 3), 1.0, 0.0).astype(jnp.bfloat16)


def unfold_matrix():
    row = lax.broadcasted_iota(jnp.int32, (GROUP * PIECES, GROUP * PIECES), 0)
    col = lax.broadcasted_iota(jnp.int32, (GROUP * PIECES, GROUP * PIECES), 1)
    return jnp.where(col == (row & (GROUP - 1)) * PIECES + (row >> 5), 1.0, 0.0).astype(jnp.bfloat16)


def unfold_rows(slab_ref, rows_ref):
    piece = slab_ref.shape[1]
    span = GROUP * PIECES
    unfold = unfold_matrix()
    for b in range(slab_ref.shape[0] // span):
        block = jnp.dot(
            unfold, slab_ref[b * span : (b + 1) * span, :], preferred_element_type=jnp.float32
        ).astype(jnp.bfloat16)
        for p in range(PIECES):
            rows_ref[b * GROUP : (b + 1) * GROUP, p * piece : (p + 1) * piece] = block[
                p * GROUP : (p + 1) * GROUP
            ]


def fold_rows(stack_ref, slab_ref):
    span = GROUP * PIECES
    fold = fold_matrix()
    for b in range(slab_ref.shape[0] // span):
        slab_ref[b * span : (b + 1) * span, :] = jnp.dot(
            fold, stack_ref[b * span : (b + 1) * span, :], preferred_element_type=jnp.float32
        ).astype(jnp.bfloat16)


def stack_piece(stack_ref, values, p):
    span = GROUP * PIECES
    for b in range(values.shape[0] // GROUP):
        stack_ref[b * span + p * GROUP : b * span + (p + 1) * GROUP, :] = values[
            b * GROUP : (b + 1) * GROUP
        ]


def slot_tables(routes_t, place_row, gates_t):
    tokens = routes_t.shape[1]
    devices = place_row.shape[1]
    slots = devices * CAP
    home = lax.broadcasted_iota(jnp.int32, (devices, slots), 0)
    slot = lax.broadcasted_iota(jnp.int32, (devices, slots), 1)
    low = home * CAP
    widen = jnp.where((slot >= low) & (slot < low + CAP), 1.0, 0.0).astype(jnp.bfloat16)
    place = jnp.dot(
        jnp.broadcast_to(place_row.astype(jnp.float32), (8, devices)).astype(jnp.bfloat16),
        widen,
        preferred_element_type=jnp.float32,
    )[:1]
    rank_of = jnp.dot(
        jnp.broadcast_to(
            lax.broadcasted_iota(jnp.int32, (1, devices), 1).astype(jnp.float32), (8, devices)
        ).astype(jnp.bfloat16),
        widen,
        preferred_element_type=jnp.float32,
    )[:1]
    order = lax.broadcasted_iota(jnp.int32, (1, slots), 1).astype(jnp.float32) - rank_of * CAP
    chosen = jnp.transpose(routes_t.astype(jnp.float32))
    gate = None if gates_t is None else jnp.transpose(gates_t)
    taken = jnp.zeros((tokens, slots), jnp.float32)
    weight = jnp.zeros((tokens, slots), jnp.float32)
    for k in range(chosen.shape[1]):
        same = chosen[:, k : k + 1] == place
        taken = jnp.where(same, 1.0, taken)
        if gate is not None:
            weight = jnp.where(same, gate[:, k : k + 1], weight)
    later = lax.broadcasted_iota(jnp.int32, (tokens, tokens), 0)
    earlier = lax.broadcasted_iota(jnp.int32, (tokens, tokens), 1)
    before = jnp.where(earlier < later, 1.0, 0.0).astype(jnp.bfloat16)
    ranks = jnp.dot(before, taken.astype(jnp.bfloat16), preferred_element_type=jnp.float32)
    mine = ranks == order
    return jnp.where(mine, taken, 0.0), jnp.where(mine, weight, 0.0)


def normalise(stream_f, gain):
    scale = lax.rsqrt(jnp.mean(stream_f * stream_f, axis=-1, keepdims=True) + EPS)
    return (stream_f * scale * gain).astype(jnp.bfloat16)


def send_rows(pick, normed, stack_ref, slab_ref):
    piece = slab_ref.shape[1]
    for p in range(PIECES):
        rows = jnp.dot(
            pick, normed[:, p * piece : (p + 1) * piece], preferred_element_type=jnp.float32
        ).astype(jnp.bfloat16)
        stack_piece(stack_ref, rows, p)
    fold_rows(stack_ref, slab_ref)


def mix(weight, slab_ref, rows_ref):
    unfold_rows(slab_ref, rows_ref)
    high = weight.astype(jnp.bfloat16)
    low = (weight - high.astype(jnp.float32)).astype(jnp.bfloat16)
    both = jnp.dot(
        jnp.concatenate([high, low], axis=0), rows_ref[...], preferred_element_type=jnp.float32
    )
    tokens = weight.shape[0]
    return both[:tokens] + both[tokens:]


def first_kernel(
    tokens_hbm, gain_hbm, routes_hbm, place_hbm, slab_ref,
    tokens_ref, gain_ref, routes_ref, place_ref, stack_ref, sems,
):
    loads = [
        pltpu.make_async_copy(src, dst, sems.at[i])
        for i, (src, dst) in enumerate(
            (
                (routes_hbm, routes_ref),
                (place_hbm, place_ref),
                (tokens_hbm, tokens_ref),
                (gain_hbm, gain_ref),
            )
        )
    ]
    for load in loads:
        load.start()
    loads[0].wait()
    loads[1].wait()
    select, _ = slot_tables(routes_ref[0], place_ref[0:1, :], None)
    pick = jnp.transpose(select).astype(jnp.bfloat16)
    loads[2].wait()
    loads[3].wait()
    normed = normalise(tokens_ref[...].astype(jnp.float32), gain_ref[0:1, :])
    send_rows(pick, normed, stack_ref, slab_ref)


def middle_kernel(
    layer, slab_in, stream_ref, gain_ref, routes_ref, gates_ref, place_ref,
    slab_ref, out_ref, rows_ref, stack_ref,
):
    _, weight = slot_tables(routes_ref[layer], place_ref[layer : layer + 1, :], gates_ref[layer])
    select, _ = slot_tables(routes_ref[layer + 1], place_ref[layer + 1 : layer + 2, :], None)
    pick = jnp.transpose(select).astype(jnp.bfloat16)
    mixed = mix(weight, slab_in, rows_ref)
    stream = (stream_ref[...].astype(jnp.float32) + mixed).astype(jnp.bfloat16)
    out_ref[...] = stream
    normed = normalise(stream.astype(jnp.float32), gain_ref[layer + 1 : layer + 2, :])
    send_rows(pick, normed, stack_ref, slab_ref)


def last_kernel(
    layer, slab_in, stream_ref, routes_ref, gates_ref, place_ref, out_ref, rows_ref
):
    _, weight = slot_tables(routes_ref[layer], place_ref[layer : layer + 1, :], gates_ref[layer])
    mixed = mix(weight, slab_in, rows_ref)
    out_ref[...] = (stream_ref[...].astype(jnp.float32) + mixed).astype(jnp.bfloat16)


def block_weight(w_ref, factor, layer, first, count):
    lines = []
    for i in range(w_ref.shape[2] // QBLK):
        line = [
            (
                w_ref[layer, 0, i * QBLK : (i + 1) * QBLK, j * QBLK : (j + 1) * QBLK].astype(
                    jnp.float32
                )
                * factor(i, j)
            ).astype(jnp.bfloat16)
            for j in range(first // QBLK, (first + count) // QBLK)
        ]
        lines.append(jnp.concatenate(line, axis=1))
    return jnp.concatenate(lines, axis=0)


def expert_kernel(
    layer, in_scale, out_scale, slab_in, w_in, w_out, slab_ref, x_ref, hid, stack_ref
):
    def into(first, count):
        return block_weight(w_in, lambda i, j: in_scale[layer, j, 0, i], layer, first, count)

    def out_of(first, count):
        return block_weight(w_out, lambda i, j: out_scale[layer, i, 0, j], layer, first, count)

    unfold_rows(slab_in, x_ref)
    ff = w_out.shape[2]
    chunk = slab_ref.shape[1]
    for n in range(ff // chunk):
        gate = jnp.dot(x_ref[...], into(n * chunk, chunk), preferred_element_type=jnp.float32)
        up = jnp.dot(x_ref[...], into(ff + n * chunk, chunk), preferred_element_type=jnp.float32)
        hid[:, n * chunk : (n + 1) * chunk] = (gate / (1.0 + jnp.exp(-gate)) * up).astype(
            jnp.bfloat16
        )
    for m in range(PIECES):
        answer = jnp.dot(
            hid[...], out_of(m * chunk, chunk), preferred_element_type=jnp.float32
        ).astype(jnp.bfloat16)
        stack_piece(stack_ref, answer, m)
    fold_rows(stack_ref, slab_ref)


VM = pl.BlockSpec(memory_space=pltpu.VMEM)
SM = pl.BlockSpec(memory_space=pltpu.SMEM)
HB = pl.BlockSpec(memory_space=pltpu.HBM)


def expert(layer, slab, weights):
    w_in, in_scale, w_out, out_scale = weights
    rows, piece = slab.shape
    slots = rows // PIECES
    width, ff = w_in.shape[2], w_out.shape[2]
    return pl.pallas_call(
        functools.partial(expert_kernel, layer),
        in_specs=[SM, SM, VM, VM, VM],
        out_specs=VM,
        out_shape=jax.ShapeDtypeStruct(slab.shape, jnp.bfloat16),
        scratch_shapes=[
            pltpu.VMEM((slots, width), jnp.bfloat16),
            pltpu.VMEM((slots, ff), jnp.bfloat16),
            pltpu.VMEM(slab.shape, jnp.bfloat16),
        ],
        compiler_params=pltpu.CompilerParams(vmem_limit_bytes=20 * MIB),
        cost_estimate=pl.CostEstimate(
            flops=6 * slots * width * ff,
            bytes_accessed=6 * width * ff + 4 * slots * width,
            transcendentals=slots * ff,
        ),
        name="expert",
    )(in_scale, out_scale, slab, w_in, w_out)


def hbm(array):
    return pltpu.with_memory_space_constraint(array, pltpu.HBM)


def exchange(slab, devices):
    split = slab.reshape(devices, slab.shape[0] // devices, slab.shape[1])
    moved = lax.all_to_all(split, AXES, split_axis=0, concat_axis=0, tiled=True)
    return moved.reshape(slab.shape)


def shards(tokens, norm_gain, routes, gates, placement, w_in, in_scale, w_out, out_scale):
    count, width = tokens.shape
    layers, devices = placement.shape
    slots = devices * CAP
    piece = width // PIECES
    routes_t = jnp.swapaxes(routes, 1, 2)
    gates_t = jnp.swapaxes(gates, 1, 2)
    slab_type = jax.ShapeDtypeStruct((slots * PIECES, piece), jnp.bfloat16)
    stream_type = jax.ShapeDtypeStruct((count, width), jnp.bfloat16)
    rows = pltpu.VMEM((slots, width), jnp.bfloat16)
    stack = pltpu.VMEM((slots * PIECES, piece), jnp.bfloat16)
    params = pltpu.CompilerParams(vmem_limit_bytes=12 * MIB)

    small = (
        pltpu.VMEM((count, width), jnp.bfloat16),
        pltpu.VMEM(norm_gain.shape, jnp.float32),
        pltpu.VMEM(routes_t.shape, jnp.int32),
        pltpu.VMEM(placement.shape, jnp.int32),
    )
    slab = pl.pallas_call(
        first_kernel,
        in_specs=[HB] * 4,
        out_specs=VM,
        out_shape=slab_type,
        scratch_shapes=[*small, stack, pltpu.SemaphoreType.DMA((4,))],
        compiler_params=params,
        cost_estimate=pl.CostEstimate(
            flops=8 * 10**9, bytes_accessed=8 * 10**6, transcendentals=0
        ),
        name="first",
    )(*[hbm(a) for a in (tokens, norm_gain, routes_t, placement)])
    weights = (
        w_in,
        jnp.transpose(in_scale, (0, 3, 1, 2)),
        w_out,
        jnp.transpose(out_scale, (0, 2, 1, 3)),
    )
    stream = tokens
    for layer in range(layers):
        answers = expert(layer, exchange(slab, devices), weights)
        back = exchange(answers, devices)
        if layer + 1 < layers:
            slab, stream = pl.pallas_call(
                functools.partial(middle_kernel, layer),
                in_specs=[VM] * 6,
                out_specs=(VM, VM),
                out_shape=(slab_type, stream_type),
                scratch_shapes=[rows, stack],
                compiler_params=params,
                name="middle",
            )(back, stream, norm_gain, routes_t, gates_t, placement)
        else:
            stream = pl.pallas_call(
                functools.partial(last_kernel, layer),
                in_specs=[VM] * 5,
                out_specs=VM,
                out_shape=stream_type,
                scratch_shapes=[rows],
                compiler_params=params,
                name="last",
            )(back, stream, routes_t, gates_t, placement)
    return stream


def solution(mesh):
    return jax.shard_map(
        shards,
        mesh=mesh,
        in_specs=(
            P(AXES, None),
            P(),
            P(None, AXES, None),
            P(None, AXES, None),
            P(),
            P(None, AXES, None, None),
            P(None, AXES, None, None),
            P(None, AXES, None, None),
            P(None, AXES, None, None),
        ),
        out_specs=P(AXES, None),
        check_vma=False,
    )
```

```python
import functools

import jax
import jax.numpy as jnp
from jax import lax
from jax.experimental import pallas as pl
from jax.experimental.pallas import tpu as pltpu
from jax.sharding import PartitionSpec as P

AXES = ("dp", "expert")
QBLK = 128
CAP = 3
PIECES = 8
GROUP = 32
EPS = 1e-06
MIB = 1 << 20


def fold_matrix():
    row = lax.broadcasted_iota(jnp.int32, (GROUP * PIECES, GROUP * PIECES), 0)
    col = lax.broadcasted_iota(jnp.int32, (GROUP * PIECES, GROUP * PIECES), 1)
    return jnp.where(col == (row & (PIECES - 1)) * GROUP + (row >> 3), 1.0, 0.0).astype(jnp.bfloat16)


def unfold_matrix():
    row = lax.broadcasted_iota(jnp.int32, (GROUP * PIECES, GROUP * PIECES), 0)
    col = lax.broadcasted_iota(jnp.int32, (GROUP * PIECES, GROUP * PIECES), 1)
    return jnp.where(col == (row & (GROUP - 1)) * PIECES + (row >> 5), 1.0, 0.0).astype(jnp.bfloat16)


def unfold_rows(slab_ref, rows_ref):
    piece = slab_ref.shape[1]
    span = GROUP * PIECES
    unfold = unfold_matrix()
    for b in range(slab_ref.shape[0] // span):
        block = jnp.dot(
            unfold, slab_ref[b * span : (b + 1) * span, :], preferred_element_type=jnp.float32
        ).astype(jnp.bfloat16)
        for p in range(PIECES):
            rows_ref[b * GROUP : (b + 1) * GROUP, p * piece : (p + 1) * piece] = block[
                p * GROUP : (p + 1) * GROUP
            ]


def fold_rows(stack_ref, slab_ref):
    span = GROUP * PIECES
    fold = fold_matrix()
    for b in range(slab_ref.shape[0] // span):
        slab_ref[b * span : (b + 1) * span, :] = jnp.dot(
            fold, stack_ref[b * span : (b + 1) * span, :], preferred_element_type=jnp.float32
        ).astype(jnp.bfloat16)


def stack_piece(stack_ref, values, p):
    span = GROUP * PIECES
    for b in range(values.shape[0] // GROUP):
        stack_ref[b * span + p * GROUP : b * span + (p + 1) * GROUP, :] = values[
            b * GROUP : (b + 1) * GROUP
        ]


def slot_tables(routes_t, place_row, gates_t):
    tokens = routes_t.shape[1]
    devices = place_row.shape[1]
    slots = devices * CAP
    home = lax.broadcasted_iota(jnp.int32, (devices, slots), 0)
    slot = lax.broadcasted_iota(jnp.int32, (devices, slots), 1)
    low = home * CAP
    widen = jnp.where((slot >= low) & (slot < low + CAP), 1.0, 0.0).astype(jnp.bfloat16)
    place = jnp.dot(
        jnp.broadcast_to(place_row.astype(jnp.float32), (8, devices)).astype(jnp.bfloat16),
        widen,
        preferred_element_type=jnp.float32,
    )[:1]
    rank_of = jnp.dot(
        jnp.broadcast_to(
            lax.broadcasted_iota(jnp.int32, (1, devices), 1).astype(jnp.float32), (8, devices)
        ).astype(jnp.bfloat16),
        widen,
        preferred_element_type=jnp.float32,
    )[:1]
    order = lax.broadcasted_iota(jnp.int32, (1, slots), 1).astype(jnp.float32) - rank_of * CAP
    chosen = jnp.transpose(routes_t.astype(jnp.float32))
    gate = None if gates_t is None else jnp.transpose(gates_t)
    taken = jnp.zeros((tokens, slots), jnp.float32)
    weight = jnp.zeros((tokens, slots), jnp.float32)
    for k in range(chosen.shape[1]):
        same = chosen[:, k : k + 1] == place
        taken = jnp.where(same, 1.0, taken)
        if gate is not None:
            weight = jnp.where(same, gate[:, k : k + 1], weight)
    later = lax.broadcasted_iota(jnp.int32, (tokens, tokens), 0)
    earlier = lax.broadcasted_iota(jnp.int32, (tokens, tokens), 1)
    before = jnp.where(earlier < later, 1.0, 0.0).astype(jnp.bfloat16)
    ranks = jnp.dot(before, taken.astype(jnp.bfloat16), preferred_element_type=jnp.float32)
    mine = ranks == order
    return jnp.where(mine, taken, 0.0), jnp.where(mine, weight, 0.0)


def normalise(stream_f, gain):
    scale = lax.rsqrt(jnp.mean(stream_f * stream_f, axis=-1, keepdims=True) + EPS)
    return (stream_f * scale * gain).astype(jnp.bfloat16)


def build_spread(select, wide_ref, spread_ref):
    tokens, slots = select.shape
    lanes = tokens * PIECES
    token = lax.broadcasted_iota(jnp.int32, (tokens, lanes), 0)
    lane = lax.broadcasted_iota(jnp.int32, (tokens, lanes), 1)
    tile = jnp.where((lane & (tokens - 1)) == token, 1.0, 0.0).astype(jnp.bfloat16)
    wide_ref[...] = jnp.dot(
        jnp.transpose(select).astype(jnp.bfloat16), tile, preferred_element_type=jnp.float32
    )
    own = lax.broadcasted_iota(jnp.int32, (PIECES, lanes), 0)
    piece = lax.broadcasted_iota(jnp.int32, (PIECES, lanes), 1) // tokens
    mine = own == piece
    for s in range(0, slots, 2):
        pair = [
            jnp.where(mine, jnp.broadcast_to(wide_ref[i : i + 1, :], (PIECES, lanes)), 0.0)
            for i in (s, s + 1)
        ]
        spread_ref[s * PIECES : (s + 2) * PIECES, :] = jnp.concatenate(pair, axis=0).astype(
            jnp.bfloat16
        )


def send_rows(spread_ref, normed, slab_ref):
    piece = slab_ref.shape[1]
    stacked = jnp.concatenate(
        [normed[:, p * piece : (p + 1) * piece] for p in range(PIECES)], axis=0
    )
    span = GROUP * PIECES
    for b in range(slab_ref.shape[0] // span):
        at = slice(b * span, (b + 1) * span)
        slab_ref[at, :] = jnp.dot(
            spread_ref[at, :], stacked, preferred_element_type=jnp.float32
        ).astype(jnp.bfloat16)


def split_weight(weight):
    high = weight.astype(jnp.bfloat16)
    low = (weight - high.astype(jnp.float32)).astype(jnp.bfloat16)
    return jnp.concatenate([high, low], axis=0)


def mix(weight, slab_ref, rows_ref):
    unfold_rows(slab_ref, rows_ref)
    both = jnp.dot(weight, rows_ref[...], preferred_element_type=jnp.float32)
    tokens = weight.shape[0] // 2
    return both[:tokens] + both[tokens:]


def first_kernel(
    tokens_hbm, gain_hbm, routes_hbm, place_hbm, slab_ref,
    tokens_ref, gain_ref, routes_ref, place_ref, wide_ref, spread_ref, sems,
):
    loads = [
        pltpu.make_async_copy(src, dst, sems.at[i])
        for i, (src, dst) in enumerate(
            (
                (routes_hbm, routes_ref),
                (place_hbm, place_ref),
                (tokens_hbm, tokens_ref),
                (gain_hbm, gain_ref),
            )
        )
    ]
    for load in loads:
        load.start()
    loads[0].wait()
    loads[1].wait()
    select, _ = slot_tables(routes_ref[0], place_ref[0:1, :], None)
    build_spread(select, wide_ref, spread_ref)
    loads[2].wait()
    loads[3].wait()
    normed = normalise(tokens_ref[...].astype(jnp.float32), gain_ref[0:1, :])
    send_rows(spread_ref, normed, slab_ref)


def middle_kernel(
    layer, slab_in, stream_ref, gain_ref, weight_ref, spread_ref, slab_ref, out_ref, rows_ref
):
    mixed = mix(weight_ref[...], slab_in, rows_ref)
    stream = (stream_ref[...].astype(jnp.float32) + mixed).astype(jnp.bfloat16)
    out_ref[...] = stream
    normed = normalise(stream.astype(jnp.float32), gain_ref[layer + 1 : layer + 2, :])
    send_rows(spread_ref, normed, slab_ref)


def last_kernel(slab_in, stream_ref, weight_ref, out_ref, rows_ref):
    mixed = mix(weight_ref[...], slab_in, rows_ref)
    out_ref[...] = (stream_ref[...].astype(jnp.float32) + mixed).astype(jnp.bfloat16)


def block_weight(w_ref, factor, layer, first, count):
    lines = []
    for i in range(w_ref.shape[2] // QBLK):
        line = [
            (
                w_ref[layer, 0, i * QBLK : (i + 1) * QBLK, j * QBLK : (j + 1) * QBLK].astype(
                    jnp.float32
                )
                * factor(i, j)
            ).astype(jnp.bfloat16)
            for j in range(first // QBLK, (first + count) // QBLK)
        ]
        lines.append(jnp.concatenate(line, axis=1))
    return jnp.concatenate(lines, axis=0)


def expert_kernel(
    layer, in_scale, out_scale, slab_in, w_in, w_out, routes_ref, gates_ref, place_ref,
    slab_ref, weight_ref, *rest,
):
    def into(first, count):
        return block_weight(w_in, lambda i, j: in_scale[layer, j, 0, i], layer, first, count)

    def out_of(first, count):
        return block_weight(w_out, lambda i, j: out_scale[layer, i, 0, j], layer, first, count)

    x_ref, hid, stack_ref = rest[-3:]
    unfold_rows(slab_in, x_ref)
    _, weight = slot_tables(routes_ref[layer], place_ref[layer : layer + 1, :], gates_ref[layer])
    weight_ref[...] = split_weight(weight)
    if len(rest) > 3:
        spread_ref, wide_ref = rest[:2]
        select, _ = slot_tables(
            routes_ref[layer + 1], place_ref[layer + 1 : layer + 2, :], None
        )
        build_spread(select, wide_ref, spread_ref)
    ff = w_out.shape[2]
    chunk = slab_ref.shape[1]
    for n in range(ff // chunk):
        gate = jnp.dot(x_ref[...], into(n * chunk, chunk), preferred_element_type=jnp.float32)
        up = jnp.dot(x_ref[...], into(ff + n * chunk, chunk), preferred_element_type=jnp.float32)
        hid[:, n * chunk : (n + 1) * chunk] = (gate / (1.0 + jnp.exp(-gate)) * up).astype(
            jnp.bfloat16
        )
    for m in range(PIECES):
        answer = jnp.dot(
            hid[...], out_of(m * chunk, chunk), preferred_element_type=jnp.float32
        ).astype(jnp.bfloat16)
        stack_piece(stack_ref, answer, m)
    fold_rows(stack_ref, slab_ref)


VM = pl.BlockSpec(memory_space=pltpu.VMEM)
SM = pl.BlockSpec(memory_space=pltpu.SMEM)
HB = pl.BlockSpec(memory_space=pltpu.HBM)


def expert(layer, layers, slab, weights, tables):
    w_in, in_scale, w_out, out_scale = weights
    rows, piece = slab.shape
    slots = rows // PIECES
    width, ff = w_in.shape[2], w_out.shape[2]
    tokens = tables[0].shape[2]
    outs = [
        jax.ShapeDtypeStruct(slab.shape, jnp.bfloat16),
        jax.ShapeDtypeStruct((2 * tokens, slots), jnp.bfloat16),
    ]
    scratch = [
        pltpu.VMEM((slots, width), jnp.bfloat16),
        pltpu.VMEM((slots, ff), jnp.bfloat16),
        pltpu.VMEM(slab.shape, jnp.bfloat16),
    ]
    if layer + 1 < layers:
        outs.append(jax.ShapeDtypeStruct((rows, tokens * PIECES), jnp.bfloat16))
        scratch.insert(0, pltpu.VMEM((slots, tokens * PIECES), jnp.float32))
    return pl.pallas_call(
        functools.partial(expert_kernel, layer),
        in_specs=[SM, SM] + [VM] * 6,
        out_specs=[VM] * len(outs),
        out_shape=outs,
        scratch_shapes=scratch,
        compiler_params=pltpu.CompilerParams(vmem_limit_bytes=20 * MIB),
        cost_estimate=pl.CostEstimate(
            flops=6 * slots * width * ff,
            bytes_accessed=6 * width * ff + 4 * slots * width,
            transcendentals=slots * ff,
        ),
        name="expert",
    )(in_scale, out_scale, slab, w_in, w_out, *tables)


def hbm(array):
    return pltpu.with_memory_space_constraint(array, pltpu.HBM)


def exchange(slab, devices):
    split = slab.reshape(devices, slab.shape[0] // devices, slab.shape[1])
    moved = lax.all_to_all(split, AXES, split_axis=0, concat_axis=0, tiled=True)
    return moved.reshape(slab.shape)


def shards(tokens, norm_gain, routes, gates, placement, w_in, in_scale, w_out, out_scale):
    count, width = tokens.shape
    layers, devices = placement.shape
    slots = devices * CAP
    piece = width // PIECES
    routes_t = jnp.swapaxes(routes, 1, 2)
    gates_t = jnp.swapaxes(gates, 1, 2)
    slab_type = jax.ShapeDtypeStruct((slots * PIECES, piece), jnp.bfloat16)
    stream_type = jax.ShapeDtypeStruct((count, width), jnp.bfloat16)
    rows = pltpu.VMEM((slots, width), jnp.bfloat16)
    wide = pltpu.VMEM((slots, count * PIECES), jnp.float32)
    spread = pltpu.VMEM((slots * PIECES, count * PIECES), jnp.bfloat16)
    params = pltpu.CompilerParams(vmem_limit_bytes=12 * MIB)

    small = (
        pltpu.VMEM((count, width), jnp.bfloat16),
        pltpu.VMEM(norm_gain.shape, jnp.float32),
        pltpu.VMEM(routes_t.shape, jnp.int32),
        pltpu.VMEM(placement.shape, jnp.int32),
    )
    slab = pl.pallas_call(
        first_kernel,
        in_specs=[HB] * 4,
        out_specs=VM,
        out_shape=slab_type,
        scratch_shapes=[*small, wide, spread, pltpu.SemaphoreType.DMA((4,))],
        compiler_params=params,
        cost_estimate=pl.CostEstimate(
            flops=8 * 10**9, bytes_accessed=8 * 10**6, transcendentals=0
        ),
        name="first",
    )(*[hbm(a) for a in (tokens, norm_gain, routes_t, placement)])
    weights = (
        w_in,
        jnp.transpose(in_scale, (0, 3, 1, 2)),
        w_out,
        jnp.transpose(out_scale, (0, 2, 1, 3)),
    )
    stream = tokens
    for layer in range(layers):
        answers, weight, *spreads = expert(
            layer, layers, exchange(slab, devices), weights, (routes_t, gates_t, placement)
        )
        back = exchange(answers, devices)
        if layer + 1 < layers:
            slab, stream = pl.pallas_call(
                functools.partial(middle_kernel, layer),
                in_specs=[VM] * 5,
                out_specs=(VM, VM),
                out_shape=(slab_type, stream_type),
                scratch_shapes=[rows],
                compiler_params=params,
                name="middle",
            )(back, stream, norm_gain, weight, spreads[0])
        else:
            stream = pl.pallas_call(
                last_kernel,
                in_specs=[VM] * 3,
                out_specs=VM,
                out_shape=stream_type,
                scratch_shapes=[rows],
                compiler_params=params,
                name="last",
            )(back, stream, weight)
    return stream


def solution(mesh):
    return jax.shard_map(
        shards,
        mesh=mesh,
        in_specs=(
            P(AXES, None),
            P(),
            P(None, AXES, None),
            P(None, AXES, None),
            P(),
            P(None, AXES, None, None),
            P(None, AXES, None, None),
            P(None, AXES, None, None),
            P(None, AXES, None, None),
        ),
        out_specs=P(AXES, None),
        check_vma=False,
    )
```

```python
import functools

import jax
import jax.numpy as jnp
from jax import lax
from jax.experimental import pallas as pl
from jax.experimental.pallas import tpu as pltpu
from jax.sharding import PartitionSpec as P

AXES = ("dp", "expert")
QBLK = 128
CAP = 3
PIECES = 8
GROUP = 32
EPS = 1e-06
MIB = 1 << 20


def fold_matrix():
    row = lax.broadcasted_iota(jnp.int32, (GROUP * PIECES, GROUP * PIECES), 0)
    col = lax.broadcasted_iota(jnp.int32, (GROUP * PIECES, GROUP * PIECES), 1)
    return jnp.where(col == (row & (PIECES - 1)) * GROUP + (row >> 3), 1.0, 0.0).astype(jnp.bfloat16)


def unfold_matrix():
    row = lax.broadcasted_iota(jnp.int32, (GROUP * PIECES, GROUP * PIECES), 0)
    col = lax.broadcasted_iota(jnp.int32, (GROUP * PIECES, GROUP * PIECES), 1)
    return jnp.where(col == (row & (GROUP - 1)) * PIECES + (row >> 5), 1.0, 0.0).astype(jnp.bfloat16)


def unfold_rows(slab_ref, rows_ref):
    piece = slab_ref.shape[1]
    span = GROUP * PIECES
    unfold = unfold_matrix()
    for b in range(slab_ref.shape[0] // span):
        block = jnp.dot(
            unfold, slab_ref[b * span : (b + 1) * span, :], preferred_element_type=jnp.float32
        ).astype(jnp.bfloat16)
        for p in range(PIECES):
            rows_ref[b * GROUP : (b + 1) * GROUP, p * piece : (p + 1) * piece] = block[
                p * GROUP : (p + 1) * GROUP
            ]


def fold_rows(stack_ref, slab_ref):
    span = GROUP * PIECES
    fold = fold_matrix()
    for b in range(slab_ref.shape[0] // span):
        slab_ref[b * span : (b + 1) * span, :] = jnp.dot(
            fold, stack_ref[b * span : (b + 1) * span, :], preferred_element_type=jnp.float32
        ).astype(jnp.bfloat16)


def stack_piece(stack_ref, values, p):
    span = GROUP * PIECES
    for b in range(values.shape[0] // GROUP):
        stack_ref[b * span + p * GROUP : b * span + (p + 1) * GROUP, :] = values[
            b * GROUP : (b + 1) * GROUP
        ]


def slot_tables(routes_t, place_row, gates_t):
    tokens = routes_t.shape[1]
    devices = place_row.shape[1]
    slots = devices * CAP
    home = lax.broadcasted_iota(jnp.int32, (devices, slots), 0)
    slot = lax.broadcasted_iota(jnp.int32, (devices, slots), 1)
    low = home * CAP
    widen = jnp.where((slot >= low) & (slot < low + CAP), 1.0, 0.0).astype(jnp.bfloat16)
    place = jnp.dot(
        jnp.broadcast_to(place_row.astype(jnp.float32), (8, devices)).astype(jnp.bfloat16),
        widen,
        preferred_element_type=jnp.float32,
    )[:1]
    rank_of = jnp.dot(
        jnp.broadcast_to(
            lax.broadcasted_iota(jnp.int32, (1, devices), 1).astype(jnp.float32), (8, devices)
        ).astype(jnp.bfloat16),
        widen,
        preferred_element_type=jnp.float32,
    )[:1]
    order = lax.broadcasted_iota(jnp.int32, (1, slots), 1).astype(jnp.float32) - rank_of * CAP
    chosen = jnp.transpose(routes_t.astype(jnp.float32))
    gate = None if gates_t is None else jnp.transpose(gates_t)
    taken = jnp.zeros((tokens, slots), jnp.float32)
    weight = jnp.zeros((tokens, slots), jnp.float32)
    for k in range(chosen.shape[1]):
        same = chosen[:, k : k + 1] == place
        taken = jnp.where(same, 1.0, taken)
        if gate is not None:
            weight = jnp.where(same, gate[:, k : k + 1], weight)
    later = lax.broadcasted_iota(jnp.int32, (tokens, tokens), 0)
    earlier = lax.broadcasted_iota(jnp.int32, (tokens, tokens), 1)
    before = jnp.where(earlier < later, 1.0, 0.0).astype(jnp.bfloat16)
    ranks = jnp.dot(before, taken.astype(jnp.bfloat16), preferred_element_type=jnp.float32)
    mine = ranks == order
    return jnp.where(mine, taken, 0.0), jnp.where(mine, weight, 0.0)


def normalise(stream_f, gain):
    scale = lax.rsqrt(jnp.mean(stream_f * stream_f, axis=-1, keepdims=True) + EPS)
    return (stream_f * scale * gain).astype(jnp.bfloat16)


def build_spread(select, wide_ref, spread_ref):
    tokens, slots = select.shape
    lanes = tokens * PIECES
    token = lax.broadcasted_iota(jnp.int32, (tokens, lanes), 0)
    lane = lax.broadcasted_iota(jnp.int32, (tokens, lanes), 1)
    tile = jnp.where((lane & (tokens - 1)) == token, 1.0, 0.0).astype(jnp.bfloat16)
    wide_ref[...] = jnp.dot(
        jnp.transpose(select).astype(jnp.bfloat16), tile, preferred_element_type=jnp.float32
    )
    own = lax.broadcasted_iota(jnp.int32, (PIECES, lanes), 0)
    piece = lax.broadcasted_iota(jnp.int32, (PIECES, lanes), 1) // tokens
    mine = own == piece
    for s in range(0, slots, 2):
        pair = [
            jnp.where(mine, jnp.broadcast_to(wide_ref[i : i + 1, :], (PIECES, lanes)), 0.0)
            for i in (s, s + 1)
        ]
        spread_ref[s * PIECES : (s + 2) * PIECES, :] = jnp.concatenate(pair, axis=0).astype(
            jnp.bfloat16
        )


def send_rows(spread_ref, normed, slab_ref):
    piece = slab_ref.shape[1]
    stacked = jnp.concatenate(
        [normed[:, p * piece : (p + 1) * piece] for p in range(PIECES)], axis=0
    )
    span = GROUP * PIECES
    for b in range(slab_ref.shape[0] // span):
        at = slice(b * span, (b + 1) * span)
        slab_ref[at, :] = jnp.dot(
            spread_ref[at, :], stacked, preferred_element_type=jnp.float32
        ).astype(jnp.bfloat16)


def split_weight(weight):
    high = weight.astype(jnp.bfloat16)
    low = (weight - high.astype(jnp.float32)).astype(jnp.bfloat16)
    return jnp.concatenate([high, low], axis=0)


def mix(weight, rows_ref):
    both = jnp.dot(weight, rows_ref[...], preferred_element_type=jnp.float32)
    tokens = weight.shape[0] // 2
    return both[:tokens] + both[tokens:]


def first_kernel(
    tokens_hbm, gain_hbm, routes_hbm, place_hbm, slab_ref,
    tokens_ref, gain_ref, routes_ref, place_ref, wide_ref, spread_ref, sems,
):
    loads = [
        pltpu.make_async_copy(src, dst, sems.at[i])
        for i, (src, dst) in enumerate(
            (
                (routes_hbm, routes_ref),
                (place_hbm, place_ref),
                (tokens_hbm, tokens_ref),
                (gain_hbm, gain_ref),
            )
        )
    ]
    for load in loads:
        load.start()
    loads[0].wait()
    loads[1].wait()
    select, _ = slot_tables(routes_ref[0], place_ref[0:1, :], None)
    build_spread(select, wide_ref, spread_ref)
    loads[2].wait()
    loads[3].wait()
    normed = normalise(tokens_ref[...].astype(jnp.float32), gain_ref[0:1, :])
    send_rows(spread_ref, normed, slab_ref)


def middle_kernel(
    layer, slab_in, stream_hbm, gain_hbm, weight_hbm, spread_hbm, slab_ref, out_ref,
    rows_ref, stream_ref, gain_ref, weight_ref, spread_ref, sems,
):
    loads = [
        pltpu.make_async_copy(src, dst, sems.at[i])
        for i, (src, dst) in enumerate(
            (
                (weight_hbm, weight_ref),
                (stream_hbm, stream_ref),
                (gain_hbm, gain_ref),
                (spread_hbm, spread_ref),
            )
        )
    ]
    for load in loads:
        load.start()
    unfold_rows(slab_in, rows_ref)
    loads[0].wait()
    mixed = mix(weight_ref[...], rows_ref)
    loads[1].wait()
    loads[2].wait()
    stream = (stream_ref[...].astype(jnp.float32) + mixed).astype(jnp.bfloat16)
    out_ref[...] = stream
    normed = normalise(stream.astype(jnp.float32), gain_ref[layer + 1 : layer + 2, :])
    loads[3].wait()
    send_rows(spread_ref, normed, slab_ref)


def last_kernel(slab_in, stream_ref, weight_ref, out_ref, rows_ref):
    unfold_rows(slab_in, rows_ref)
    mixed = mix(weight_ref[...], rows_ref)
    out_ref[...] = (stream_ref[...].astype(jnp.float32) + mixed).astype(jnp.bfloat16)


def block_weight(w_ref, factor, layer, first, count):
    lines = []
    for i in range(w_ref.shape[2] // QBLK):
        line = [
            (
                w_ref[layer, 0, i * QBLK : (i + 1) * QBLK, j * QBLK : (j + 1) * QBLK].astype(
                    jnp.float32
                )
                * factor(i, j)
            ).astype(jnp.bfloat16)
            for j in range(first // QBLK, (first + count) // QBLK)
        ]
        lines.append(jnp.concatenate(line, axis=1))
    return jnp.concatenate(lines, axis=0)


def expert_steps(slab_in, x_ref, hid, stack_ref, in_chunk, out_chunk):
    unfold_rows(slab_in, x_ref)
    chunk = slab_in.shape[1]
    chunks = hid.shape[1] // chunk
    for n in range(chunks):
        gate = jnp.dot(x_ref[...], in_chunk(n), preferred_element_type=jnp.float32)
        up = jnp.dot(x_ref[...], in_chunk(chunks + n), preferred_element_type=jnp.float32)
        hid[:, n * chunk : (n + 1) * chunk] = (gate / (1.0 + jnp.exp(-gate)) * up).astype(
            jnp.bfloat16
        )
    for m in range(PIECES):
        answer = jnp.dot(hid[...], out_chunk(m), preferred_element_type=jnp.float32).astype(
            jnp.bfloat16
        )
        stack_piece(stack_ref, answer, m)


def first_expert_kernel(
    layer, in_scale, out_scale, slab_in, w_in, w_out, slab_hbm,
    x_ref, hid, stack_ref, slab_ref, sems,
):
    chunk = slab_in.shape[1]
    expert_steps(
        slab_in, x_ref, hid, stack_ref,
        lambda n: block_weight(
            w_in, lambda i, j: in_scale[layer, j, 0, i], layer, n * chunk, chunk
        ),
        lambda m: block_weight(
            w_out, lambda i, j: out_scale[layer, i, 0, j], layer, m * chunk, chunk
        ),
    )
    span = GROUP * PIECES
    fold = fold_matrix()
    stores = []
    blocks = slab_ref.shape[0] // span
    for b in range(blocks):
        at = slice(b * span, (b + 1) * span)
        slab_ref[at, :] = jnp.dot(
            fold, stack_ref[at, :], preferred_element_type=jnp.float32
        ).astype(jnp.bfloat16)
        if b % 3 == 2:
            rows = pl.ds((b - 2) * span, 3 * span)
            store = pltpu.make_async_copy(
                slab_ref.at[rows, :], slab_hbm.at[rows, :], sems.at[b // 3]
            )
            store.start()
            stores.append(store)
    for store in stores:
        store.wait()


def expert_kernel(slab_in, win, wout, slab_ref, x_ref, hid, stack_ref):
    expert_steps(
        slab_in, x_ref, hid, stack_ref, lambda c: win[c], lambda c: wout[c]
    )
    fold_rows(stack_ref, slab_ref)


def prepare_kernel(
    layer, in_scale, out_scale, w_in, w_out, routes_ref, gates_ref, place_ref, after,
    win_hbm, wout_hbm, weight_ref, spread_hbm, next_ref,
    win, wout, wide_ref, spread_ref, load_sems, in_sems, out_sems, spread_sem,
):
    del after
    rows = 2 * QBLK
    chunk = win_hbm.shape[2]
    loads = []
    for src, buf, dst, sems, inner in (
        (w_in, win, win_hbm, in_sems, True),
        (w_out, wout, wout_hbm, out_sems, False),
    ):
        for r in range(buf.shape[0] // rows):
            span = pl.ds(r * rows, rows)
            load = pltpu.make_async_copy(
                src.at[layer, 0, span, :], buf.at[span, :], load_sems.at[len(loads)]
            )
            load.start()
            loads.append((load, buf, dst, sems, inner, r))
    select, weight = slot_tables(
        routes_ref[layer], place_ref[layer : layer + 1, :], gates_ref[layer]
    )
    next_ref[...] = split_weight(weight)
    _, weight = slot_tables(
        routes_ref[layer - 1], place_ref[layer - 1 : layer, :], gates_ref[layer - 1]
    )
    weight_ref[...] = split_weight(weight)
    build_spread(select, wide_ref, spread_ref)
    stores = [pltpu.make_async_copy(spread_ref, spread_hbm, spread_sem)]
    stores[0].start()
    for load, buf, dst, sems, inner, r in loads:
        load.wait()
        for i in range(rows // QBLK):
            for j in range(buf.shape[1] // QBLK):
                at = (
                    slice(r * rows + i * QBLK, r * rows + (i + 1) * QBLK),
                    slice(j * QBLK, (j + 1) * QBLK),
                )
                block = r * (rows // QBLK) + i
                factor = in_scale[layer, j, 0, block] if inner else out_scale[layer, block, 0, j]
                buf[at] = (buf[at].astype(jnp.float32) * factor).astype(jnp.bfloat16)
        for c in range(dst.shape[0]):
            store = pltpu.make_async_copy(
                buf.at[pl.ds(r * rows, rows), pl.ds(c * chunk, chunk)],
                dst.at[c, pl.ds(r * rows, rows), :],
                sems.at[r, c],
            )
            store.start()
            stores.append(store)
    for store in stores:
        store.wait()


VM = pl.BlockSpec(memory_space=pltpu.VMEM)
SM = pl.BlockSpec(memory_space=pltpu.SMEM)
HB = pl.BlockSpec(memory_space=pltpu.HBM)


def expert_cost(slots, width, ff):
    return pl.CostEstimate(
        flops=6 * slots * width * ff,
        bytes_accessed=6 * width * ff + 4 * slots * width,
        transcendentals=slots * ff,
    )


def first_expert(slab, weights):
    w_in, in_scale, w_out, out_scale = weights
    rows, piece = slab.shape
    slots = rows // PIECES
    width, ff = w_in.shape[2], w_out.shape[2]
    return pl.pallas_call(
        functools.partial(first_expert_kernel, 0),
        in_specs=[SM, SM, VM, VM, VM],
        out_specs=HB,
        out_shape=pltpu.HBM(slab.shape, jnp.bfloat16),
        scratch_shapes=[
            pltpu.VMEM((slots, width), jnp.bfloat16),
            pltpu.VMEM((slots, ff), jnp.bfloat16),
            pltpu.VMEM(slab.shape, jnp.bfloat16),
            pltpu.VMEM(slab.shape, jnp.bfloat16),
            pltpu.SemaphoreType.DMA((rows // (3 * GROUP * PIECES),)),
        ],
        compiler_params=pltpu.CompilerParams(vmem_limit_bytes=20 * MIB),
        cost_estimate=expert_cost(slots, width, ff),
        name="first_expert",
    )(in_scale, out_scale, slab, w_in, w_out)


def expert(slab, win, wout):
    rows, piece = slab.shape
    slots = rows // PIECES
    width, ff = win.shape[1], wout.shape[1]
    return pl.pallas_call(
        expert_kernel,
        in_specs=[VM] * 3,
        out_specs=VM,
        out_shape=jax.ShapeDtypeStruct(slab.shape, jnp.bfloat16),
        scratch_shapes=[
            pltpu.VMEM((slots, width), jnp.bfloat16),
            pltpu.VMEM((slots, ff), jnp.bfloat16),
            pltpu.VMEM(slab.shape, jnp.bfloat16),
        ],
        compiler_params=pltpu.CompilerParams(vmem_limit_bytes=20 * MIB),
        cost_estimate=expert_cost(slots, width, ff),
        name="expert",
    )(slab, win, wout)


def prepare(layer, weights, tables, slots, chunk, after):
    w_in, in_scale, w_out, out_scale = weights
    tokens = tables[0].shape[2]
    width, gated = w_in.shape[2:]
    ff = w_out.shape[2]
    rows = 2 * QBLK
    size = width * gated + ff * width
    spread = (slots * PIECES, tokens * PIECES)
    return pl.pallas_call(
        functools.partial(prepare_kernel, layer),
        in_specs=[SM, SM, HB, HB, VM, VM, VM, HB],
        out_specs=[HB, HB, VM, HB, VM],
        out_shape=[
            pltpu.HBM((gated // chunk, width, chunk), jnp.bfloat16),
            pltpu.HBM((width // chunk, ff, chunk), jnp.bfloat16),
            jax.ShapeDtypeStruct((2 * tokens, slots), jnp.bfloat16),
            pltpu.HBM(spread, jnp.bfloat16),
            jax.ShapeDtypeStruct((2 * tokens, slots), jnp.bfloat16),
        ],
        scratch_shapes=[
            pltpu.VMEM((width, gated), jnp.bfloat16),
            pltpu.VMEM((ff, width), jnp.bfloat16),
            pltpu.VMEM((slots, tokens * PIECES), jnp.float32),
            pltpu.VMEM(spread, jnp.bfloat16),
            pltpu.SemaphoreType.DMA(((width + ff) // rows,)),
            pltpu.SemaphoreType.DMA((width // rows, gated // chunk)),
            pltpu.SemaphoreType.DMA((ff // rows, width // chunk)),
            pltpu.SemaphoreType.DMA,
        ],
        compiler_params=pltpu.CompilerParams(vmem_limit_bytes=24 * MIB),
        cost_estimate=pl.CostEstimate(flops=size, bytes_accessed=4 * size, transcendentals=0),
        name="prepare",
    )(in_scale, out_scale, hbm(w_in), hbm(w_out), *tables, after)


def hbm(array):
    return pltpu.with_memory_space_constraint(array, pltpu.HBM)


def exchange(slab, devices):
    split = slab.reshape(devices, slab.shape[0] // devices, slab.shape[1])
    moved = lax.all_to_all(split, AXES, split_axis=0, concat_axis=0, tiled=True)
    return moved.reshape(slab.shape)


def shards(tokens, norm_gain, routes, gates, placement, w_in, in_scale, w_out, out_scale):
    count, width = tokens.shape
    layers, devices = placement.shape
    slots = devices * CAP
    piece = width // PIECES
    routes_t = jnp.swapaxes(routes, 1, 2)
    gates_t = jnp.swapaxes(gates, 1, 2)
    slab_type = jax.ShapeDtypeStruct((slots * PIECES, piece), jnp.bfloat16)
    stream_type = jax.ShapeDtypeStruct((count, width), jnp.bfloat16)
    rows = pltpu.VMEM((slots, width), jnp.bfloat16)
    wide = pltpu.VMEM((slots, count * PIECES), jnp.float32)
    scatter = pltpu.VMEM((slots * PIECES, count * PIECES), jnp.bfloat16)
    params = pltpu.CompilerParams(vmem_limit_bytes=12 * MIB)

    small = (
        pltpu.VMEM((count, width), jnp.bfloat16),
        pltpu.VMEM(norm_gain.shape, jnp.float32),
        pltpu.VMEM(routes_t.shape, jnp.int32),
        pltpu.VMEM(placement.shape, jnp.int32),
    )
    slab = pl.pallas_call(
        first_kernel,
        in_specs=[HB] * 4,
        out_specs=VM,
        out_shape=slab_type,
        scratch_shapes=[*small, wide, scatter, pltpu.SemaphoreType.DMA((4,))],
        compiler_params=params,
        cost_estimate=pl.CostEstimate(
            flops=8 * 10**9, bytes_accessed=8 * 10**6, transcendentals=0
        ),
        name="first",
    )(*[hbm(a) for a in (tokens, norm_gain, routes_t, placement)])
    weights = (
        w_in,
        jnp.transpose(in_scale, (0, 3, 1, 2)),
        w_out,
        jnp.transpose(out_scale, (0, 2, 1, 3)),
    )
    stream = tokens
    tables = (routes_t, gates_t, placement)
    for layer in range(layers):
        arrived = exchange(slab, devices)
        answers = first_expert(arrived, weights) if layer == 0 else expert(arrived, win, wout)
        if layer + 1 < layers:
            win, wout, weight, spread, next_weight = prepare(
                layer + 1, weights, tables, slots, piece, answers
            )
        back = exchange(answers, devices)
        if layer + 1 < layers:
            slab, stream = pl.pallas_call(
                functools.partial(middle_kernel, layer),
                in_specs=[VM] + [HB] * 4,
                out_specs=(VM, VM),
                out_shape=(slab_type, stream_type),
                scratch_shapes=[
                    rows,
                    pltpu.VMEM((count, width), jnp.bfloat16),
                    pltpu.VMEM(norm_gain.shape, jnp.float32),
                    pltpu.VMEM(weight.shape, jnp.bfloat16),
                    pltpu.VMEM(spread.shape, jnp.bfloat16),
                    pltpu.SemaphoreType.DMA((4,)),
                ],
                compiler_params=params,
                cost_estimate=pl.CostEstimate(
                    flops=8 * 10**9, bytes_accessed=8 * 10**6, transcendentals=0
                ),
                name="middle",
            )(back, hbm(stream), hbm(norm_gain), hbm(weight), hbm(spread))
        else:
            stream = pl.pallas_call(
                last_kernel,
                in_specs=[VM] * 3,
                out_specs=VM,
                out_shape=stream_type,
                scratch_shapes=[rows],
                compiler_params=params,
                name="last",
            )(back, stream, next_weight)
    return stream


def solution(mesh):
    return jax.shard_map(
        shards,
        mesh=mesh,
        in_specs=(
            P(AXES, None),
            P(),
            P(None, AXES, None),
            P(None, AXES, None),
            P(),
            P(None, AXES, None, None),
            P(None, AXES, None, None),
            P(None, AXES, None, None),
            P(None, AXES, None, None),
        ),
        out_specs=P(AXES, None),
        check_vma=False,
    )
```

```python
import functools

import jax
import jax.numpy as jnp
from jax import lax
from jax.experimental import pallas as pl
from jax.experimental.pallas import tpu as pltpu
from jax.sharding import PartitionSpec as P

AXES = ("dp", "expert")
QBLK = 128
CAP = 3
PIECES = 8
GROUP = 32
EPS = 1e-06
MIB = 1 << 20


def fold_matrix():
    row = lax.broadcasted_iota(jnp.int32, (GROUP * PIECES, GROUP * PIECES), 0)
    col = lax.broadcasted_iota(jnp.int32, (GROUP * PIECES, GROUP * PIECES), 1)
    return jnp.where(col == (row & (PIECES - 1)) * GROUP + (row >> 3), 1.0, 0.0).astype(jnp.bfloat16)


def unfold_matrix():
    row = lax.broadcasted_iota(jnp.int32, (GROUP * PIECES, GROUP * PIECES), 0)
    col = lax.broadcasted_iota(jnp.int32, (GROUP * PIECES, GROUP * PIECES), 1)
    return jnp.where(col == (row & (GROUP - 1)) * PIECES + (row >> 5), 1.0, 0.0).astype(jnp.bfloat16)


def unfold_rows(slab_ref, rows_ref):
    piece = slab_ref.shape[1]
    span = GROUP * PIECES
    unfold = unfold_matrix()
    for b in range(slab_ref.shape[0] // span):
        block = jnp.dot(
            unfold, slab_ref[b * span : (b + 1) * span, :], preferred_element_type=jnp.float32
        ).astype(jnp.bfloat16)
        for p in range(PIECES):
            rows_ref[b * GROUP : (b + 1) * GROUP, p * piece : (p + 1) * piece] = block[
                p * GROUP : (p + 1) * GROUP
            ]


def fold_rows(stack_ref, slab_ref):
    span = GROUP * PIECES
    fold = fold_matrix()
    for b in range(slab_ref.shape[0] // span):
        slab_ref[b * span : (b + 1) * span, :] = jnp.dot(
            fold, stack_ref[b * span : (b + 1) * span, :], preferred_element_type=jnp.float32
        ).astype(jnp.bfloat16)


def stack_piece(stack_ref, values, p):
    span = GROUP * PIECES
    for b in range(values.shape[0] // GROUP):
        stack_ref[b * span + p * GROUP : b * span + (p + 1) * GROUP, :] = values[
            b * GROUP : (b + 1) * GROUP
        ]


def slot_tables(routes_t, place_row, gates_t):
    tokens = routes_t.shape[1]
    devices = place_row.shape[1]
    slots = devices * CAP
    home = lax.broadcasted_iota(jnp.int32, (devices, slots), 0)
    slot = lax.broadcasted_iota(jnp.int32, (devices, slots), 1)
    low = home * CAP
    widen = jnp.where((slot >= low) & (slot < low + CAP), 1.0, 0.0).astype(jnp.bfloat16)
    place = jnp.dot(
        jnp.broadcast_to(place_row.astype(jnp.float32), (8, devices)).astype(jnp.bfloat16),
        widen,
        preferred_element_type=jnp.float32,
    )[:1]
    rank_of = jnp.dot(
        jnp.broadcast_to(
            lax.broadcasted_iota(jnp.int32, (1, devices), 1).astype(jnp.float32), (8, devices)
        ).astype(jnp.bfloat16),
        widen,
        preferred_element_type=jnp.float32,
    )[:1]
    order = lax.broadcasted_iota(jnp.int32, (1, slots), 1).astype(jnp.float32) - rank_of * CAP
    chosen = jnp.transpose(routes_t.astype(jnp.float32))
    gate = None if gates_t is None else jnp.transpose(gates_t)
    taken = jnp.zeros((tokens, slots), jnp.float32)
    weight = jnp.zeros((tokens, slots), jnp.float32)
    for k in range(chosen.shape[1]):
        same = chosen[:, k : k + 1] == place
        taken = jnp.where(same, 1.0, taken)
        if gate is not None:
            weight = jnp.where(same, gate[:, k : k + 1], weight)
    later = lax.broadcasted_iota(jnp.int32, (tokens, tokens), 0)
    earlier = lax.broadcasted_iota(jnp.int32, (tokens, tokens), 1)
    before = jnp.where(earlier < later, 1.0, 0.0).astype(jnp.bfloat16)
    ranks = jnp.dot(before, taken.astype(jnp.bfloat16), preferred_element_type=jnp.float32)
    mine = ranks == order
    return jnp.where(mine, taken, 0.0), jnp.where(mine, weight, 0.0)


def normalise(stream_f, gain):
    scale = lax.rsqrt(jnp.mean(stream_f * stream_f, axis=-1, keepdims=True) + EPS)
    return (stream_f * scale * gain).astype(jnp.bfloat16)


def send_rows(pick, normed, stack_ref, slab_ref):
    piece = slab_ref.shape[1]
    for p in range(PIECES):
        rows = jnp.dot(
            pick, normed[:, p * piece : (p + 1) * piece], preferred_element_type=jnp.float32
        ).astype(jnp.bfloat16)
        stack_piece(stack_ref, rows, p)
    fold_rows(stack_ref, slab_ref)


def slot_numbers(routes_t, place_row):
    choices, tokens = routes_t.shape
    devices = place_row.shape[1]
    place = place_row.astype(jnp.float32)
    chosen = jnp.transpose(routes_t.astype(jnp.float32))
    same = [chosen[:, k : k + 1] == place for k in range(choices)]
    taken = jnp.zeros((tokens, devices), jnp.float32)
    for k in range(choices):
        taken = jnp.where(same[k], 1.0, taken)
    later = lax.broadcasted_iota(jnp.int32, (tokens, tokens), 0)
    earlier = lax.broadcasted_iota(jnp.int32, (tokens, tokens), 1)
    before = jnp.where(earlier < later, 1.0, 0.0).astype(jnp.bfloat16)
    ranks = jnp.dot(before, taken.astype(jnp.bfloat16), preferred_element_type=jnp.float32)
    home = lax.broadcasted_iota(jnp.int32, (tokens, devices), 1).astype(jnp.float32)
    number = home * CAP + ranks
    column = lax.broadcasted_iota(jnp.int32, (tokens, choices), 1)
    slots = jnp.zeros((tokens, choices), jnp.float32)
    for k in range(choices):
        found = jnp.sum(jnp.where(same[k], number, 0.0), axis=1, keepdims=True)
        slots = jnp.where(column == k, found, slots)
    return jnp.transpose(slots).astype(jnp.int32)


def mix_blocks(layer, slots_ref, gates_ref, back_ref, mixed_ref):
    for t in range(mixed_ref.shape[0]):
        total = None
        for k in range(gates_ref.shape[1]):
            block = back_ref[slots_ref[layer, k, t]].astype(jnp.float32) * gates_ref[layer, k, t]
            total = block if total is None else total + block
        mixed_ref[t] = total


def first_kernel(
    tokens_hbm, gain_hbm, routes_hbm, place_hbm, slab_ref, slots_ref,
    tokens_ref, gain_ref, routes_ref, place_ref, stack_ref, sems,
):
    loads = [
        pltpu.make_async_copy(src, dst, sems.at[i])
        for i, (src, dst) in enumerate(
            (
                (routes_hbm, routes_ref),
                (place_hbm, place_ref),
                (tokens_hbm, tokens_ref),
                (gain_hbm, gain_ref),
            )
        )
    ]
    for load in loads:
        load.start()
    loads[0].wait()
    loads[1].wait()
    select, _ = slot_tables(routes_ref[0], place_ref[0:1, :], None)
    pick = jnp.transpose(select).astype(jnp.bfloat16)
    loads[2].wait()
    loads[3].wait()
    normed = normalise(tokens_ref[...].astype(jnp.float32), gain_ref[0:1, :])
    send_rows(pick, normed, stack_ref, slab_ref)
    for layer in range(routes_ref.shape[0]):
        slots_ref[layer] = slot_numbers(routes_ref[layer], place_ref[layer : layer + 1, :])


def blocks_of(stream_ref, stack_ref):
    piece = stack_ref.shape[1]
    for p in range(PIECES):
        stack_ref[p * GROUP : (p + 1) * GROUP, :] = stream_ref[:, p * piece : (p + 1) * piece]
    return jnp.dot(fold_matrix(), stack_ref[...], preferred_element_type=jnp.float32)


def middle_kernel(
    layer, first, slots_ref, gates_ref, back_ref, stream_ref, gain_ref,
    slab_ref, out_ref, mixed_ref, gain_rows, stack_ref,
):
    slab_ref[...] = jnp.zeros(slab_ref.shape, jnp.bfloat16)
    tokens, pieces, piece = mixed_ref.shape
    if first:
        blocks = blocks_of(stream_ref, stack_ref)
    else:
        blocks = stream_ref[...].astype(jnp.float32)
    for p in range(pieces):
        gain_rows[p : p + 1, :] = gain_ref[
            layer + 1 : layer + 2, p * piece : (p + 1) * piece
        ]
    mix_blocks(layer, slots_ref, gates_ref, back_ref, mixed_ref)
    stream = (blocks + mixed_ref[...].reshape(tokens * pieces, piece)).astype(jnp.bfloat16)
    out_ref[...] = stream
    wide = stream.astype(jnp.float32).reshape(tokens, pieces, piece)
    total = jnp.sum(jnp.sum(wide * wide, axis=2, keepdims=True), axis=1, keepdims=True)
    scale = lax.rsqrt(total / (pieces * piece) + EPS)
    mixed_ref[...] = wide * scale * gain_rows[...][None]
    for t in range(tokens):
        row = mixed_ref[t].astype(jnp.bfloat16)
        for k in range(slots_ref.shape[1]):
            slab_ref[slots_ref[layer + 1, k, t]] = row


def last_kernel(
    layer, slots_ref, gates_ref, back_ref, stream_ref, out_ref, mixed_ref
):
    tokens, pieces, piece = mixed_ref.shape
    mix_blocks(layer, slots_ref, gates_ref, back_ref, mixed_ref)
    stream = (
        stream_ref[...].astype(jnp.float32) + mixed_ref[...].reshape(tokens * pieces, piece)
    ).astype(jnp.bfloat16)
    rows = jnp.dot(unfold_matrix(), stream, preferred_element_type=jnp.float32).astype(
        jnp.bfloat16
    )
    for p in range(pieces):
        out_ref[:, p * piece : (p + 1) * piece] = rows[p * tokens : (p + 1) * tokens]


def block_weight(w_ref, factor, layer, first, count):
    lines = []
    for i in range(w_ref.shape[2] // QBLK):
        line = [
            (
                w_ref[layer, 0, i * QBLK : (i + 1) * QBLK, j * QBLK : (j + 1) * QBLK].astype(
                    jnp.float32
                )
                * factor(i, j)
            ).astype(jnp.bfloat16)
            for j in range(first // QBLK, (first + count) // QBLK)
        ]
        lines.append(jnp.concatenate(line, axis=1))
    return jnp.concatenate(lines, axis=0)


def expert_kernel(
    layer, in_scale, out_scale, slab_in, w_in, w_out, slab_ref, x_ref, hid, stack_ref
):
    def into(first, count):
        return block_weight(w_in, lambda i, j: in_scale[layer, j, 0, i], layer, first, count)

    def out_of(first, count):
        return block_weight(w_out, lambda i, j: out_scale[layer, i, 0, j], layer, first, count)

    unfold_rows(slab_in, x_ref)
    ff = w_out.shape[2]
    chunk = slab_ref.shape[1]
    for n in range(ff // chunk):
        gate = jnp.dot(x_ref[...], into(n * chunk, chunk), preferred_element_type=jnp.float32)
        up = jnp.dot(x_ref[...], into(ff + n * chunk, chunk), preferred_element_type=jnp.float32)
        hid[:, n * chunk : (n + 1) * chunk] = (gate / (1.0 + jnp.exp(-gate)) * up).astype(
            jnp.bfloat16
        )
    for m in range(PIECES):
        answer = jnp.dot(
            hid[...], out_of(m * chunk, chunk), preferred_element_type=jnp.float32
        ).astype(jnp.bfloat16)
        stack_piece(stack_ref, answer, m)
    fold_rows(stack_ref, slab_ref)


VM = pl.BlockSpec(memory_space=pltpu.VMEM)
SM = pl.BlockSpec(memory_space=pltpu.SMEM)
HB = pl.BlockSpec(memory_space=pltpu.HBM)


def expert(layer, slab, weights):
    w_in, in_scale, w_out, out_scale = weights
    rows, piece = slab.shape
    slots = rows // PIECES
    width, ff = w_in.shape[2], w_out.shape[2]
    return pl.pallas_call(
        functools.partial(expert_kernel, layer),
        in_specs=[SM, SM, VM, VM, VM],
        out_specs=VM,
        out_shape=jax.ShapeDtypeStruct(slab.shape, jnp.bfloat16),
        scratch_shapes=[
            pltpu.VMEM((slots, width), jnp.bfloat16),
            pltpu.VMEM((slots, ff), jnp.bfloat16),
            pltpu.VMEM(slab.shape, jnp.bfloat16),
        ],
        compiler_params=pltpu.CompilerParams(vmem_limit_bytes=20 * MIB),
        cost_estimate=pl.CostEstimate(
            flops=6 * slots * width * ff,
            bytes_accessed=6 * width * ff + 4 * slots * width,
            transcendentals=slots * ff,
        ),
        name="expert",
    )(in_scale, out_scale, slab, w_in, w_out)


def hbm(array):
    return pltpu.with_memory_space_constraint(array, pltpu.HBM)


def exchange(slab, devices):
    split = slab.reshape(devices, slab.shape[0] // devices, slab.shape[1])
    moved = lax.all_to_all(split, AXES, split_axis=0, concat_axis=0, tiled=True)
    return moved.reshape(slab.shape)


def shards(tokens, norm_gain, routes, gates, placement, w_in, in_scale, w_out, out_scale):
    count, width = tokens.shape
    layers, devices = placement.shape
    slots = devices * CAP
    piece = width // PIECES
    routes_t = jnp.swapaxes(routes, 1, 2)
    gates_t = jnp.swapaxes(gates, 1, 2)
    slab_type = jax.ShapeDtypeStruct((slots * PIECES, piece), jnp.bfloat16)
    slots_type = jax.ShapeDtypeStruct(routes_t.shape, jnp.int32)
    stream_type = jax.ShapeDtypeStruct((count, width), jnp.bfloat16)
    mixed = pltpu.VMEM((count, PIECES, piece), jnp.float32)
    stack = pltpu.VMEM((slots * PIECES, piece), jnp.bfloat16)
    params = pltpu.CompilerParams(vmem_limit_bytes=12 * MIB)

    small = (
        pltpu.VMEM((count, width), jnp.bfloat16),
        pltpu.VMEM(norm_gain.shape, jnp.float32),
        pltpu.VMEM(routes_t.shape, jnp.int32),
        pltpu.VMEM(placement.shape, jnp.int32),
    )
    slab, numbers = pl.pallas_call(
        first_kernel,
        in_specs=[HB] * 4,
        out_specs=(VM, VM),
        out_shape=(slab_type, slots_type),
        scratch_shapes=[*small, stack, pltpu.SemaphoreType.DMA((4,))],
        compiler_params=params,
        cost_estimate=pl.CostEstimate(
            flops=8 * 10**9, bytes_accessed=8 * 10**6, transcendentals=0
        ),
        name="first",
    )(*[hbm(a) for a in (tokens, norm_gain, routes_t, placement)])
    weights = (
        w_in,
        jnp.transpose(in_scale, (0, 3, 1, 2)),
        w_out,
        jnp.transpose(out_scale, (0, 2, 1, 3)),
    )
    stream = tokens
    for layer in range(layers):
        answers = expert(layer, exchange(slab, devices), weights)
        back = exchange(answers, devices).reshape(slots, PIECES, piece)
        if layer + 1 < layers:
            slab, stream = pl.pallas_call(
                functools.partial(middle_kernel, layer, layer == 0),
                in_specs=[SM, SM, VM, VM, VM],
                out_specs=(VM, VM),
                out_shape=(
                    jax.ShapeDtypeStruct(back.shape, jnp.bfloat16),
                    jax.ShapeDtypeStruct((count * PIECES, piece), jnp.bfloat16),
                ),
                scratch_shapes=[
                    mixed,
                    pltpu.VMEM((PIECES, piece), jnp.float32),
                    pltpu.VMEM((count * PIECES, piece), jnp.bfloat16),
                ],
                compiler_params=params,
                name="middle",
            )(numbers, gates_t, back, stream, norm_gain)
            slab = slab.reshape(slots * PIECES, piece)
        else:
            stream = pl.pallas_call(
                functools.partial(last_kernel, layer),
                in_specs=[SM, SM, VM, VM],
                out_specs=VM,
                out_shape=stream_type,
                scratch_shapes=[mixed],
                compiler_params=params,
                name="last",
            )(numbers, gates_t, back, stream)
    return stream


def solution(mesh):
    return jax.shard_map(
        shards,
        mesh=mesh,
        in_specs=(
            P(AXES, None),
            P(),
            P(None, AXES, None),
            P(None, AXES, None),
            P(),
            P(None, AXES, None, None),
            P(None, AXES, None, None),
            P(None, AXES, None, None),
            P(None, AXES, None, None),
        ),
        out_specs=P(AXES, None),
        check_vma=False,
    )
```

```python
import functools

import jax
import jax.numpy as jnp
from jax import lax
from jax.experimental import pallas as pl
from jax.experimental.pallas import tpu as pltpu
from jax.sharding import PartitionSpec as P

AXES = ("dp", "expert")
QBLK = 128
CAP = 3
PIECES = 8
GROUP = 32
EPS = 1e-06
MIB = 1 << 20


def fold_matrix():
    row = lax.broadcasted_iota(jnp.int32, (GROUP * PIECES, GROUP * PIECES), 0)
    col = lax.broadcasted_iota(jnp.int32, (GROUP * PIECES, GROUP * PIECES), 1)
    return jnp.where(col == (row & (PIECES - 1)) * GROUP + (row >> 3), 1.0, 0.0).astype(jnp.bfloat16)


def unfold_matrix():
    row = lax.broadcasted_iota(jnp.int32, (GROUP * PIECES, GROUP * PIECES), 0)
    col = lax.broadcasted_iota(jnp.int32, (GROUP * PIECES, GROUP * PIECES), 1)
    return jnp.where(col == (row & (GROUP - 1)) * PIECES + (row >> 5), 1.0, 0.0).astype(jnp.bfloat16)


def unfold_rows(slab_ref, rows_ref):
    piece = slab_ref.shape[1]
    span = GROUP * PIECES
    unfold = unfold_matrix()
    for b in range(slab_ref.shape[0] // span):
        block = jnp.dot(
            unfold, slab_ref[b * span : (b + 1) * span, :], preferred_element_type=jnp.float32
        ).astype(jnp.bfloat16)
        for p in range(PIECES):
            rows_ref[b * GROUP : (b + 1) * GROUP, p * piece : (p + 1) * piece] = block[
                p * GROUP : (p + 1) * GROUP
            ]


def fold_rows(stack_ref, slab_ref):
    span = GROUP * PIECES
    fold = fold_matrix()
    for b in range(slab_ref.shape[0] // span):
        slab_ref[b * span : (b + 1) * span, :] = jnp.dot(
            fold, stack_ref[b * span : (b + 1) * span, :], preferred_element_type=jnp.float32
        ).astype(jnp.bfloat16)


def stack_piece(stack_ref, values, p):
    span = GROUP * PIECES
    for b in range(values.shape[0] // GROUP):
        stack_ref[b * span + p * GROUP : b * span + (p + 1) * GROUP, :] = values[
            b * GROUP : (b + 1) * GROUP
        ]


def slot_tables(routes_t, place_row, gates_t):
    tokens = routes_t.shape[1]
    devices = place_row.shape[1]
    slots = devices * CAP
    home = lax.broadcasted_iota(jnp.int32, (devices, slots), 0)
    slot = lax.broadcasted_iota(jnp.int32, (devices, slots), 1)
    low = home * CAP
    widen = jnp.where((slot >= low) & (slot < low + CAP), 1.0, 0.0).astype(jnp.bfloat16)
    place = jnp.dot(
        jnp.broadcast_to(place_row.astype(jnp.float32), (8, devices)).astype(jnp.bfloat16),
        widen,
        preferred_element_type=jnp.float32,
    )[:1]
    rank_of = jnp.dot(
        jnp.broadcast_to(
            lax.broadcasted_iota(jnp.int32, (1, devices), 1).astype(jnp.float32), (8, devices)
        ).astype(jnp.bfloat16),
        widen,
        preferred_element_type=jnp.float32,
    )[:1]
    order = lax.broadcasted_iota(jnp.int32, (1, slots), 1).astype(jnp.float32) - rank_of * CAP
    chosen = jnp.transpose(routes_t.astype(jnp.float32))
    gate = None if gates_t is None else jnp.transpose(gates_t)
    taken = jnp.zeros((tokens, slots), jnp.float32)
    weight = jnp.zeros((tokens, slots), jnp.float32)
    for k in range(chosen.shape[1]):
        same = chosen[:, k : k + 1] == place
        taken = jnp.where(same, 1.0, taken)
        if gate is not None:
            weight = jnp.where(same, gate[:, k : k + 1], weight)
    later = lax.broadcasted_iota(jnp.int32, (tokens, tokens), 0)
    earlier = lax.broadcasted_iota(jnp.int32, (tokens, tokens), 1)
    before = jnp.where(earlier < later, 1.0, 0.0).astype(jnp.bfloat16)
    ranks = jnp.dot(before, taken.astype(jnp.bfloat16), preferred_element_type=jnp.float32)
    mine = ranks == order
    return jnp.where(mine, taken, 0.0), jnp.where(mine, weight, 0.0)


def normalise(stream_f, gain):
    scale = lax.rsqrt(jnp.mean(stream_f * stream_f, axis=-1, keepdims=True) + EPS)
    return (stream_f * scale * gain).astype(jnp.bfloat16)


def send_rows(pick, normed, stack_ref, slab_ref):
    piece = slab_ref.shape[1]
    for p in range(PIECES):
        rows = jnp.dot(
            pick, normed[:, p * piece : (p + 1) * piece], preferred_element_type=jnp.float32
        ).astype(jnp.bfloat16)
        stack_piece(stack_ref, rows, p)
    fold_rows(stack_ref, slab_ref)


def slot_numbers(routes_t, place_row):
    choices, tokens = routes_t.shape
    devices = place_row.shape[1]
    place = place_row.astype(jnp.float32)
    chosen = jnp.transpose(routes_t.astype(jnp.float32))
    same = [chosen[:, k : k + 1] == place for k in range(choices)]
    taken = jnp.zeros((tokens, devices), jnp.float32)
    for k in range(choices):
        taken = jnp.where(same[k], 1.0, taken)
    later = lax.broadcasted_iota(jnp.int32, (tokens, tokens), 0)
    earlier = lax.broadcasted_iota(jnp.int32, (tokens, tokens), 1)
    before = jnp.where(earlier < later, 1.0, 0.0).astype(jnp.bfloat16)
    ranks = jnp.dot(before, taken.astype(jnp.bfloat16), preferred_element_type=jnp.float32)
    home = lax.broadcasted_iota(jnp.int32, (tokens, devices), 1).astype(jnp.float32)
    number = home * CAP + ranks
    column = lax.broadcasted_iota(jnp.int32, (tokens, choices), 1)
    slots = jnp.zeros((tokens, choices), jnp.float32)
    for k in range(choices):
        found = jnp.sum(jnp.where(same[k], number, 0.0), axis=1, keepdims=True)
        slots = jnp.where(column == k, found, slots)
    return jnp.transpose(slots).astype(jnp.int32)


def mix_blocks(layer, slots_ref, gates_ref, back_ref, mixed_ref):
    for t in range(mixed_ref.shape[0]):
        total = None
        for k in range(gates_ref.shape[1]):
            block = back_ref[slots_ref[layer, k, t]].astype(jnp.float32) * gates_ref[layer, k, t]
            total = block if total is None else total + block
        mixed_ref[t] = total


def first_kernel(
    tokens_hbm, gain_hbm, routes_hbm, place_hbm, slab_ref, slots_ref,
    tokens_ref, gain_ref, routes_ref, place_ref, stack_ref, sems,
):
    loads = [
        pltpu.make_async_copy(src, dst, sems.at[i])
        for i, (src, dst) in enumerate(
            (
                (routes_hbm, routes_ref),
                (place_hbm, place_ref),
                (tokens_hbm, tokens_ref),
                (gain_hbm, gain_ref),
            )
        )
    ]
    for load in loads:
        load.start()
    loads[0].wait()
    loads[1].wait()
    select, _ = slot_tables(routes_ref[0], place_ref[0:1, :], None)
    pick = jnp.transpose(select).astype(jnp.bfloat16)
    loads[2].wait()
    loads[3].wait()
    normed = normalise(tokens_ref[...].astype(jnp.float32), gain_ref[0:1, :])
    send_rows(pick, normed, stack_ref, slab_ref)
    for layer in range(routes_ref.shape[0]):
        slots_ref[layer] = slot_numbers(routes_ref[layer], place_ref[layer : layer + 1, :])


def blocks_of(stream_ref, stack_ref):
    piece = stack_ref.shape[1]
    for p in range(PIECES):
        stack_ref[p * GROUP : (p + 1) * GROUP, :] = stream_ref[:, p * piece : (p + 1) * piece]
    return jnp.dot(fold_matrix(), stack_ref[...], preferred_element_type=jnp.float32)


def middle_kernel(
    layer, first, slots_in, gates_in, back_ref, stream_ref, gain_ref,
    slab_ref, out_ref, mixed_ref, gain_rows, stack_ref, slots_ref, gates_ref, sems,
):
    loads = [
        pltpu.make_async_copy(slots_in, slots_ref, sems.at[0]),
        pltpu.make_async_copy(gates_in, gates_ref, sems.at[1]),
    ]
    for load in loads:
        load.start()
    slab_ref[...] = jnp.zeros(slab_ref.shape, jnp.bfloat16)
    tokens, pieces, piece = mixed_ref.shape
    if first:
        blocks = blocks_of(stream_ref, stack_ref)
    else:
        blocks = stream_ref[...].astype(jnp.float32)
    for p in range(pieces):
        gain_rows[p : p + 1, :] = gain_ref[
            layer + 1 : layer + 2, p * piece : (p + 1) * piece
        ]
    for load in loads:
        load.wait()
    mix_blocks(layer, slots_ref, gates_ref, back_ref, mixed_ref)
    stream = (blocks + mixed_ref[...].reshape(tokens * pieces, piece)).astype(jnp.bfloat16)
    out_ref[...] = stream
    wide = stream.astype(jnp.float32).reshape(tokens, pieces, piece)
    total = jnp.sum(jnp.sum(wide * wide, axis=2, keepdims=True), axis=1, keepdims=True)
    scale = lax.rsqrt(total / (pieces * piece) + EPS)
    mixed_ref[...] = wide * scale * gain_rows[...][None]
    for t in range(tokens):
        row = mixed_ref[t].astype(jnp.bfloat16)
        for k in range(slots_ref.shape[1]):
            slab_ref[slots_ref[layer + 1, k, t]] = row


def last_kernel(
    layer, slab_in, stream_ref, routes_ref, gates_ref, place_ref, out_ref, rows_ref
):
    _, weight = slot_tables(routes_ref[layer], place_ref[layer : layer + 1, :], gates_ref[layer])
    tokens, piece = weight.shape[0], slab_in.shape[1]
    stream = jnp.dot(unfold_matrix(), stream_ref[...], preferred_element_type=jnp.float32)
    unfold_rows(slab_in, rows_ref)
    high = weight.astype(jnp.bfloat16)
    low = (weight - high.astype(jnp.float32)).astype(jnp.bfloat16)
    both = jnp.dot(
        jnp.concatenate([high, low], axis=0), rows_ref[...], preferred_element_type=jnp.float32
    )
    mixed = both[:tokens] + both[tokens:]
    for p in range(PIECES):
        cols = slice(p * piece, (p + 1) * piece)
        out_ref[:, cols] = (stream[p * tokens : (p + 1) * tokens] + mixed[:, cols]).astype(
            jnp.bfloat16
        )


def block_weight(w_ref, factor, layer, first, count):
    lines = []
    for i in range(w_ref.shape[2] // QBLK):
        line = [
            (
                w_ref[layer, 0, i * QBLK : (i + 1) * QBLK, j * QBLK : (j + 1) * QBLK].astype(
                    jnp.float32
                )
                * factor(i, j)
            ).astype(jnp.bfloat16)
            for j in range(first // QBLK, (first + count) // QBLK)
        ]
        lines.append(jnp.concatenate(line, axis=1))
    return jnp.concatenate(lines, axis=0)


def expert_kernel(
    layer, in_factors, out_factors, slab_in, w_in, w_out,
    slab_ref, x_ref, hid, stack_ref, in_scale, out_scale, sems,
):
    loads = [
        pltpu.make_async_copy(in_factors.at[layer : layer + 1], in_scale, sems.at[0]),
        pltpu.make_async_copy(out_factors.at[layer : layer + 1], out_scale, sems.at[1]),
    ]
    for load in loads:
        load.start()

    def into(first, count):
        return block_weight(w_in, lambda i, j: in_scale[0, j, 0, i], layer, first, count)

    def out_of(first, count):
        return block_weight(w_out, lambda i, j: out_scale[0, i, 0, j], layer, first, count)

    unfold_rows(slab_in, x_ref)
    for load in loads:
        load.wait()
    ff = w_out.shape[2]
    chunk = slab_ref.shape[1]
    for n in range(ff // chunk):
        gate = jnp.dot(x_ref[...], into(n * chunk, chunk), preferred_element_type=jnp.float32)
        up = jnp.dot(x_ref[...], into(ff + n * chunk, chunk), preferred_element_type=jnp.float32)
        hid[:, n * chunk : (n + 1) * chunk] = (gate / (1.0 + jnp.exp(-gate)) * up).astype(
            jnp.bfloat16
        )
    for m in range(PIECES):
        answer = jnp.dot(
            hid[...], out_of(m * chunk, chunk), preferred_element_type=jnp.float32
        ).astype(jnp.bfloat16)
        stack_piece(stack_ref, answer, m)
    fold_rows(stack_ref, slab_ref)


VM = pl.BlockSpec(memory_space=pltpu.VMEM)
HB = pl.BlockSpec(memory_space=pltpu.HBM)


def expert(layer, slab, weights):
    w_in, in_scale, w_out, out_scale = weights
    rows, piece = slab.shape
    slots = rows // PIECES
    width, ff = w_in.shape[2], w_out.shape[2]
    return pl.pallas_call(
        functools.partial(expert_kernel, layer),
        in_specs=[VM] * 5,
        out_specs=VM,
        out_shape=jax.ShapeDtypeStruct(slab.shape, jnp.bfloat16),
        scratch_shapes=[
            pltpu.VMEM((slots, width), jnp.bfloat16),
            pltpu.VMEM((slots, ff), jnp.bfloat16),
            pltpu.VMEM(slab.shape, jnp.bfloat16),
            pltpu.SMEM((1, *in_scale.shape[1:]), jnp.float32),
            pltpu.SMEM((1, *out_scale.shape[1:]), jnp.float32),
            pltpu.SemaphoreType.DMA((2,)),
        ],
        compiler_params=pltpu.CompilerParams(vmem_limit_bytes=20 * MIB),
        cost_estimate=pl.CostEstimate(
            flops=6 * slots * width * ff,
            bytes_accessed=6 * width * ff + 4 * slots * width,
            transcendentals=slots * ff,
        ),
        name="expert",
    )(in_scale, out_scale, slab, w_in, w_out)


def hbm(array):
    return pltpu.with_memory_space_constraint(array, pltpu.HBM)


def exchange(slab, devices):
    split = slab.reshape(devices, slab.shape[0] // devices, slab.shape[1])
    moved = lax.all_to_all(split, AXES, split_axis=0, concat_axis=0, tiled=True)
    return moved.reshape(slab.shape)


def shards(tokens, norm_gain, routes, gates, placement, w_in, in_scale, w_out, out_scale):
    count, width = tokens.shape
    layers, devices = placement.shape
    slots = devices * CAP
    piece = width // PIECES
    routes_t = jnp.swapaxes(routes, 1, 2)
    gates_t = jnp.swapaxes(gates, 1, 2)
    slab_type = jax.ShapeDtypeStruct((slots * PIECES, piece), jnp.bfloat16)
    slots_type = jax.ShapeDtypeStruct(routes_t.shape, jnp.int32)
    stream_type = jax.ShapeDtypeStruct((count, width), jnp.bfloat16)
    mixed = pltpu.VMEM((count, PIECES, piece), jnp.float32)
    stack = pltpu.VMEM((slots * PIECES, piece), jnp.bfloat16)
    params = pltpu.CompilerParams(vmem_limit_bytes=12 * MIB)

    small = (
        pltpu.VMEM((count, width), jnp.bfloat16),
        pltpu.VMEM(norm_gain.shape, jnp.float32),
        pltpu.VMEM(routes_t.shape, jnp.int32),
        pltpu.VMEM(placement.shape, jnp.int32),
    )
    slab, numbers = pl.pallas_call(
        first_kernel,
        in_specs=[HB] * 4,
        out_specs=(VM, VM),
        out_shape=(slab_type, slots_type),
        scratch_shapes=[*small, stack, pltpu.SemaphoreType.DMA((4,))],
        compiler_params=params,
        cost_estimate=pl.CostEstimate(
            flops=8 * 10**9, bytes_accessed=8 * 10**6, transcendentals=0
        ),
        name="first",
    )(*[hbm(a) for a in (tokens, norm_gain, routes_t, placement)])
    weights = (
        w_in,
        jnp.transpose(in_scale, (0, 3, 1, 2)),
        w_out,
        jnp.transpose(out_scale, (0, 2, 1, 3)),
    )
    stream = tokens
    for layer in range(layers):
        answers = expert(layer, exchange(slab, devices), weights)
        back = exchange(answers, devices)
        if layer + 1 < layers:
            slab, stream = pl.pallas_call(
                functools.partial(middle_kernel, layer, layer == 0),
                in_specs=[VM] * 5,
                out_specs=(VM, VM),
                out_shape=(
                    jax.ShapeDtypeStruct((slots, PIECES, piece), jnp.bfloat16),
                    jax.ShapeDtypeStruct((count * PIECES, piece), jnp.bfloat16),
                ),
                scratch_shapes=[
                    mixed,
                    pltpu.VMEM((PIECES, piece), jnp.float32),
                    pltpu.VMEM((count * PIECES, piece), jnp.bfloat16),
                    pltpu.SMEM(numbers.shape, jnp.int32),
                    pltpu.SMEM(gates_t.shape, jnp.float32),
                    pltpu.SemaphoreType.DMA((2,)),
                ],
                compiler_params=params,
                name="middle",
            )(numbers, gates_t, back.reshape(slots, PIECES, piece), stream, norm_gain)
            slab = slab.reshape(slots * PIECES, piece)
        else:
            stream = pl.pallas_call(
                functools.partial(last_kernel, layer),
                in_specs=[VM] * 5,
                out_specs=VM,
                out_shape=stream_type,
                scratch_shapes=[pltpu.VMEM((slots, width), jnp.bfloat16)],
                compiler_params=params,
                name="last",
            )(back, stream, routes_t, gates_t, placement)
    return stream


def solution(mesh):
    return jax.shard_map(
        shards,
        mesh=mesh,
        in_specs=(
            P(AXES, None),
            P(),
            P(None, AXES, None),
            P(None, AXES, None),
            P(),
            P(None, AXES, None, None),
            P(None, AXES, None, None),
            P(None, AXES, None, None),
            P(None, AXES, None, None),
        ),
        out_specs=P(AXES, None),
        check_vma=False,
    )
```

```python
import functools

import jax
import jax.numpy as jnp
from jax import lax
from jax.experimental import pallas as pl
from jax.experimental.pallas import tpu as pltpu
from jax.sharding import PartitionSpec as P

AXES = ("dp", "expert")
QBLK = 128
CAP = 3
PIECES = 8
GROUP = 32
EPS = 1e-06
MIB = 1 << 20


def fold_matrix():
    row = lax.broadcasted_iota(jnp.int32, (GROUP * PIECES, GROUP * PIECES), 0)
    col = lax.broadcasted_iota(jnp.int32, (GROUP * PIECES, GROUP * PIECES), 1)
    return jnp.where(col == (row & (PIECES - 1)) * GROUP + (row >> 3), 1.0, 0.0).astype(jnp.bfloat16)


def unfold_matrix():
    row = lax.broadcasted_iota(jnp.int32, (GROUP * PIECES, GROUP * PIECES), 0)
    col = lax.broadcasted_iota(jnp.int32, (GROUP * PIECES, GROUP * PIECES), 1)
    return jnp.where(col == (row & (GROUP - 1)) * PIECES + (row >> 5), 1.0, 0.0).astype(jnp.bfloat16)


def unfold_rows(slab_ref, rows_ref):
    piece = slab_ref.shape[1]
    span = GROUP * PIECES
    unfold = unfold_matrix()
    for b in range(slab_ref.shape[0] // span):
        block = jnp.dot(
            unfold, slab_ref[b * span : (b + 1) * span, :], preferred_element_type=jnp.float32
        ).astype(jnp.bfloat16)
        for p in range(PIECES):
            rows_ref[b * GROUP : (b + 1) * GROUP, p * piece : (p + 1) * piece] = block[
                p * GROUP : (p + 1) * GROUP
            ]


def fold_rows(stack_ref, slab_ref):
    span = GROUP * PIECES
    fold = fold_matrix()
    for b in range(slab_ref.shape[0] // span):
        slab_ref[b * span : (b + 1) * span, :] = jnp.dot(
            fold, stack_ref[b * span : (b + 1) * span, :], preferred_element_type=jnp.float32
        ).astype(jnp.bfloat16)


def stack_piece(stack_ref, values, p):
    span = GROUP * PIECES
    for b in range(values.shape[0] // GROUP):
        stack_ref[b * span + p * GROUP : b * span + (p + 1) * GROUP, :] = values[
            b * GROUP : (b + 1) * GROUP
        ]


def slot_tables(routes_t, place_row, gates_t):
    tokens = routes_t.shape[1]
    devices = place_row.shape[1]
    slots = devices * CAP
    home = lax.broadcasted_iota(jnp.int32, (devices, slots), 0)
    slot = lax.broadcasted_iota(jnp.int32, (devices, slots), 1)
    low = home * CAP
    widen = jnp.where((slot >= low) & (slot < low + CAP), 1.0, 0.0).astype(jnp.bfloat16)
    place = jnp.dot(
        jnp.broadcast_to(place_row.astype(jnp.float32), (8, devices)).astype(jnp.bfloat16),
        widen,
        preferred_element_type=jnp.float32,
    )[:1]
    rank_of = jnp.dot(
        jnp.broadcast_to(
            lax.broadcasted_iota(jnp.int32, (1, devices), 1).astype(jnp.float32), (8, devices)
        ).astype(jnp.bfloat16),
        widen,
        preferred_element_type=jnp.float32,
    )[:1]
    order = lax.broadcasted_iota(jnp.int32, (1, slots), 1).astype(jnp.float32) - rank_of * CAP
    chosen = jnp.transpose(routes_t.astype(jnp.float32))
    gate = None if gates_t is None else jnp.transpose(gates_t)
    taken = jnp.zeros((tokens, slots), jnp.float32)
    weight = jnp.zeros((tokens, slots), jnp.float32)
    for k in range(chosen.shape[1]):
        same = chosen[:, k : k + 1] == place
        taken = jnp.where(same, 1.0, taken)
        if gate is not None:
            weight = jnp.where(same, gate[:, k : k + 1], weight)
    later = lax.broadcasted_iota(jnp.int32, (tokens, tokens), 0)
    earlier = lax.broadcasted_iota(jnp.int32, (tokens, tokens), 1)
    before = jnp.where(earlier < later, 1.0, 0.0).astype(jnp.bfloat16)
    ranks = jnp.dot(before, taken.astype(jnp.bfloat16), preferred_element_type=jnp.float32)
    mine = ranks == order
    return jnp.where(mine, taken, 0.0), jnp.where(mine, weight, 0.0)


def normalise(stream_f, gain):
    scale = lax.rsqrt(jnp.mean(stream_f * stream_f, axis=-1, keepdims=True) + EPS)
    return (stream_f * scale * gain).astype(jnp.bfloat16)


def send_rows(pick, normed, stack_ref, slab_ref):
    piece = slab_ref.shape[1]
    for p in range(PIECES):
        rows = jnp.dot(
            pick, normed[:, p * piece : (p + 1) * piece], preferred_element_type=jnp.float32
        ).astype(jnp.bfloat16)
        stack_piece(stack_ref, rows, p)
    fold_rows(stack_ref, slab_ref)


def slot_numbers(routes_t, place_row):
    choices, tokens = routes_t.shape
    devices = place_row.shape[1]
    place = place_row.astype(jnp.float32)
    chosen = jnp.transpose(routes_t.astype(jnp.float32))
    same = [chosen[:, k : k + 1] == place for k in range(choices)]
    taken = jnp.zeros((tokens, devices), jnp.float32)
    for k in range(choices):
        taken = jnp.where(same[k], 1.0, taken)
    later = lax.broadcasted_iota(jnp.int32, (tokens, tokens), 0)
    earlier = lax.broadcasted_iota(jnp.int32, (tokens, tokens), 1)
    before = jnp.where(earlier < later, 1.0, 0.0).astype(jnp.bfloat16)
    ranks = jnp.dot(before, taken.astype(jnp.bfloat16), preferred_element_type=jnp.float32)
    home = lax.broadcasted_iota(jnp.int32, (tokens, devices), 1).astype(jnp.float32)
    number = home * CAP + ranks
    column = lax.broadcasted_iota(jnp.int32, (tokens, choices), 1)
    slots = jnp.zeros((tokens, choices), jnp.float32)
    for k in range(choices):
        found = jnp.sum(jnp.where(same[k], number, 0.0), axis=1, keepdims=True)
        slots = jnp.where(column == k, found, slots)
    return jnp.transpose(slots).astype(jnp.int32)


def mix_blocks(slots_ref, gates_ref, back_ref, mixed_ref):
    for t in range(mixed_ref.shape[0]):
        total = None
        for k in range(gates_ref.shape[1]):
            block = back_ref[slots_ref[0, k, t]].astype(jnp.float32) * gates_ref[0, k, t]
            total = block if total is None else total + block
        mixed_ref[t] = total


def first_kernel(
    tokens_hbm, gain_hbm, routes_hbm, place_hbm, slab_ref, slots_ref,
    tokens_ref, gain_ref, routes_ref, place_ref, stack_ref, sems,
):
    loads = [
        pltpu.make_async_copy(src, dst, sems.at[i])
        for i, (src, dst) in enumerate(
            (
                (routes_hbm, routes_ref),
                (place_hbm, place_ref),
                (tokens_hbm, tokens_ref),
                (gain_hbm, gain_ref),
            )
        )
    ]
    for load in loads:
        load.start()
    loads[0].wait()
    loads[1].wait()
    select, _ = slot_tables(routes_ref[0], place_ref[0:1, :], None)
    pick = jnp.transpose(select).astype(jnp.bfloat16)
    loads[2].wait()
    loads[3].wait()
    normed = normalise(tokens_ref[...].astype(jnp.float32), gain_ref[0:1, :])
    send_rows(pick, normed, stack_ref, slab_ref)
    for layer in range(routes_ref.shape[0]):
        slots_ref[layer] = slot_numbers(routes_ref[layer], place_ref[layer : layer + 1, :])


def blocks_of(stream_ref, stack_ref):
    piece = stack_ref.shape[1]
    for p in range(PIECES):
        stack_ref[p * GROUP : (p + 1) * GROUP, :] = stream_ref[:, p * piece : (p + 1) * piece]
    return jnp.dot(fold_matrix(), stack_ref[...], preferred_element_type=jnp.float32)


def middle_kernel(
    layer, first, slots_in, gates_in, back_ref, stream_ref, gain_ref,
    slab_ref, out_ref, mixed_ref, gain_rows, stack_ref, slots_ref, gates_ref, sems,
):
    loads = [
        pltpu.make_async_copy(
            slots_in.at[layer : layer + 1], slots_ref.at[0:1], sems.at[0]
        ),
        pltpu.make_async_copy(gates_in.at[layer : layer + 1], gates_ref, sems.at[1]),
        pltpu.make_async_copy(
            slots_in.at[layer + 1 : layer + 2], slots_ref.at[1:2], sems.at[2]
        ),
    ]
    for load in loads:
        load.start()
    slab_ref[...] = jnp.zeros(slab_ref.shape, jnp.bfloat16)
    tokens, pieces, piece = mixed_ref.shape
    if first:
        blocks = blocks_of(stream_ref, stack_ref)
    else:
        blocks = stream_ref[...].astype(jnp.float32)
    for p in range(pieces):
        gain_rows[p : p + 1, :] = gain_ref[
            layer + 1 : layer + 2, p * piece : (p + 1) * piece
        ]
    loads[0].wait()
    loads[1].wait()
    mix_blocks(slots_ref, gates_ref, back_ref, mixed_ref)
    stream = (blocks + mixed_ref[...].reshape(tokens * pieces, piece)).astype(jnp.bfloat16)
    out_ref[...] = stream
    wide = stream.astype(jnp.float32).reshape(tokens, pieces, piece)
    total = jnp.sum(jnp.sum(wide * wide, axis=2, keepdims=True), axis=1, keepdims=True)
    scale = lax.rsqrt(total / (pieces * piece) + EPS)
    mixed_ref[...] = wide * scale * gain_rows[...][None]
    loads[2].wait()
    for t in range(tokens):
        row = mixed_ref[t].astype(jnp.bfloat16)
        for k in range(slots_ref.shape[1]):
            slab_ref[slots_ref[1, k, t]] = row


def last_kernel(
    layer, slab_in, blocks_ref, routes_ref, gates_ref, place_ref, out_ref, rows_ref, stream_ref
):
    _, weight = slot_tables(routes_ref[layer], place_ref[layer : layer + 1, :], gates_ref[layer])
    unfold_rows(blocks_ref, stream_ref)
    unfold_rows(slab_in, rows_ref)
    high = weight.astype(jnp.bfloat16)
    low = (weight - high.astype(jnp.float32)).astype(jnp.bfloat16)
    both = jnp.dot(
        jnp.concatenate([high, low], axis=0), rows_ref[...], preferred_element_type=jnp.float32
    )
    tokens = weight.shape[0]
    mixed = both[:tokens] + both[tokens:]
    out_ref[...] = (stream_ref[...].astype(jnp.float32) + mixed).astype(jnp.bfloat16)


def block_weight(w_ref, factor, layer, first, count):
    lines = []
    for i in range(w_ref.shape[2] // QBLK):
        line = [
            (
                w_ref[layer, 0, i * QBLK : (i + 1) * QBLK, j * QBLK : (j + 1) * QBLK].astype(
                    jnp.float32
                )
                * factor(i, j)
            ).astype(jnp.bfloat16)
            for j in range(first // QBLK, (first + count) // QBLK)
        ]
        lines.append(jnp.concatenate(line, axis=1))
    return jnp.concatenate(lines, axis=0)


def expert_kernel(
    layer, in_factors, out_factors, slab_in, w_in, w_out,
    slab_ref, x_ref, hid, stack_ref, in_scale, out_scale, sems,
):
    loads = [
        pltpu.make_async_copy(in_factors.at[layer : layer + 1], in_scale, sems.at[0]),
        pltpu.make_async_copy(out_factors.at[layer : layer + 1], out_scale, sems.at[1]),
    ]
    for load in loads:
        load.start()

    def into(first, count):
        return block_weight(w_in, lambda i, j: in_scale[0, j, 0, i], layer, first, count)

    def out_of(first, count):
        return block_weight(w_out, lambda i, j: out_scale[0, i, 0, j], layer, first, count)

    unfold_rows(slab_in, x_ref)
    for load in loads:
        load.wait()
    ff = w_out.shape[2]
    chunk = slab_ref.shape[1]
    for n in range(ff // chunk):
        gate = jnp.dot(x_ref[...], into(n * chunk, chunk), preferred_element_type=jnp.float32)
        up = jnp.dot(x_ref[...], into(ff + n * chunk, chunk), preferred_element_type=jnp.float32)
        hid[:, n * chunk : (n + 1) * chunk] = (gate / (1.0 + jnp.exp(-gate)) * up).astype(
            jnp.bfloat16
        )
    for m in range(PIECES):
        answer = jnp.dot(
            hid[...], out_of(m * chunk, chunk), preferred_element_type=jnp.float32
        ).astype(jnp.bfloat16)
        stack_piece(stack_ref, answer, m)
    fold_rows(stack_ref, slab_ref)


VM = pl.BlockSpec(memory_space=pltpu.VMEM)
HB = pl.BlockSpec(memory_space=pltpu.HBM)


def expert(layer, slab, weights):
    w_in, in_scale, w_out, out_scale = weights
    rows, piece = slab.shape
    slots = rows // PIECES
    width, ff = w_in.shape[2], w_out.shape[2]
    return pl.pallas_call(
        functools.partial(expert_kernel, layer),
        in_specs=[VM] * 5,
        out_specs=VM,
        out_shape=jax.ShapeDtypeStruct(slab.shape, jnp.bfloat16),
        scratch_shapes=[
            pltpu.VMEM((slots, width), jnp.bfloat16),
            pltpu.VMEM((slots, ff), jnp.bfloat16),
            pltpu.VMEM(slab.shape, jnp.bfloat16),
            pltpu.SMEM((1, *in_scale.shape[1:]), jnp.float32),
            pltpu.SMEM((1, *out_scale.shape[1:]), jnp.float32),
            pltpu.SemaphoreType.DMA((2,)),
        ],
        compiler_params=pltpu.CompilerParams(vmem_limit_bytes=20 * MIB),
        cost_estimate=pl.CostEstimate(
            flops=6 * slots * width * ff,
            bytes_accessed=6 * width * ff + 4 * slots * width,
            transcendentals=slots * ff,
        ),
        name="expert",
    )(in_scale, out_scale, slab, w_in, w_out)


def hbm(array):
    return pltpu.with_memory_space_constraint(array, pltpu.HBM)


def exchange(slab, devices):
    split = slab.reshape(devices, slab.shape[0] // devices, slab.shape[1])
    moved = lax.all_to_all(split, AXES, split_axis=0, concat_axis=0, tiled=True)
    return moved.reshape(slab.shape)


def shards(tokens, norm_gain, routes, gates, placement, w_in, in_scale, w_out, out_scale):
    count, width = tokens.shape
    layers, devices = placement.shape
    slots = devices * CAP
    piece = width // PIECES
    routes_t = jnp.swapaxes(routes, 1, 2)
    gates_t = jnp.swapaxes(gates, 1, 2)
    slab_type = jax.ShapeDtypeStruct((slots * PIECES, piece), jnp.bfloat16)
    slots_type = jax.ShapeDtypeStruct(routes_t.shape, jnp.int32)
    stream_type = jax.ShapeDtypeStruct((count, width), jnp.bfloat16)
    mixed = pltpu.VMEM((count, PIECES, piece), jnp.float32)
    stack = pltpu.VMEM((slots * PIECES, piece), jnp.bfloat16)
    params = pltpu.CompilerParams(vmem_limit_bytes=12 * MIB)

    small = (
        pltpu.VMEM((count, width), jnp.bfloat16),
        pltpu.VMEM(norm_gain.shape, jnp.float32),
        pltpu.VMEM(routes_t.shape, jnp.int32),
        pltpu.VMEM(placement.shape, jnp.int32),
    )
    slab, numbers = pl.pallas_call(
        first_kernel,
        in_specs=[HB] * 4,
        out_specs=(VM, VM),
        out_shape=(slab_type, slots_type),
        scratch_shapes=[*small, stack, pltpu.SemaphoreType.DMA((4,))],
        compiler_params=params,
        cost_estimate=pl.CostEstimate(
            flops=8 * 10**9, bytes_accessed=8 * 10**6, transcendentals=0
        ),
        name="first",
    )(*[hbm(a) for a in (tokens, norm_gain, routes_t, placement)])
    weights = (
        w_in,
        jnp.transpose(in_scale, (0, 3, 1, 2)),
        w_out,
        jnp.transpose(out_scale, (0, 2, 1, 3)),
    )
    stream = tokens
    for layer in range(layers):
        answers = expert(layer, exchange(slab, devices), weights)
        back = exchange(answers, devices)
        if layer + 1 < layers:
            slab, stream = pl.pallas_call(
                functools.partial(middle_kernel, layer, layer == 0),
                in_specs=[VM] * 5,
                out_specs=(VM, VM),
                out_shape=(
                    jax.ShapeDtypeStruct((slots, PIECES, piece), jnp.bfloat16),
                    jax.ShapeDtypeStruct((count * PIECES, piece), jnp.bfloat16),
                ),
                scratch_shapes=[
                    mixed,
                    pltpu.VMEM((PIECES, piece), jnp.float32),
                    pltpu.VMEM((count * PIECES, piece), jnp.bfloat16),
                    pltpu.SMEM((2, *numbers.shape[1:]), jnp.int32),
                    pltpu.SMEM((1, *gates_t.shape[1:]), jnp.float32),
                    pltpu.SemaphoreType.DMA((3,)),
                ],
                compiler_params=params,
                name="middle",
            )(numbers, gates_t, back.reshape(slots, PIECES, piece), stream, norm_gain)
            slab = slab.reshape(slots * PIECES, piece)
        else:
            stream = pl.pallas_call(
                functools.partial(last_kernel, layer),
                in_specs=[VM] * 5,
                out_specs=VM,
                out_shape=stream_type,
                scratch_shapes=[
                    pltpu.VMEM((slots, width), jnp.bfloat16),
                    pltpu.VMEM((count, width), jnp.bfloat16),
                ],
                compiler_params=params,
                name="last",
            )(back, stream, routes_t, gates_t, placement)
    return stream


def solution(mesh):
    return jax.shard_map(
        shards,
        mesh=mesh,
        in_specs=(
            P(AXES, None),
            P(),
            P(None, AXES, None),
            P(None, AXES, None),
            P(),
            P(None, AXES, None, None),
            P(None, AXES, None, None),
            P(None, AXES, None, None),
            P(None, AXES, None, None),
        ),
        out_specs=P(AXES, None),
        check_vma=False,
    )
```

```python
import functools

import jax
import jax.numpy as jnp
from jax import lax
from jax.experimental import pallas as pl
from jax.experimental.pallas import tpu as pltpu
from jax.sharding import PartitionSpec as P

AXES = ("dp", "expert")
QBLK = 128
CAP = 3
PIECES = 8
GROUP = 32
EPS = 1e-06
MIB = 1 << 20


def fold_matrix():
    row = lax.broadcasted_iota(jnp.int32, (GROUP * PIECES, GROUP * PIECES), 0)
    col = lax.broadcasted_iota(jnp.int32, (GROUP * PIECES, GROUP * PIECES), 1)
    return jnp.where(col == (row & (PIECES - 1)) * GROUP + (row >> 3), 1.0, 0.0).astype(jnp.bfloat16)


def unfold_matrix():
    row = lax.broadcasted_iota(jnp.int32, (GROUP * PIECES, GROUP * PIECES), 0)
    col = lax.broadcasted_iota(jnp.int32, (GROUP * PIECES, GROUP * PIECES), 1)
    return jnp.where(col == (row & (GROUP - 1)) * PIECES + (row >> 5), 1.0, 0.0).astype(jnp.bfloat16)


def unfold_rows(slab_ref, rows_ref):
    piece = slab_ref.shape[1]
    span = GROUP * PIECES
    unfold = unfold_matrix()
    for b in range(slab_ref.shape[0] // span):
        block = jnp.dot(
            unfold, slab_ref[b * span : (b + 1) * span, :], preferred_element_type=jnp.float32
        ).astype(jnp.bfloat16)
        for p in range(PIECES):
            rows_ref[b * GROUP : (b + 1) * GROUP, p * piece : (p + 1) * piece] = block[
                p * GROUP : (p + 1) * GROUP
            ]


def fold_rows(stack_ref, slab_ref):
    span = GROUP * PIECES
    fold = fold_matrix()
    for b in range(slab_ref.shape[0] // span):
        slab_ref[b * span : (b + 1) * span, :] = jnp.dot(
            fold, stack_ref[b * span : (b + 1) * span, :], preferred_element_type=jnp.float32
        ).astype(jnp.bfloat16)


def stack_piece(stack_ref, values, p):
    span = GROUP * PIECES
    for b in range(values.shape[0] // GROUP):
        stack_ref[b * span + p * GROUP : b * span + (p + 1) * GROUP, :] = values[
            b * GROUP : (b + 1) * GROUP
        ]


def slot_tables(routes_t, place_row, gates_t):
    tokens = routes_t.shape[1]
    devices = place_row.shape[1]
    slots = devices * CAP
    home = lax.broadcasted_iota(jnp.int32, (devices, slots), 0)
    slot = lax.broadcasted_iota(jnp.int32, (devices, slots), 1)
    low = home * CAP
    widen = jnp.where((slot >= low) & (slot < low + CAP), 1.0, 0.0).astype(jnp.bfloat16)
    place = jnp.dot(
        jnp.broadcast_to(place_row.astype(jnp.float32), (8, devices)).astype(jnp.bfloat16),
        widen,
        preferred_element_type=jnp.float32,
    )[:1]
    rank_of = jnp.dot(
        jnp.broadcast_to(
            lax.broadcasted_iota(jnp.int32, (1, devices), 1).astype(jnp.float32), (8, devices)
        ).astype(jnp.bfloat16),
        widen,
        preferred_element_type=jnp.float32,
    )[:1]
    order = lax.broadcasted_iota(jnp.int32, (1, slots), 1).astype(jnp.float32) - rank_of * CAP
    chosen = jnp.transpose(routes_t.astype(jnp.float32))
    gate = None if gates_t is None else jnp.transpose(gates_t)
    taken = jnp.zeros((tokens, slots), jnp.float32)
    weight = jnp.zeros((tokens, slots), jnp.float32)
    for k in range(chosen.shape[1]):
        same = chosen[:, k : k + 1] == place
        taken = jnp.where(same, 1.0, taken)
        if gate is not None:
            weight = jnp.where(same, gate[:, k : k + 1], weight)
    later = lax.broadcasted_iota(jnp.int32, (tokens, tokens), 0)
    earlier = lax.broadcasted_iota(jnp.int32, (tokens, tokens), 1)
    before = jnp.where(earlier < later, 1.0, 0.0).astype(jnp.bfloat16)
    ranks = jnp.dot(before, taken.astype(jnp.bfloat16), preferred_element_type=jnp.float32)
    mine = ranks == order
    return jnp.where(mine, taken, 0.0), jnp.where(mine, weight, 0.0)


def normalise(stream_f, gain):
    scale = lax.rsqrt(jnp.mean(stream_f * stream_f, axis=-1, keepdims=True) + EPS)
    return (stream_f * scale * gain).astype(jnp.bfloat16)


def send_rows(pick, normed, stack_ref, slab_ref):
    piece = slab_ref.shape[1]
    for p in range(PIECES):
        rows = jnp.dot(
            pick, normed[:, p * piece : (p + 1) * piece], preferred_element_type=jnp.float32
        ).astype(jnp.bfloat16)
        stack_piece(stack_ref, rows, p)
    fold_rows(stack_ref, slab_ref)


def slot_numbers(routes_t, place_row):
    choices, tokens = routes_t.shape
    devices = place_row.shape[1]
    place = place_row.astype(jnp.float32)
    chosen = jnp.transpose(routes_t.astype(jnp.float32))
    same = [chosen[:, k : k + 1] == place for k in range(choices)]
    taken = jnp.zeros((tokens, devices), jnp.float32)
    for k in range(choices):
        taken = jnp.where(same[k], 1.0, taken)
    later = lax.broadcasted_iota(jnp.int32, (tokens, tokens), 0)
    earlier = lax.broadcasted_iota(jnp.int32, (tokens, tokens), 1)
    before = jnp.where(earlier < later, 1.0, 0.0).astype(jnp.bfloat16)
    ranks = jnp.dot(before, taken.astype(jnp.bfloat16), preferred_element_type=jnp.float32)
    home = lax.broadcasted_iota(jnp.int32, (tokens, devices), 1).astype(jnp.float32)
    number = home * CAP + ranks
    column = lax.broadcasted_iota(jnp.int32, (tokens, choices), 1)
    slots = jnp.zeros((tokens, choices), jnp.float32)
    for k in range(choices):
        found = jnp.sum(jnp.where(same[k], number, 0.0), axis=1, keepdims=True)
        slots = jnp.where(column == k, found, slots)
    return jnp.transpose(slots).astype(jnp.int32)


def mix_blocks(slots_ref, gates_ref, back_ref, mixed_ref):
    for t in range(mixed_ref.shape[0]):
        total = None
        for k in range(gates_ref.shape[1]):
            block = back_ref[slots_ref[0, k, t]].astype(jnp.float32) * gates_ref[0, k, t]
            total = block if total is None else total + block
        mixed_ref[t] = total


def first_kernel(
    tokens_hbm, gain_hbm, routes_hbm, place_hbm, slab_ref, slots_ref,
    tokens_ref, gain_ref, routes_ref, place_ref, stack_ref, sems,
):
    loads = [
        pltpu.make_async_copy(src, dst, sems.at[i])
        for i, (src, dst) in enumerate(
            (
                (routes_hbm, routes_ref),
                (place_hbm, place_ref),
                (tokens_hbm, tokens_ref),
                (gain_hbm, gain_ref),
            )
        )
    ]
    for load in loads:
        load.start()
    loads[0].wait()
    loads[1].wait()
    select, _ = slot_tables(routes_ref[0], place_ref[0:1, :], None)
    pick = jnp.transpose(select).astype(jnp.bfloat16)
    slots_ref[0] = slot_numbers(routes_ref[0], place_ref[0:1, :])
    loads[2].wait()
    loads[3].wait()
    normed = normalise(tokens_ref[...].astype(jnp.float32), gain_ref[0:1, :])
    send_rows(pick, normed, stack_ref, slab_ref)


def blocks_of(stream_ref, stack_ref):
    piece = stack_ref.shape[1]
    for p in range(PIECES):
        stack_ref[p * GROUP : (p + 1) * GROUP, :] = stream_ref[:, p * piece : (p + 1) * piece]
    return jnp.dot(fold_matrix(), stack_ref[...], preferred_element_type=jnp.float32)


def middle_kernel(
    layer, first, slots_in, gates_in, back_ref, stream_ref, gain_ref, routes_ref, place_ref,
    slab_ref, out_ref, next_ref, mixed_ref, gain_rows, stack_ref, numbers_ref,
    slots_ref, gates_ref, sems,
):
    loads = [
        pltpu.make_async_copy(slots_in, slots_ref.at[0:1], sems.at[0]),
        pltpu.make_async_copy(gates_in.at[layer : layer + 1], gates_ref, sems.at[1]),
        pltpu.make_async_copy(numbers_ref, slots_ref.at[1:2], sems.at[2]),
    ]
    loads[0].start()
    loads[1].start()
    later = slice(layer + 1, layer + 2)
    numbers_ref[0] = slot_numbers(routes_ref[layer + 1], place_ref[later, :])
    loads[2].start()
    _, weight = slot_tables(routes_ref[layer + 1], place_ref[later, :], gates_in[layer + 1])
    high = weight.astype(jnp.bfloat16)
    low = (weight - high.astype(jnp.float32)).astype(jnp.bfloat16)
    next_ref[...] = jnp.concatenate([high, low], axis=0)
    slab_ref[...] = jnp.zeros(slab_ref.shape, jnp.bfloat16)
    tokens, pieces, piece = mixed_ref.shape
    if first:
        blocks = blocks_of(stream_ref, stack_ref)
    else:
        blocks = stream_ref[...].astype(jnp.float32)
    for p in range(pieces):
        gain_rows[p : p + 1, :] = gain_ref[
            layer + 1 : layer + 2, p * piece : (p + 1) * piece
        ]
    loads[0].wait()
    loads[1].wait()
    mix_blocks(slots_ref, gates_ref, back_ref, mixed_ref)
    stream = (blocks + mixed_ref[...].reshape(tokens * pieces, piece)).astype(jnp.bfloat16)
    out_ref[...] = stream
    wide = stream.astype(jnp.float32).reshape(tokens, pieces, piece)
    total = jnp.sum(jnp.sum(wide * wide, axis=2, keepdims=True), axis=1, keepdims=True)
    scale = lax.rsqrt(total / (pieces * piece) + EPS)
    mixed_ref[...] = wide * scale * gain_rows[...][None]
    loads[2].wait()
    for t in range(tokens):
        row = mixed_ref[t].astype(jnp.bfloat16)
        for k in range(slots_ref.shape[1]):
            slab_ref[slots_ref[1, k, t]] = row


def last_kernel(slab_in, blocks_ref, weight_ref, out_ref, rows_ref, stream_ref):
    unfold_rows(blocks_ref, stream_ref)
    unfold_rows(slab_in, rows_ref)
    both = jnp.dot(weight_ref[...], rows_ref[...], preferred_element_type=jnp.float32)
    tokens = weight_ref.shape[0] // 2
    mixed = both[:tokens] + both[tokens:]
    out_ref[...] = (stream_ref[...].astype(jnp.float32) + mixed).astype(jnp.bfloat16)


def block_weight(w_ref, factor, layer, first, count):
    lines = []
    for i in range(w_ref.shape[2] // QBLK):
        line = [
            (
                w_ref[layer, 0, i * QBLK : (i + 1) * QBLK, j * QBLK : (j + 1) * QBLK].astype(
                    jnp.float32
                )
                * factor(i, j)
            ).astype(jnp.bfloat16)
            for j in range(first // QBLK, (first + count) // QBLK)
        ]
        lines.append(jnp.concatenate(line, axis=1))
    return jnp.concatenate(lines, axis=0)


def expert_kernel(
    layer, in_factors, out_factors, slab_in, w_in, w_out,
    slab_ref, x_ref, hid, stack_ref, in_scale, out_scale, sems,
):
    loads = [
        pltpu.make_async_copy(in_factors.at[layer : layer + 1], in_scale, sems.at[0]),
        pltpu.make_async_copy(out_factors.at[layer : layer + 1], out_scale, sems.at[1]),
    ]
    for load in loads:
        load.start()

    def into(first, count):
        return block_weight(w_in, lambda i, j: in_scale[0, j, 0, i], layer, first, count)

    def out_of(first, count):
        return block_weight(w_out, lambda i, j: out_scale[0, i, 0, j], layer, first, count)

    unfold_rows(slab_in, x_ref)
    for load in loads:
        load.wait()
    ff = w_out.shape[2]
    chunk = slab_ref.shape[1]
    for n in range(ff // chunk):
        gate = jnp.dot(x_ref[...], into(n * chunk, chunk), preferred_element_type=jnp.float32)
        up = jnp.dot(x_ref[...], into(ff + n * chunk, chunk), preferred_element_type=jnp.float32)
        hid[:, n * chunk : (n + 1) * chunk] = (gate / (1.0 + jnp.exp(-gate)) * up).astype(
            jnp.bfloat16
        )
    for m in range(PIECES):
        answer = jnp.dot(
            hid[...], out_of(m * chunk, chunk), preferred_element_type=jnp.float32
        ).astype(jnp.bfloat16)
        stack_piece(stack_ref, answer, m)
    fold_rows(stack_ref, slab_ref)


VM = pl.BlockSpec(memory_space=pltpu.VMEM)
HB = pl.BlockSpec(memory_space=pltpu.HBM)


def expert(layer, slab, weights):
    w_in, in_scale, w_out, out_scale = weights
    rows, piece = slab.shape
    slots = rows // PIECES
    width, ff = w_in.shape[2], w_out.shape[2]
    return pl.pallas_call(
        functools.partial(expert_kernel, layer),
        in_specs=[VM] * 5,
        out_specs=VM,
        out_shape=jax.ShapeDtypeStruct(slab.shape, jnp.bfloat16),
        scratch_shapes=[
            pltpu.VMEM((slots, width), jnp.bfloat16),
            pltpu.VMEM((slots, ff), jnp.bfloat16),
            pltpu.VMEM(slab.shape, jnp.bfloat16),
            pltpu.SMEM((1, *in_scale.shape[1:]), jnp.float32),
            pltpu.SMEM((1, *out_scale.shape[1:]), jnp.float32),
            pltpu.SemaphoreType.DMA((2,)),
        ],
        compiler_params=pltpu.CompilerParams(vmem_limit_bytes=20 * MIB),
        cost_estimate=pl.CostEstimate(
            flops=6 * slots * width * ff,
            bytes_accessed=6 * width * ff + 4 * slots * width,
            transcendentals=slots * ff,
        ),
        name="expert",
    )(in_scale, out_scale, slab, w_in, w_out)


def hbm(array):
    return pltpu.with_memory_space_constraint(array, pltpu.HBM)


def exchange(slab, devices):
    split = slab.reshape(devices, slab.shape[0] // devices, slab.shape[1])
    moved = lax.all_to_all(split, AXES, split_axis=0, concat_axis=0, tiled=True)
    return moved.reshape(slab.shape)


def shards(tokens, norm_gain, routes, gates, placement, w_in, in_scale, w_out, out_scale):
    count, width = tokens.shape
    layers, devices = placement.shape
    slots = devices * CAP
    piece = width // PIECES
    routes_t = jnp.swapaxes(routes, 1, 2)
    gates_t = jnp.swapaxes(gates, 1, 2)
    slab_type = jax.ShapeDtypeStruct((slots * PIECES, piece), jnp.bfloat16)
    slots_type = jax.ShapeDtypeStruct((1, *routes_t.shape[1:]), jnp.int32)
    stream_type = jax.ShapeDtypeStruct((count, width), jnp.bfloat16)
    mixed = pltpu.VMEM((count, PIECES, piece), jnp.float32)
    stack = pltpu.VMEM((slots * PIECES, piece), jnp.bfloat16)
    params = pltpu.CompilerParams(vmem_limit_bytes=12 * MIB)

    small = (
        pltpu.VMEM((count, width), jnp.bfloat16),
        pltpu.VMEM(norm_gain.shape, jnp.float32),
        pltpu.VMEM(routes_t.shape, jnp.int32),
        pltpu.VMEM(placement.shape, jnp.int32),
    )
    slab, numbers = pl.pallas_call(
        first_kernel,
        in_specs=[HB] * 4,
        out_specs=(VM, VM),
        out_shape=(slab_type, slots_type),
        scratch_shapes=[*small, stack, pltpu.SemaphoreType.DMA((4,))],
        compiler_params=params,
        cost_estimate=pl.CostEstimate(
            flops=8 * 10**9, bytes_accessed=8 * 10**6, transcendentals=0
        ),
        name="first",
    )(*[hbm(a) for a in (tokens, norm_gain, routes_t, placement)])
    weights = (
        w_in,
        jnp.transpose(in_scale, (0, 3, 1, 2)),
        w_out,
        jnp.transpose(out_scale, (0, 2, 1, 3)),
    )
    stream = tokens
    for layer in range(layers):
        answers = expert(layer, exchange(slab, devices), weights)
        back = exchange(answers, devices)
        if layer + 1 < layers:
            slab, stream, weight = pl.pallas_call(
                functools.partial(middle_kernel, layer, layer == 0),
                in_specs=[VM] * 7,
                out_specs=(VM, VM, VM),
                out_shape=(
                    jax.ShapeDtypeStruct((slots, PIECES, piece), jnp.bfloat16),
                    jax.ShapeDtypeStruct((count * PIECES, piece), jnp.bfloat16),
                    jax.ShapeDtypeStruct((2 * count, slots), jnp.bfloat16),
                ),
                scratch_shapes=[
                    mixed,
                    pltpu.VMEM((PIECES, piece), jnp.float32),
                    pltpu.VMEM((count * PIECES, piece), jnp.bfloat16),
                    pltpu.VMEM(numbers.shape, jnp.int32),
                    pltpu.SMEM((2, *numbers.shape[1:]), jnp.int32),
                    pltpu.SMEM((1, *gates_t.shape[1:]), jnp.float32),
                    pltpu.SemaphoreType.DMA((3,)),
                ],
                compiler_params=params,
                name="middle",
            )(
                numbers, gates_t, back.reshape(slots, PIECES, piece), stream, norm_gain,
                routes_t, placement,
            )
            slab = slab.reshape(slots * PIECES, piece)
        else:
            stream = pl.pallas_call(
                last_kernel,
                in_specs=[VM] * 3,
                out_specs=VM,
                out_shape=stream_type,
                scratch_shapes=[
                    pltpu.VMEM((slots, width), jnp.bfloat16),
                    pltpu.VMEM((count, width), jnp.bfloat16),
                ],
                compiler_params=params,
                name="last",
            )(back, stream, weight)
    return stream


def solution(mesh):
    return jax.shard_map(
        shards,
        mesh=mesh,
        in_specs=(
            P(AXES, None),
            P(),
            P(None, AXES, None),
            P(None, AXES, None),
            P(),
            P(None, AXES, None, None),
            P(None, AXES, None, None),
            P(None, AXES, None, None),
            P(None, AXES, None, None),
        ),
        out_specs=P(AXES, None),
        check_vma=False,
    )
```

```python
import functools

import jax
import jax.numpy as jnp
from jax import lax
from jax.experimental import pallas as pl
from jax.experimental.pallas import tpu as pltpu
from jax.sharding import PartitionSpec as P

AXES = ("dp", "expert")
QBLK = 128
CAP = 3
PIECES = 8
GROUP = 32
EPS = 1e-06
MIB = 1 << 20


def fold_matrix():
    row = lax.broadcasted_iota(jnp.int32, (GROUP * PIECES, GROUP * PIECES), 0)
    col = lax.broadcasted_iota(jnp.int32, (GROUP * PIECES, GROUP * PIECES), 1)
    return jnp.where(col == (row & (PIECES - 1)) * GROUP + (row >> 3), 1.0, 0.0).astype(jnp.bfloat16)


def unfold_matrix():
    row = lax.broadcasted_iota(jnp.int32, (GROUP * PIECES, GROUP * PIECES), 0)
    col = lax.broadcasted_iota(jnp.int32, (GROUP * PIECES, GROUP * PIECES), 1)
    return jnp.where(col == (row & (GROUP - 1)) * PIECES + (row >> 5), 1.0, 0.0).astype(jnp.bfloat16)


def unfold_rows(slab_ref, rows_ref):
    piece = slab_ref.shape[1]
    span = GROUP * PIECES
    unfold = unfold_matrix()
    for b in range(slab_ref.shape[0] // span):
        block = jnp.dot(
            unfold, slab_ref[b * span : (b + 1) * span, :], preferred_element_type=jnp.float32
        ).astype(jnp.bfloat16)
        for p in range(PIECES):
            rows_ref[b * GROUP : (b + 1) * GROUP, p * piece : (p + 1) * piece] = block[
                p * GROUP : (p + 1) * GROUP
            ]


def fold_rows(stack_ref, slab_ref):
    span = GROUP * PIECES
    fold = fold_matrix()
    for b in range(slab_ref.shape[0] // span):
        slab_ref[b * span : (b + 1) * span, :] = jnp.dot(
            fold, stack_ref[b * span : (b + 1) * span, :], preferred_element_type=jnp.float32
        ).astype(jnp.bfloat16)


def stack_piece(stack_ref, values, p):
    span = GROUP * PIECES
    for b in range(values.shape[0] // GROUP):
        stack_ref[b * span + p * GROUP : b * span + (p + 1) * GROUP, :] = values[
            b * GROUP : (b + 1) * GROUP
        ]


def slot_tables(routes_t, place_row, gates_t):
    tokens = routes_t.shape[1]
    devices = place_row.shape[1]
    slots = devices * CAP
    home = lax.broadcasted_iota(jnp.int32, (devices, slots), 0)
    slot = lax.broadcasted_iota(jnp.int32, (devices, slots), 1)
    low = home * CAP
    widen = jnp.where((slot >= low) & (slot < low + CAP), 1.0, 0.0).astype(jnp.bfloat16)
    place = jnp.dot(
        jnp.broadcast_to(place_row.astype(jnp.float32), (8, devices)).astype(jnp.bfloat16),
        widen,
        preferred_element_type=jnp.float32,
    )[:1]
    rank_of = jnp.dot(
        jnp.broadcast_to(
            lax.broadcasted_iota(jnp.int32, (1, devices), 1).astype(jnp.float32), (8, devices)
        ).astype(jnp.bfloat16),
        widen,
        preferred_element_type=jnp.float32,
    )[:1]
    order = lax.broadcasted_iota(jnp.int32, (1, slots), 1).astype(jnp.float32) - rank_of * CAP
    chosen = jnp.transpose(routes_t.astype(jnp.float32))
    gate = None if gates_t is None else jnp.transpose(gates_t)
    taken = jnp.zeros((tokens, slots), jnp.float32)
    weight = jnp.zeros((tokens, slots), jnp.float32)
    for k in range(chosen.shape[1]):
        same = chosen[:, k : k + 1] == place
        taken = jnp.where(same, 1.0, taken)
        if gate is not None:
            weight = jnp.where(same, gate[:, k : k + 1], weight)
    later = lax.broadcasted_iota(jnp.int32, (tokens, tokens), 0)
    earlier = lax.broadcasted_iota(jnp.int32, (tokens, tokens), 1)
    before = jnp.where(earlier < later, 1.0, 0.0).astype(jnp.bfloat16)
    ranks = jnp.dot(before, taken.astype(jnp.bfloat16), preferred_element_type=jnp.float32)
    mine = ranks == order
    return jnp.where(mine, taken, 0.0), jnp.where(mine, weight, 0.0)


def normalise(stream_f, gain):
    scale = lax.rsqrt(jnp.mean(stream_f * stream_f, axis=-1, keepdims=True) + EPS)
    return (stream_f * scale * gain).astype(jnp.bfloat16)


def send_rows(pick, normed, stack_ref, slab_ref):
    piece = slab_ref.shape[1]
    for p in range(PIECES):
        rows = jnp.dot(
            pick, normed[:, p * piece : (p + 1) * piece], preferred_element_type=jnp.float32
        ).astype(jnp.bfloat16)
        stack_piece(stack_ref, rows, p)
    fold_rows(stack_ref, slab_ref)


def slot_numbers(routes_t, place_row):
    choices, tokens = routes_t.shape
    devices = place_row.shape[1]
    place = place_row.astype(jnp.float32)
    chosen = jnp.transpose(routes_t.astype(jnp.float32))
    same = [chosen[:, k : k + 1] == place for k in range(choices)]
    taken = jnp.zeros((tokens, devices), jnp.float32)
    for k in range(choices):
        taken = jnp.where(same[k], 1.0, taken)
    later = lax.broadcasted_iota(jnp.int32, (tokens, tokens), 0)
    earlier = lax.broadcasted_iota(jnp.int32, (tokens, tokens), 1)
    before = jnp.where(earlier < later, 1.0, 0.0).astype(jnp.bfloat16)
    ranks = jnp.dot(before, taken.astype(jnp.bfloat16), preferred_element_type=jnp.float32)
    home = lax.broadcasted_iota(jnp.int32, (tokens, devices), 1).astype(jnp.float32)
    number = home * CAP + ranks
    column = lax.broadcasted_iota(jnp.int32, (tokens, choices), 1)
    slots = jnp.zeros((tokens, choices), jnp.float32)
    for k in range(choices):
        found = jnp.sum(jnp.where(same[k], number, 0.0), axis=1, keepdims=True)
        slots = jnp.where(column == k, found, slots)
    return jnp.transpose(slots).astype(jnp.int32)


def mix_blocks(slots_ref, gates_ref, back_ref, mixed_ref):
    for t in range(mixed_ref.shape[0]):
        total = None
        for k in range(gates_ref.shape[1]):
            block = back_ref[slots_ref[0, k, t]].astype(jnp.float32) * gates_ref[0, k, t]
            total = block if total is None else total + block
        mixed_ref[t] = total


def first_kernel(
    tokens_hbm, gain_hbm, routes_hbm, place_hbm, slab_ref, slots_ref,
    tokens_ref, gain_ref, routes_ref, place_ref, stack_ref, sems,
):
    loads = [
        pltpu.make_async_copy(src, dst, sems.at[i])
        for i, (src, dst) in enumerate(
            (
                (routes_hbm, routes_ref),
                (place_hbm, place_ref),
                (tokens_hbm, tokens_ref),
                (gain_hbm, gain_ref),
            )
        )
    ]
    for load in loads:
        load.start()
    loads[0].wait()
    loads[1].wait()
    select, _ = slot_tables(routes_ref[0], place_ref[0:1, :], None)
    pick = jnp.transpose(select).astype(jnp.bfloat16)
    slots_ref[0] = slot_numbers(routes_ref[0], place_ref[0:1, :])
    loads[2].wait()
    loads[3].wait()
    normed = normalise(tokens_ref[...].astype(jnp.float32), gain_ref[0:1, :])
    send_rows(pick, normed, stack_ref, slab_ref)


def blocks_of(stream_ref, stack_ref):
    piece = stack_ref.shape[1]
    for p in range(PIECES):
        stack_ref[p * GROUP : (p + 1) * GROUP, :] = stream_ref[:, p * piece : (p + 1) * piece]
    return jnp.dot(fold_matrix(), stack_ref[...], preferred_element_type=jnp.float32)


def middle_kernel(
    layer, first, slots_in, gates_in, back_ref, stream_ref, gain_ref, routes_ref, place_ref,
    slab_ref, out_ref, next_ref, mixed_ref, gain_rows, stack_ref, numbers_ref,
    slots_ref, gates_ref, sems,
):
    loads = [
        pltpu.make_async_copy(slots_in, slots_ref.at[0:1], sems.at[0]),
        pltpu.make_async_copy(gates_in.at[layer : layer + 1], gates_ref, sems.at[1]),
        pltpu.make_async_copy(numbers_ref, slots_ref.at[1:2], sems.at[2]),
    ]
    loads[0].start()
    loads[1].start()
    later = slice(layer + 1, layer + 2)
    numbers_ref[0] = slot_numbers(routes_ref[layer + 1], place_ref[later, :])
    loads[2].start()
    _, weight = slot_tables(routes_ref[layer + 1], place_ref[later, :], gates_in[layer + 1])
    high = weight.astype(jnp.bfloat16)
    low = (weight - high.astype(jnp.float32)).astype(jnp.bfloat16)
    next_ref[...] = jnp.concatenate([high, low], axis=0)
    slab_ref[...] = jnp.zeros(slab_ref.shape, jnp.bfloat16)
    tokens, pieces, piece = mixed_ref.shape
    if first:
        blocks = blocks_of(stream_ref, stack_ref)
    else:
        blocks = stream_ref[...].astype(jnp.float32)
    for p in range(pieces):
        gain_rows[p : p + 1, :] = gain_ref[
            layer + 1 : layer + 2, p * piece : (p + 1) * piece
        ]
    loads[0].wait()
    loads[1].wait()
    mix_blocks(slots_ref, gates_ref, back_ref, mixed_ref)
    stream = (blocks + mixed_ref[...].reshape(tokens * pieces, piece)).astype(jnp.bfloat16)
    out_ref[...] = stream
    wide = stream.astype(jnp.float32).reshape(tokens, pieces, piece)
    total = jnp.sum(jnp.sum(wide * wide, axis=2, keepdims=True), axis=1, keepdims=True)
    scale = lax.rsqrt(total / (pieces * piece) + EPS)
    mixed_ref[...] = wide * scale * gain_rows[...][None]
    loads[2].wait()
    for t in range(tokens):
        row = mixed_ref[t].astype(jnp.bfloat16)
        for k in range(slots_ref.shape[1]):
            slab_ref[slots_ref[1, k, t]] = row


def last_kernel(slab_in, blocks_ref, weight_ref, out_ref, rows_ref, stream_ref):
    unfold_rows(blocks_ref, stream_ref)
    unfold_rows(slab_in, rows_ref)
    both = jnp.dot(weight_ref[...], rows_ref[...], preferred_element_type=jnp.float32)
    tokens = weight_ref.shape[0] // 2
    mixed = both[:tokens] + both[tokens:]
    out_ref[...] = (stream_ref[...].astype(jnp.float32) + mixed).astype(jnp.bfloat16)


def block_weight(w_ref, factor, layer, first, count):
    lines = []
    for i in range(w_ref.shape[2] // QBLK):
        line = [
            (
                w_ref[layer, 0, i * QBLK : (i + 1) * QBLK, j * QBLK : (j + 1) * QBLK].astype(
                    jnp.float32
                )
                * factor(i, j)
            ).astype(jnp.bfloat16)
            for j in range(first // QBLK, (first + count) // QBLK)
        ]
        lines.append(jnp.concatenate(line, axis=1))
    return jnp.concatenate(lines, axis=0)


def expert_kernel(
    layer, in_factors, out_factors, slab_in, w_in, w_out,
    slab_ref, x_ref, hid, stack_ref,
):
    def into(first, count):
        return block_weight(w_in, lambda i, j: in_factors[layer, j, :, i : i + 1], layer, first, count)

    def out_of(first, count):
        return block_weight(w_out, lambda i, j: out_factors[layer, i, :, j : j + 1], layer, first, count)

    unfold_rows(slab_in, x_ref)
    ff = w_out.shape[2]
    chunk = slab_ref.shape[1]
    for n in range(ff // chunk):
        gate = jnp.dot(x_ref[...], into(n * chunk, chunk), preferred_element_type=jnp.float32)
        up = jnp.dot(x_ref[...], into(ff + n * chunk, chunk), preferred_element_type=jnp.float32)
        hid[:, n * chunk : (n + 1) * chunk] = (gate / (1.0 + jnp.exp(-gate)) * up).astype(
            jnp.bfloat16
        )
    for m in range(PIECES):
        answer = jnp.dot(
            hid[...], out_of(m * chunk, chunk), preferred_element_type=jnp.float32
        ).astype(jnp.bfloat16)
        stack_piece(stack_ref, answer, m)
    fold_rows(stack_ref, slab_ref)


VM = pl.BlockSpec(memory_space=pltpu.VMEM)
HB = pl.BlockSpec(memory_space=pltpu.HBM)


def expert(layer, slab, weights):
    w_in, in_scale, w_out, out_scale = weights
    rows, piece = slab.shape
    slots = rows // PIECES
    width, ff = w_in.shape[2], w_out.shape[2]
    return pl.pallas_call(
        functools.partial(expert_kernel, layer),
        in_specs=[VM] * 5,
        out_specs=VM,
        out_shape=jax.ShapeDtypeStruct(slab.shape, jnp.bfloat16),
        scratch_shapes=[
            pltpu.VMEM((slots, width), jnp.bfloat16),
            pltpu.VMEM((slots, ff), jnp.bfloat16),
            pltpu.VMEM(slab.shape, jnp.bfloat16),
        ],
        compiler_params=pltpu.CompilerParams(vmem_limit_bytes=20 * MIB),
        cost_estimate=pl.CostEstimate(
            flops=6 * slots * width * ff,
            bytes_accessed=6 * width * ff + 4 * slots * width,
            transcendentals=slots * ff,
        ),
        name="expert",
    )(in_scale, out_scale, slab, w_in, w_out)


def hbm(array):
    return pltpu.with_memory_space_constraint(array, pltpu.HBM)


def exchange(slab, devices):
    split = slab.reshape(devices, slab.shape[0] // devices, slab.shape[1])
    moved = lax.all_to_all(split, AXES, split_axis=0, concat_axis=0, tiled=True)
    return moved.reshape(slab.shape)


def shards(tokens, norm_gain, routes, gates, placement, w_in, in_scale, w_out, out_scale):
    count, width = tokens.shape
    layers, devices = placement.shape
    slots = devices * CAP
    piece = width // PIECES
    routes_t = jnp.swapaxes(routes, 1, 2)
    gates_t = jnp.swapaxes(gates, 1, 2)
    slab_type = jax.ShapeDtypeStruct((slots * PIECES, piece), jnp.bfloat16)
    slots_type = jax.ShapeDtypeStruct((1, *routes_t.shape[1:]), jnp.int32)
    stream_type = jax.ShapeDtypeStruct((count, width), jnp.bfloat16)
    mixed = pltpu.VMEM((count, PIECES, piece), jnp.float32)
    stack = pltpu.VMEM((slots * PIECES, piece), jnp.bfloat16)
    params = pltpu.CompilerParams(vmem_limit_bytes=12 * MIB)

    small = (
        pltpu.VMEM((count, width), jnp.bfloat16),
        pltpu.VMEM(norm_gain.shape, jnp.float32),
        pltpu.VMEM(routes_t.shape, jnp.int32),
        pltpu.VMEM(placement.shape, jnp.int32),
    )
    slab, numbers = pl.pallas_call(
        first_kernel,
        in_specs=[HB] * 4,
        out_specs=(VM, VM),
        out_shape=(slab_type, slots_type),
        scratch_shapes=[*small, stack, pltpu.SemaphoreType.DMA((4,))],
        compiler_params=params,
        cost_estimate=pl.CostEstimate(
            flops=8 * 10**9, bytes_accessed=8 * 10**6, transcendentals=0
        ),
        name="first",
    )(*[hbm(a) for a in (tokens, norm_gain, routes_t, placement)])
    weights = (
        w_in,
        jnp.transpose(in_scale, (0, 3, 1, 2)),
        w_out,
        jnp.transpose(out_scale, (0, 2, 1, 3)),
    )
    stream = tokens
    for layer in range(layers):
        answers = expert(layer, exchange(slab, devices), weights)
        back = exchange(answers, devices)
        if layer + 1 < layers:
            slab, stream, weight = pl.pallas_call(
                functools.partial(middle_kernel, layer, layer == 0),
                in_specs=[VM] * 7,
                out_specs=(VM, VM, VM),
                out_shape=(
                    jax.ShapeDtypeStruct((slots, PIECES, piece), jnp.bfloat16),
                    jax.ShapeDtypeStruct((count * PIECES, piece), jnp.bfloat16),
                    jax.ShapeDtypeStruct((2 * count, slots), jnp.bfloat16),
                ),
                scratch_shapes=[
                    mixed,
                    pltpu.VMEM((PIECES, piece), jnp.float32),
                    pltpu.VMEM((count * PIECES, piece), jnp.bfloat16),
                    pltpu.VMEM(numbers.shape, jnp.int32),
                    pltpu.SMEM((2, *numbers.shape[1:]), jnp.int32),
                    pltpu.SMEM((1, *gates_t.shape[1:]), jnp.float32),
                    pltpu.SemaphoreType.DMA((3,)),
                ],
                compiler_params=params,
                name="middle",
            )(
                numbers, gates_t, back.reshape(slots, PIECES, piece), stream, norm_gain,
                routes_t, placement,
            )
            slab = slab.reshape(slots * PIECES, piece)
        else:
            stream = pl.pallas_call(
                last_kernel,
                in_specs=[VM] * 3,
                out_specs=VM,
                out_shape=stream_type,
                scratch_shapes=[
                    pltpu.VMEM((slots, width), jnp.bfloat16),
                    pltpu.VMEM((count, width), jnp.bfloat16),
                ],
                compiler_params=params,
                name="last",
            )(back, stream, weight)
    return stream


def solution(mesh):
    return jax.shard_map(
        shards,
        mesh=mesh,
        in_specs=(
            P(AXES, None),
            P(),
            P(None, AXES, None),
            P(None, AXES, None),
            P(),
            P(None, AXES, None, None),
            P(None, AXES, None, None),
            P(None, AXES, None, None),
            P(None, AXES, None, None),
        ),
        out_specs=P(AXES, None),
        check_vma=False,
    )
```

```python
import functools

import jax
import jax.numpy as jnp
from jax import lax
from jax.experimental import pallas as pl
from jax.experimental.pallas import tpu as pltpu
from jax.sharding import PartitionSpec as P

AXES = ("dp", "expert")
QBLK = 128
CAP = 3
PIECES = 8
GROUP = 32
EPS = 1e-06
MIB = 1 << 20


def fold_matrix():
    row = lax.broadcasted_iota(jnp.int32, (GROUP * PIECES, GROUP * PIECES), 0)
    col = lax.broadcasted_iota(jnp.int32, (GROUP * PIECES, GROUP * PIECES), 1)
    return jnp.where(col == (row & (PIECES - 1)) * GROUP + (row >> 3), 1.0, 0.0).astype(jnp.bfloat16)


def unfold_matrix():
    row = lax.broadcasted_iota(jnp.int32, (GROUP * PIECES, GROUP * PIECES), 0)
    col = lax.broadcasted_iota(jnp.int32, (GROUP * PIECES, GROUP * PIECES), 1)
    return jnp.where(col == (row & (GROUP - 1)) * PIECES + (row >> 5), 1.0, 0.0).astype(jnp.bfloat16)


def unfold_rows(slab_ref, rows_ref):
    piece = slab_ref.shape[1]
    span = GROUP * PIECES
    unfold = unfold_matrix()
    for b in range(slab_ref.shape[0] // span):
        block = jnp.dot(
            unfold, slab_ref[b * span : (b + 1) * span, :], preferred_element_type=jnp.float32
        ).astype(jnp.bfloat16)
        for p in range(PIECES):
            rows_ref[b * GROUP : (b + 1) * GROUP, p * piece : (p + 1) * piece] = block[
                p * GROUP : (p + 1) * GROUP
            ]


def fold_rows(stack_ref, slab_ref):
    span = GROUP * PIECES
    fold = fold_matrix()
    for b in range(slab_ref.shape[0] // span):
        slab_ref[b * span : (b + 1) * span, :] = jnp.dot(
            fold, stack_ref[b * span : (b + 1) * span, :], preferred_element_type=jnp.float32
        ).astype(jnp.bfloat16)


def stack_piece(stack_ref, values, p):
    span = GROUP * PIECES
    for b in range(values.shape[0] // GROUP):
        stack_ref[b * span + p * GROUP : b * span + (p + 1) * GROUP, :] = values[
            b * GROUP : (b + 1) * GROUP
        ]


def slot_tables(routes_t, place_row, gates_t):
    tokens = routes_t.shape[1]
    devices = place_row.shape[1]
    slots = devices * CAP
    home = lax.broadcasted_iota(jnp.int32, (devices, slots), 0)
    slot = lax.broadcasted_iota(jnp.int32, (devices, slots), 1)
    low = home * CAP
    widen = jnp.where((slot >= low) & (slot < low + CAP), 1.0, 0.0).astype(jnp.bfloat16)
    place = jnp.dot(
        jnp.broadcast_to(place_row.astype(jnp.float32), (8, devices)).astype(jnp.bfloat16),
        widen,
        preferred_element_type=jnp.float32,
    )[:1]
    rank_of = jnp.dot(
        jnp.broadcast_to(
            lax.broadcasted_iota(jnp.int32, (1, devices), 1).astype(jnp.float32), (8, devices)
        ).astype(jnp.bfloat16),
        widen,
        preferred_element_type=jnp.float32,
    )[:1]
    order = lax.broadcasted_iota(jnp.int32, (1, slots), 1).astype(jnp.float32) - rank_of * CAP
    chosen = jnp.transpose(routes_t.astype(jnp.float32))
    gate = None if gates_t is None else jnp.transpose(gates_t)
    taken = jnp.zeros((tokens, slots), jnp.float32)
    weight = jnp.zeros((tokens, slots), jnp.float32)
    for k in range(chosen.shape[1]):
        same = chosen[:, k : k + 1] == place
        taken = jnp.where(same, 1.0, taken)
        if gate is not None:
            weight = jnp.where(same, gate[:, k : k + 1], weight)
    later = lax.broadcasted_iota(jnp.int32, (tokens, tokens), 0)
    earlier = lax.broadcasted_iota(jnp.int32, (tokens, tokens), 1)
    before = jnp.where(earlier < later, 1.0, 0.0).astype(jnp.bfloat16)
    ranks = jnp.dot(before, taken.astype(jnp.bfloat16), preferred_element_type=jnp.float32)
    mine = ranks == order
    return jnp.where(mine, taken, 0.0), jnp.where(mine, weight, 0.0)


def normalise(stream_f, gain):
    scale = lax.rsqrt(jnp.mean(stream_f * stream_f, axis=-1, keepdims=True) + EPS)
    return (stream_f * scale * gain).astype(jnp.bfloat16)


def send_rows(pick, normed, stack_ref, slab_ref):
    piece = slab_ref.shape[1]
    for p in range(PIECES):
        rows = jnp.dot(
            pick, normed[:, p * piece : (p + 1) * piece], preferred_element_type=jnp.float32
        ).astype(jnp.bfloat16)
        stack_piece(stack_ref, rows, p)
    fold_rows(stack_ref, slab_ref)


def slot_numbers(routes_t, place_row):
    choices, tokens = routes_t.shape
    devices = place_row.shape[1]
    place = place_row.astype(jnp.float32)
    chosen = jnp.transpose(routes_t.astype(jnp.float32))
    same = [chosen[:, k : k + 1] == place for k in range(choices)]
    taken = jnp.zeros((tokens, devices), jnp.float32)
    for k in range(choices):
        taken = jnp.where(same[k], 1.0, taken)
    later = lax.broadcasted_iota(jnp.int32, (tokens, tokens), 0)
    earlier = lax.broadcasted_iota(jnp.int32, (tokens, tokens), 1)
    before = jnp.where(earlier < later, 1.0, 0.0).astype(jnp.bfloat16)
    ranks = jnp.dot(before, taken.astype(jnp.bfloat16), preferred_element_type=jnp.float32)
    home = lax.broadcasted_iota(jnp.int32, (tokens, devices), 1).astype(jnp.float32)
    number = home * CAP + ranks
    column = lax.broadcasted_iota(jnp.int32, (tokens, choices), 1)
    slots = jnp.zeros((tokens, choices), jnp.float32)
    for k in range(choices):
        found = jnp.sum(jnp.where(same[k], number, 0.0), axis=1, keepdims=True)
        slots = jnp.where(column == k, found, slots)
    return jnp.transpose(slots).astype(jnp.int32)


def mix_blocks(slots_ref, gates_ref, back_ref, mixed_ref):
    for t in range(mixed_ref.shape[0]):
        total = None
        for k in range(gates_ref.shape[1]):
            block = back_ref[slots_ref[0, k, t]].astype(jnp.float32) * gates_ref[0, k, t]
            total = block if total is None else total + block
        mixed_ref[t] = total


def first_kernel(
    tokens_hbm, gain_hbm, routes_hbm, place_hbm, slab_ref, slots_ref,
    tokens_ref, gain_ref, routes_ref, place_ref, stack_ref, sems,
):
    loads = [
        pltpu.make_async_copy(src, dst, sems.at[i])
        for i, (src, dst) in enumerate(
            (
                (routes_hbm, routes_ref),
                (place_hbm, place_ref),
                (tokens_hbm, tokens_ref),
                (gain_hbm, gain_ref),
            )
        )
    ]
    for load in loads:
        load.start()
    loads[0].wait()
    loads[1].wait()
    select, _ = slot_tables(routes_ref[0], place_ref[0:1, :], None)
    pick = jnp.transpose(select).astype(jnp.bfloat16)
    slots_ref[0] = slot_numbers(routes_ref[0], place_ref[0:1, :])
    loads[2].wait()
    loads[3].wait()
    normed = normalise(tokens_ref[...].astype(jnp.float32), gain_ref[0:1, :])
    send_rows(pick, normed, stack_ref, slab_ref)


def blocks_of(stream_ref, stack_ref):
    piece = stack_ref.shape[1]
    for p in range(PIECES):
        stack_ref[p * GROUP : (p + 1) * GROUP, :] = stream_ref[:, p * piece : (p + 1) * piece]
    return jnp.dot(fold_matrix(), stack_ref[...], preferred_element_type=jnp.float32)


def middle_kernel(
    layer, first, slots_in, gates_in, back_ref, stream_ref, gain_ref, routes_ref, place_ref,
    slab_ref, out_ref, next_ref, mixed_ref, gain_rows, stack_ref, numbers_ref,
    slots_ref, gates_ref, sems,
):
    loads = [
        pltpu.make_async_copy(slots_in, slots_ref.at[0:1], sems.at[0]),
        pltpu.make_async_copy(gates_in.at[layer : layer + 1], gates_ref, sems.at[1]),
        pltpu.make_async_copy(numbers_ref, slots_ref.at[1:2], sems.at[2]),
    ]
    loads[0].start()
    loads[1].start()
    later = slice(layer + 1, layer + 2)
    numbers_ref[0] = slot_numbers(routes_ref[layer + 1], place_ref[later, :])
    loads[2].start()
    _, weight = slot_tables(routes_ref[layer + 1], place_ref[later, :], gates_in[layer + 1])
    high = weight.astype(jnp.bfloat16)
    low = (weight - high.astype(jnp.float32)).astype(jnp.bfloat16)
    next_ref[...] = jnp.concatenate([high, low], axis=0)
    slab_ref[...] = jnp.zeros(slab_ref.shape, jnp.bfloat16)
    tokens, pieces, piece = mixed_ref.shape
    if first:
        blocks = blocks_of(stream_ref, stack_ref)
    else:
        blocks = stream_ref[...].astype(jnp.float32)
    for p in range(pieces):
        gain_rows[p : p + 1, :] = gain_ref[
            layer + 1 : layer + 2, p * piece : (p + 1) * piece
        ]
    loads[0].wait()
    loads[1].wait()
    mix_blocks(slots_ref, gates_ref, back_ref, mixed_ref)
    stream = (blocks + mixed_ref[...].reshape(tokens * pieces, piece)).astype(jnp.bfloat16)
    out_ref[...] = stream
    wide = stream.astype(jnp.float32).reshape(tokens, pieces, piece)
    total = jnp.sum(jnp.sum(wide * wide, axis=2, keepdims=True), axis=1, keepdims=True)
    scale = lax.rsqrt(total / (pieces * piece) + EPS)
    mixed_ref[...] = wide * scale * gain_rows[...][None]
    loads[2].wait()
    for t in range(tokens):
        row = mixed_ref[t].astype(jnp.bfloat16)
        for k in range(slots_ref.shape[1]):
            slab_ref[slots_ref[1, k, t]] = row


def last_kernel(
    slab_in, blocks_ref, weight_ref, out_hbm, rows_ref, stream_ref, out_ref, sems
):
    unfold_rows(blocks_ref, stream_ref)
    unfold_rows(slab_in, rows_ref)
    tokens = weight_ref.shape[0] // 2
    span = out_ref.shape[1] // sems.shape[0]
    stores = []
    for i in range(sems.shape[0]):
        cols = slice(i * span, (i + 1) * span)
        both = jnp.dot(weight_ref[...], rows_ref[:, cols], preferred_element_type=jnp.float32)
        mixed = both[:tokens] + both[tokens:]
        out_ref[:, cols] = (stream_ref[:, cols].astype(jnp.float32) + mixed).astype(
            jnp.bfloat16
        )
        at = pl.ds(i * span, span)
        store = pltpu.make_async_copy(out_ref.at[:, at], out_hbm.at[:, at], sems.at[i])
        store.start()
        stores.append(store)
    for store in stores:
        store.wait()


def block_weight(w_ref, factor, layer, first, count):
    lines = []
    for i in range(w_ref.shape[2] // QBLK):
        line = [
            (
                w_ref[layer, 0, i * QBLK : (i + 1) * QBLK, j * QBLK : (j + 1) * QBLK].astype(
                    jnp.float32
                )
                * factor(i, j)
            ).astype(jnp.bfloat16)
            for j in range(first // QBLK, (first + count) // QBLK)
        ]
        lines.append(jnp.concatenate(line, axis=1))
    return jnp.concatenate(lines, axis=0)


def expert_kernel(
    layer, in_factors, out_factors, slab_in, w_in, w_out,
    slab_ref, x_ref, hid, stack_ref,
):
    def into(first, count):
        return block_weight(w_in, lambda i, j: in_factors[layer, j, :, i : i + 1], layer, first, count)

    def out_of(first, count):
        return block_weight(w_out, lambda i, j: out_factors[layer, i, :, j : j + 1], layer, first, count)

    unfold_rows(slab_in, x_ref)
    ff = w_out.shape[2]
    chunk = slab_ref.shape[1]
    for n in range(ff // chunk):
        gate = jnp.dot(x_ref[...], into(n * chunk, chunk), preferred_element_type=jnp.float32)
        up = jnp.dot(x_ref[...], into(ff + n * chunk, chunk), preferred_element_type=jnp.float32)
        hid[:, n * chunk : (n + 1) * chunk] = (gate / (1.0 + jnp.exp(-gate)) * up).astype(
            jnp.bfloat16
        )
    for m in range(PIECES):
        answer = jnp.dot(
            hid[...], out_of(m * chunk, chunk), preferred_element_type=jnp.float32
        ).astype(jnp.bfloat16)
        stack_piece(stack_ref, answer, m)
    fold_rows(stack_ref, slab_ref)


VM = pl.BlockSpec(memory_space=pltpu.VMEM)
HB = pl.BlockSpec(memory_space=pltpu.HBM)


def expert(layer, slab, weights):
    w_in, in_scale, w_out, out_scale = weights
    rows, piece = slab.shape
    slots = rows // PIECES
    width, ff = w_in.shape[2], w_out.shape[2]
    return pl.pallas_call(
        functools.partial(expert_kernel, layer),
        in_specs=[VM] * 5,
        out_specs=VM,
        out_shape=jax.ShapeDtypeStruct(slab.shape, jnp.bfloat16),
        scratch_shapes=[
            pltpu.VMEM((slots, width), jnp.bfloat16),
            pltpu.VMEM((slots, ff), jnp.bfloat16),
            pltpu.VMEM(slab.shape, jnp.bfloat16),
        ],
        compiler_params=pltpu.CompilerParams(vmem_limit_bytes=20 * MIB),
        cost_estimate=pl.CostEstimate(
            flops=6 * slots * width * ff,
            bytes_accessed=6 * width * ff + 4 * slots * width,
            transcendentals=slots * ff,
        ),
        name="expert",
    )(in_scale, out_scale, slab, w_in, w_out)


def hbm(array):
    return pltpu.with_memory_space_constraint(array, pltpu.HBM)


def exchange(slab, devices):
    split = slab.reshape(devices, slab.shape[0] // devices, slab.shape[1])
    moved = lax.all_to_all(split, AXES, split_axis=0, concat_axis=0, tiled=True)
    return moved.reshape(slab.shape)


def shards(tokens, norm_gain, routes, gates, placement, w_in, in_scale, w_out, out_scale):
    count, width = tokens.shape
    layers, devices = placement.shape
    slots = devices * CAP
    piece = width // PIECES
    routes_t = jnp.swapaxes(routes, 1, 2)
    gates_t = jnp.swapaxes(gates, 1, 2)
    slab_type = jax.ShapeDtypeStruct((slots * PIECES, piece), jnp.bfloat16)
    slots_type = jax.ShapeDtypeStruct((1, *routes_t.shape[1:]), jnp.int32)
    stream_type = jax.ShapeDtypeStruct((count, width), jnp.bfloat16)
    mixed = pltpu.VMEM((count, PIECES, piece), jnp.float32)
    stack = pltpu.VMEM((slots * PIECES, piece), jnp.bfloat16)
    params = pltpu.CompilerParams(vmem_limit_bytes=12 * MIB)

    small = (
        pltpu.VMEM((count, width), jnp.bfloat16),
        pltpu.VMEM(norm_gain.shape, jnp.float32),
        pltpu.VMEM(routes_t.shape, jnp.int32),
        pltpu.VMEM(placement.shape, jnp.int32),
    )
    slab, numbers = pl.pallas_call(
        first_kernel,
        in_specs=[HB] * 4,
        out_specs=(VM, VM),
        out_shape=(slab_type, slots_type),
        scratch_shapes=[*small, stack, pltpu.SemaphoreType.DMA((4,))],
        compiler_params=params,
        cost_estimate=pl.CostEstimate(
            flops=8 * 10**9, bytes_accessed=8 * 10**6, transcendentals=0
        ),
        name="first",
    )(*[hbm(a) for a in (tokens, norm_gain, routes_t, placement)])
    weights = (
        w_in,
        jnp.transpose(in_scale, (0, 3, 1, 2)),
        w_out,
        jnp.transpose(out_scale, (0, 2, 1, 3)),
    )
    stream = tokens
    for layer in range(layers):
        answers = expert(layer, exchange(slab, devices), weights)
        back = exchange(answers, devices)
        if layer + 1 < layers:
            slab, stream, weight = pl.pallas_call(
                functools.partial(middle_kernel, layer, layer == 0),
                in_specs=[VM] * 7,
                out_specs=(VM, VM, VM),
                out_shape=(
                    jax.ShapeDtypeStruct((slots, PIECES, piece), jnp.bfloat16),
                    jax.ShapeDtypeStruct((count * PIECES, piece), jnp.bfloat16),
                    jax.ShapeDtypeStruct((2 * count, slots), jnp.bfloat16),
                ),
                scratch_shapes=[
                    mixed,
                    pltpu.VMEM((PIECES, piece), jnp.float32),
                    pltpu.VMEM((count * PIECES, piece), jnp.bfloat16),
                    pltpu.VMEM(numbers.shape, jnp.int32),
                    pltpu.SMEM((2, *numbers.shape[1:]), jnp.int32),
                    pltpu.SMEM((1, *gates_t.shape[1:]), jnp.float32),
                    pltpu.SemaphoreType.DMA((3,)),
                ],
                compiler_params=params,
                name="middle",
            )(
                numbers, gates_t, back.reshape(slots, PIECES, piece), stream, norm_gain,
                routes_t, placement,
            )
            slab = slab.reshape(slots * PIECES, piece)
        else:
            stream = pl.pallas_call(
                last_kernel,
                in_specs=[VM] * 3,
                out_specs=HB,
                out_shape=pltpu.HBM((count, width), jnp.bfloat16),
                scratch_shapes=[
                    pltpu.VMEM((slots, width), jnp.bfloat16),
                    pltpu.VMEM((count, width), jnp.bfloat16),
                    pltpu.VMEM((count, width), jnp.bfloat16),
                    pltpu.SemaphoreType.DMA((4,)),
                ],
                compiler_params=params,
                name="last",
            )(back, stream, weight)
    return stream


def solution(mesh):
    return jax.shard_map(
        shards,
        mesh=mesh,
        in_specs=(
            P(AXES, None),
            P(),
            P(None, AXES, None),
            P(None, AXES, None),
            P(),
            P(None, AXES, None, None),
            P(None, AXES, None, None),
            P(None, AXES, None, None),
            P(None, AXES, None, None),
        ),
        out_specs=P(AXES, None),
        check_vma=False,
    )
```

```python
import functools

import jax
import jax.numpy as jnp
from jax import lax
from jax.experimental import pallas as pl
from jax.experimental.pallas import tpu as pltpu
from jax.sharding import PartitionSpec as P

AXES = ("dp", "expert")
QBLK = 128
CAP = 3
PIECES = 8
GROUP = 32
EPS = 1e-06
MIB = 1 << 20


def fold_matrix():
    row = lax.broadcasted_iota(jnp.int32, (GROUP * PIECES, GROUP * PIECES), 0)
    col = lax.broadcasted_iota(jnp.int32, (GROUP * PIECES, GROUP * PIECES), 1)
    return jnp.where(col == (row & (PIECES - 1)) * GROUP + (row >> 3), 1.0, 0.0).astype(jnp.bfloat16)


def unfold_matrix():
    row = lax.broadcasted_iota(jnp.int32, (GROUP * PIECES, GROUP * PIECES), 0)
    col = lax.broadcasted_iota(jnp.int32, (GROUP * PIECES, GROUP * PIECES), 1)
    return jnp.where(col == (row & (GROUP - 1)) * PIECES + (row >> 5), 1.0, 0.0).astype(jnp.bfloat16)


def unfold_rows(slab_ref, rows_ref):
    piece = slab_ref.shape[1]
    span = GROUP * PIECES
    unfold = unfold_matrix()
    for b in range(slab_ref.shape[0] // span):
        block = jnp.dot(
            unfold, slab_ref[b * span : (b + 1) * span, :], preferred_element_type=jnp.float32
        ).astype(jnp.bfloat16)
        for p in range(PIECES):
            rows_ref[b * GROUP : (b + 1) * GROUP, p * piece : (p + 1) * piece] = block[
                p * GROUP : (p + 1) * GROUP
            ]


def fold_rows(stack_ref, slab_ref):
    span = GROUP * PIECES
    fold = fold_matrix()
    for b in range(slab_ref.shape[0] // span):
        slab_ref[b * span : (b + 1) * span, :] = jnp.dot(
            fold, stack_ref[b * span : (b + 1) * span, :], preferred_element_type=jnp.float32
        ).astype(jnp.bfloat16)


def stack_piece(stack_ref, values, p):
    span = GROUP * PIECES
    for b in range(values.shape[0] // GROUP):
        stack_ref[b * span + p * GROUP : b * span + (p + 1) * GROUP, :] = values[
            b * GROUP : (b + 1) * GROUP
        ]


def slot_tables(routes_t, place_row, gates_t):
    tokens = routes_t.shape[1]
    devices = place_row.shape[1]
    slots = devices * CAP
    home = lax.broadcasted_iota(jnp.int32, (devices, slots), 0)
    slot = lax.broadcasted_iota(jnp.int32, (devices, slots), 1)
    low = home * CAP
    widen = jnp.where((slot >= low) & (slot < low + CAP), 1.0, 0.0).astype(jnp.bfloat16)
    place = jnp.dot(
        jnp.broadcast_to(place_row.astype(jnp.float32), (8, devices)).astype(jnp.bfloat16),
        widen,
        preferred_element_type=jnp.float32,
    )[:1]
    rank_of = jnp.dot(
        jnp.broadcast_to(
            lax.broadcasted_iota(jnp.int32, (1, devices), 1).astype(jnp.float32), (8, devices)
        ).astype(jnp.bfloat16),
        widen,
        preferred_element_type=jnp.float32,
    )[:1]
    order = lax.broadcasted_iota(jnp.int32, (1, slots), 1).astype(jnp.float32) - rank_of * CAP
    chosen = jnp.transpose(routes_t.astype(jnp.float32))
    gate = None if gates_t is None else jnp.transpose(gates_t)
    taken = jnp.zeros((tokens, slots), jnp.float32)
    weight = jnp.zeros((tokens, slots), jnp.float32)
    for k in range(chosen.shape[1]):
        same = chosen[:, k : k + 1] == place
        taken = jnp.where(same, 1.0, taken)
        if gate is not None:
            weight = jnp.where(same, gate[:, k : k + 1], weight)
    later = lax.broadcasted_iota(jnp.int32, (tokens, tokens), 0)
    earlier = lax.broadcasted_iota(jnp.int32, (tokens, tokens), 1)
    before = jnp.where(earlier < later, 1.0, 0.0).astype(jnp.bfloat16)
    ranks = jnp.dot(before, taken.astype(jnp.bfloat16), preferred_element_type=jnp.float32)
    mine = ranks == order
    return jnp.where(mine, taken, 0.0), jnp.where(mine, weight, 0.0)


def normalise(stream_f, gain):
    scale = lax.rsqrt(jnp.mean(stream_f * stream_f, axis=-1, keepdims=True) + EPS)
    return (stream_f * scale * gain).astype(jnp.bfloat16)


def send_rows(pick, normed, stack_ref, slab_ref):
    piece = slab_ref.shape[1]
    for p in range(PIECES):
        rows = jnp.dot(
            pick, normed[:, p * piece : (p + 1) * piece], preferred_element_type=jnp.float32
        ).astype(jnp.bfloat16)
        stack_piece(stack_ref, rows, p)
    fold_rows(stack_ref, slab_ref)


def slot_numbers(routes_t, place_row):
    choices, tokens = routes_t.shape
    devices = place_row.shape[1]
    place = place_row.astype(jnp.float32)
    chosen = jnp.transpose(routes_t.astype(jnp.float32))
    same = [chosen[:, k : k + 1] == place for k in range(choices)]
    taken = jnp.zeros((tokens, devices), jnp.float32)
    for k in range(choices):
        taken = jnp.where(same[k], 1.0, taken)
    later = lax.broadcasted_iota(jnp.int32, (tokens, tokens), 0)
    earlier = lax.broadcasted_iota(jnp.int32, (tokens, tokens), 1)
    before = jnp.where(earlier < later, 1.0, 0.0).astype(jnp.bfloat16)
    ranks = jnp.dot(before, taken.astype(jnp.bfloat16), preferred_element_type=jnp.float32)
    home = lax.broadcasted_iota(jnp.int32, (tokens, devices), 1).astype(jnp.float32)
    number = home * CAP + ranks
    column = lax.broadcasted_iota(jnp.int32, (tokens, choices), 1)
    slots = jnp.zeros((tokens, choices), jnp.float32)
    for k in range(choices):
        found = jnp.sum(jnp.where(same[k], number, 0.0), axis=1, keepdims=True)
        slots = jnp.where(column == k, found, slots)
    return jnp.transpose(slots).astype(jnp.int32)


def mix_blocks(slots_ref, gates_ref, back_ref, mixed_ref):
    for t in range(mixed_ref.shape[0]):
        total = None
        for k in range(gates_ref.shape[1]):
            block = back_ref[slots_ref[0, k, t]].astype(jnp.float32) * gates_ref[0, k, t]
            total = block if total is None else total + block
        mixed_ref[t] = total


def first_kernel(
    tokens_hbm, gain_hbm, routes_hbm, place_hbm, slab_ref,
    tokens_ref, gain_ref, routes_ref, place_ref, stack_ref, sems,
):
    loads = [
        pltpu.make_async_copy(src, dst, sems.at[i])
        for i, (src, dst) in enumerate(
            (
                (routes_hbm, routes_ref),
                (place_hbm, place_ref),
                (tokens_hbm, tokens_ref),
                (gain_hbm, gain_ref),
            )
        )
    ]
    for load in loads:
        load.start()
    loads[0].wait()
    loads[1].wait()
    select, _ = slot_tables(routes_ref[0], place_ref[0:1, :], None)
    pick = jnp.transpose(select).astype(jnp.bfloat16)
    loads[2].wait()
    loads[3].wait()
    normed = normalise(tokens_ref[...].astype(jnp.float32), gain_ref[0:1, :])
    send_rows(pick, normed, stack_ref, slab_ref)


def blocks_of(stream_ref, stack_ref):
    piece = stack_ref.shape[1]
    for p in range(PIECES):
        stack_ref[p * GROUP : (p + 1) * GROUP, :] = stream_ref[:, p * piece : (p + 1) * piece]
    return jnp.dot(fold_matrix(), stack_ref[...], preferred_element_type=jnp.float32)


def middle_kernel(
    layer, first, slots_in, gates_in, back_ref, stream_ref, gain_ref, routes_ref, place_ref,
    slab_ref, out_ref, next_ref, mixed_ref, gain_rows, stack_ref, numbers_ref,
    slots_ref, gates_ref, sems,
):
    loads = [
        pltpu.make_async_copy(slots_in, slots_ref.at[0:1], sems.at[0]),
        pltpu.make_async_copy(gates_in.at[layer : layer + 1], gates_ref, sems.at[1]),
        pltpu.make_async_copy(numbers_ref, slots_ref.at[1:2], sems.at[2]),
    ]
    loads[0].start()
    loads[1].start()
    later = slice(layer + 1, layer + 2)
    numbers_ref[0] = slot_numbers(routes_ref[layer + 1], place_ref[later, :])
    loads[2].start()
    _, weight = slot_tables(routes_ref[layer + 1], place_ref[later, :], gates_in[layer + 1])
    high = weight.astype(jnp.bfloat16)
    low = (weight - high.astype(jnp.float32)).astype(jnp.bfloat16)
    next_ref[...] = jnp.concatenate([high, low], axis=0)
    slab_ref[...] = jnp.zeros(slab_ref.shape, jnp.bfloat16)
    tokens, pieces, piece = mixed_ref.shape
    if first:
        blocks = blocks_of(stream_ref, stack_ref)
    else:
        blocks = stream_ref[...].astype(jnp.float32)
    for p in range(pieces):
        gain_rows[p : p + 1, :] = gain_ref[
            layer + 1 : layer + 2, p * piece : (p + 1) * piece
        ]
    loads[0].wait()
    loads[1].wait()
    mix_blocks(slots_ref, gates_ref, back_ref, mixed_ref)
    stream = (blocks + mixed_ref[...].reshape(tokens * pieces, piece)).astype(jnp.bfloat16)
    out_ref[...] = stream
    wide = stream.astype(jnp.float32).reshape(tokens, pieces, piece)
    total = jnp.sum(jnp.sum(wide * wide, axis=2, keepdims=True), axis=1, keepdims=True)
    scale = lax.rsqrt(total / (pieces * piece) + EPS)
    mixed_ref[...] = wide * scale * gain_rows[...][None]
    loads[2].wait()
    for t in range(tokens):
        row = mixed_ref[t].astype(jnp.bfloat16)
        for k in range(slots_ref.shape[1]):
            slab_ref[slots_ref[1, k, t]] = row


def last_kernel(slab_in, blocks_ref, weight_ref, out_ref, rows_ref, stream_ref):
    unfold_rows(blocks_ref, stream_ref)
    unfold_rows(slab_in, rows_ref)
    both = jnp.dot(weight_ref[...], rows_ref[...], preferred_element_type=jnp.float32)
    tokens = weight_ref.shape[0] // 2
    mixed = both[:tokens] + both[tokens:]
    out_ref[...] = (stream_ref[...].astype(jnp.float32) + mixed).astype(jnp.bfloat16)


def block_weight(w_ref, factor, layer, first, count):
    lines = []
    for i in range(w_ref.shape[2] // QBLK):
        line = [
            (
                w_ref[layer, 0, i * QBLK : (i + 1) * QBLK, j * QBLK : (j + 1) * QBLK].astype(
                    jnp.float32
                )
                * factor(i, j)
            ).astype(jnp.bfloat16)
            for j in range(first // QBLK, (first + count) // QBLK)
        ]
        lines.append(jnp.concatenate(line, axis=1))
    return jnp.concatenate(lines, axis=0)


def expert_kernel(
    layer, in_factors, out_factors, slab_in, w_in, w_out, routes_ref, place_ref,
    slab_ref, slots_ref, x_ref, hid, stack_ref,
):
    def into(first, count):
        return block_weight(w_in, lambda i, j: in_factors[layer, j, :, i : i + 1], layer, first, count)

    def out_of(first, count):
        return block_weight(w_out, lambda i, j: out_factors[layer, i, :, j : j + 1], layer, first, count)

    if layer + 1 < routes_ref.shape[0]:
        slots_ref[0] = slot_numbers(routes_ref[layer], place_ref[layer : layer + 1, :])
    else:
        slots_ref[...] = jnp.zeros(slots_ref.shape, jnp.int32)
    unfold_rows(slab_in, x_ref)
    ff = w_out.shape[2]
    chunk = slab_ref.shape[1]
    for n in range(ff // chunk):
        gate = jnp.dot(x_ref[...], into(n * chunk, chunk), preferred_element_type=jnp.float32)
        up = jnp.dot(x_ref[...], into(ff + n * chunk, chunk), preferred_element_type=jnp.float32)
        hid[:, n * chunk : (n + 1) * chunk] = (gate / (1.0 + jnp.exp(-gate)) * up).astype(
            jnp.bfloat16
        )
    for m in range(PIECES):
        answer = jnp.dot(
            hid[...], out_of(m * chunk, chunk), preferred_element_type=jnp.float32
        ).astype(jnp.bfloat16)
        stack_piece(stack_ref, answer, m)
    fold_rows(stack_ref, slab_ref)


VM = pl.BlockSpec(memory_space=pltpu.VMEM)
HB = pl.BlockSpec(memory_space=pltpu.HBM)


def expert(layer, slab, weights, routes_t, place):
    w_in, in_scale, w_out, out_scale = weights
    rows, piece = slab.shape
    slots = rows // PIECES
    width, ff = w_in.shape[2], w_out.shape[2]
    return pl.pallas_call(
        functools.partial(expert_kernel, layer),
        in_specs=[VM] * 7,
        out_specs=(VM, VM),
        out_shape=(
            jax.ShapeDtypeStruct(slab.shape, jnp.bfloat16),
            jax.ShapeDtypeStruct((1, *routes_t.shape[1:]), jnp.int32),
        ),
        scratch_shapes=[
            pltpu.VMEM((slots, width), jnp.bfloat16),
            pltpu.VMEM((slots, ff), jnp.bfloat16),
            pltpu.VMEM(slab.shape, jnp.bfloat16),
        ],
        compiler_params=pltpu.CompilerParams(vmem_limit_bytes=20 * MIB),
        cost_estimate=pl.CostEstimate(
            flops=6 * slots * width * ff,
            bytes_accessed=6 * width * ff + 4 * slots * width,
            transcendentals=slots * ff,
        ),
        name="expert",
    )(in_scale, out_scale, slab, w_in, w_out, routes_t, place)


def hbm(array):
    return pltpu.with_memory_space_constraint(array, pltpu.HBM)


def exchange(slab, devices):
    split = slab.reshape(devices, slab.shape[0] // devices, slab.shape[1])
    moved = lax.all_to_all(split, AXES, split_axis=0, concat_axis=0, tiled=True)
    return moved.reshape(slab.shape)


def shards(tokens, norm_gain, routes, gates, placement, w_in, in_scale, w_out, out_scale):
    count, width = tokens.shape
    layers, devices = placement.shape
    slots = devices * CAP
    piece = width // PIECES
    routes_t = jnp.swapaxes(routes, 1, 2)
    gates_t = jnp.swapaxes(gates, 1, 2)
    slab_type = jax.ShapeDtypeStruct((slots * PIECES, piece), jnp.bfloat16)
    stream_type = jax.ShapeDtypeStruct((count, width), jnp.bfloat16)
    mixed = pltpu.VMEM((count, PIECES, piece), jnp.float32)
    stack = pltpu.VMEM((slots * PIECES, piece), jnp.bfloat16)
    params = pltpu.CompilerParams(vmem_limit_bytes=12 * MIB)

    small = (
        pltpu.VMEM((count, width), jnp.bfloat16),
        pltpu.VMEM(norm_gain.shape, jnp.float32),
        pltpu.VMEM(routes_t.shape, jnp.int32),
        pltpu.VMEM(placement.shape, jnp.int32),
    )
    slab = pl.pallas_call(
        first_kernel,
        in_specs=[HB] * 4,
        out_specs=VM,
        out_shape=slab_type,
        scratch_shapes=[*small, stack, pltpu.SemaphoreType.DMA((4,))],
        compiler_params=params,
        cost_estimate=pl.CostEstimate(
            flops=8 * 10**9, bytes_accessed=8 * 10**6, transcendentals=0
        ),
        name="first",
    )(*[hbm(a) for a in (tokens, norm_gain, routes_t, placement)])
    weights = (
        w_in,
        jnp.transpose(in_scale, (0, 3, 1, 2)),
        w_out,
        jnp.transpose(out_scale, (0, 2, 1, 3)),
    )
    stream = tokens
    for layer in range(layers):
        answers, numbers = expert(
            layer, exchange(slab, devices), weights, routes_t, placement
        )
        back = exchange(answers, devices)
        if layer + 1 < layers:
            slab, stream, weight = pl.pallas_call(
                functools.partial(middle_kernel, layer, layer == 0),
                in_specs=[VM] * 7,
                out_specs=(VM, VM, VM),
                out_shape=(
                    jax.ShapeDtypeStruct((slots, PIECES, piece), jnp.bfloat16),
                    jax.ShapeDtypeStruct((count * PIECES, piece), jnp.bfloat16),
                    jax.ShapeDtypeStruct((2 * count, slots), jnp.bfloat16),
                ),
                scratch_shapes=[
                    mixed,
                    pltpu.VMEM((PIECES, piece), jnp.float32),
                    pltpu.VMEM((count * PIECES, piece), jnp.bfloat16),
                    pltpu.VMEM(numbers.shape, jnp.int32),
                    pltpu.SMEM((2, *numbers.shape[1:]), jnp.int32),
                    pltpu.SMEM((1, *gates_t.shape[1:]), jnp.float32),
                    pltpu.SemaphoreType.DMA((3,)),
                ],
                compiler_params=params,
                name="middle",
            )(
                numbers, gates_t, back.reshape(slots, PIECES, piece), stream, norm_gain,
                routes_t, placement,
            )
            slab = slab.reshape(slots * PIECES, piece)
        else:
            stream = pl.pallas_call(
                last_kernel,
                in_specs=[VM] * 3,
                out_specs=VM,
                out_shape=stream_type,
                scratch_shapes=[
                    pltpu.VMEM((slots, width), jnp.bfloat16),
                    pltpu.VMEM((count, width), jnp.bfloat16),
                ],
                compiler_params=params,
                name="last",
            )(back, stream, weight)
    return stream


def solution(mesh):
    return jax.shard_map(
        shards,
        mesh=mesh,
        in_specs=(
            P(AXES, None),
            P(),
            P(None, AXES, None),
            P(None, AXES, None),
            P(),
            P(None, AXES, None, None),
            P(None, AXES, None, None),
            P(None, AXES, None, None),
            P(None, AXES, None, None),
        ),
        out_specs=P(AXES, None),
        check_vma=False,
    )
```

```python
import functools

import jax
import jax.numpy as jnp
from jax import lax
from jax.experimental import pallas as pl
from jax.experimental.pallas import tpu as pltpu
from jax.sharding import PartitionSpec as P

AXES = ("dp", "expert")
QBLK = 128
CAP = 3
PIECES = 8
GROUP = 32
EPS = 1e-06
MIB = 1 << 20


def fold_matrix():
    row = lax.broadcasted_iota(jnp.int32, (GROUP * PIECES, GROUP * PIECES), 0)
    col = lax.broadcasted_iota(jnp.int32, (GROUP * PIECES, GROUP * PIECES), 1)
    return jnp.where(col == (row & (PIECES - 1)) * GROUP + (row >> 3), 1.0, 0.0).astype(jnp.bfloat16)


def unfold_matrix():
    row = lax.broadcasted_iota(jnp.int32, (GROUP * PIECES, GROUP * PIECES), 0)
    col = lax.broadcasted_iota(jnp.int32, (GROUP * PIECES, GROUP * PIECES), 1)
    return jnp.where(col == (row & (GROUP - 1)) * PIECES + (row >> 5), 1.0, 0.0).astype(jnp.bfloat16)


def unfold_rows(slab_ref, rows_ref):
    piece = slab_ref.shape[1]
    span = GROUP * PIECES
    unfold = unfold_matrix()
    for b in range(slab_ref.shape[0] // span):
        block = jnp.dot(
            unfold, slab_ref[b * span : (b + 1) * span, :], preferred_element_type=jnp.float32
        ).astype(jnp.bfloat16)
        for p in range(PIECES):
            rows_ref[b * GROUP : (b + 1) * GROUP, p * piece : (p + 1) * piece] = block[
                p * GROUP : (p + 1) * GROUP
            ]


def fold_rows(stack_ref, slab_ref):
    span = GROUP * PIECES
    fold = fold_matrix()
    for b in range(slab_ref.shape[0] // span):
        slab_ref[b * span : (b + 1) * span, :] = jnp.dot(
            fold, stack_ref[b * span : (b + 1) * span, :], preferred_element_type=jnp.float32
        ).astype(jnp.bfloat16)


def stack_piece(stack_ref, values, p):
    span = GROUP * PIECES
    for b in range(values.shape[0] // GROUP):
        stack_ref[b * span + p * GROUP : b * span + (p + 1) * GROUP, :] = values[
            b * GROUP : (b + 1) * GROUP
        ]


def slot_tables(routes_t, place_row, gates_t):
    tokens = routes_t.shape[1]
    devices = place_row.shape[1]
    slots = devices * CAP
    home = lax.broadcasted_iota(jnp.int32, (devices, slots), 0)
    slot = lax.broadcasted_iota(jnp.int32, (devices, slots), 1)
    low = home * CAP
    widen = jnp.where((slot >= low) & (slot < low + CAP), 1.0, 0.0).astype(jnp.bfloat16)
    place = jnp.dot(
        jnp.broadcast_to(place_row.astype(jnp.float32), (8, devices)).astype(jnp.bfloat16),
        widen,
        preferred_element_type=jnp.float32,
    )[:1]
    rank_of = jnp.dot(
        jnp.broadcast_to(
            lax.broadcasted_iota(jnp.int32, (1, devices), 1).astype(jnp.float32), (8, devices)
        ).astype(jnp.bfloat16),
        widen,
        preferred_element_type=jnp.float32,
    )[:1]
    order = lax.broadcasted_iota(jnp.int32, (1, slots), 1).astype(jnp.float32) - rank_of * CAP
    chosen = jnp.transpose(routes_t.astype(jnp.float32))
    gate = None if gates_t is None else jnp.transpose(gates_t)
    taken = jnp.zeros((tokens, slots), jnp.float32)
    weight = jnp.zeros((tokens, slots), jnp.float32)
    for k in range(chosen.shape[1]):
        same = chosen[:, k : k + 1] == place
        taken = jnp.where(same, 1.0, taken)
        if gate is not None:
            weight = jnp.where(same, gate[:, k : k + 1], weight)
    later = lax.broadcasted_iota(jnp.int32, (tokens, tokens), 0)
    earlier = lax.broadcasted_iota(jnp.int32, (tokens, tokens), 1)
    before = jnp.where(earlier < later, 1.0, 0.0).astype(jnp.bfloat16)
    ranks = jnp.dot(before, taken.astype(jnp.bfloat16), preferred_element_type=jnp.float32)
    mine = ranks == order
    return jnp.where(mine, taken, 0.0), jnp.where(mine, weight, 0.0)


def normalise(stream_f, gain):
    scale = lax.rsqrt(jnp.mean(stream_f * stream_f, axis=-1, keepdims=True) + EPS)
    return (stream_f * scale * gain).astype(jnp.bfloat16)


def send_rows(pick, normed, stack_ref, slab_ref):
    piece = slab_ref.shape[1]
    for p in range(PIECES):
        rows = jnp.dot(
            pick, normed[:, p * piece : (p + 1) * piece], preferred_element_type=jnp.float32
        ).astype(jnp.bfloat16)
        stack_piece(stack_ref, rows, p)
    fold_rows(stack_ref, slab_ref)


def slot_numbers(routes_t, place_row):
    choices, tokens = routes_t.shape
    devices = place_row.shape[1]
    place = place_row.astype(jnp.float32)
    chosen = jnp.transpose(routes_t.astype(jnp.float32))
    same = [chosen[:, k : k + 1] == place for k in range(choices)]
    taken = jnp.zeros((tokens, devices), jnp.float32)
    for k in range(choices):
        taken = jnp.where(same[k], 1.0, taken)
    later = lax.broadcasted_iota(jnp.int32, (tokens, tokens), 0)
    earlier = lax.broadcasted_iota(jnp.int32, (tokens, tokens), 1)
    before = jnp.where(earlier < later, 1.0, 0.0).astype(jnp.bfloat16)
    ranks = jnp.dot(before, taken.astype(jnp.bfloat16), preferred_element_type=jnp.float32)
    home = lax.broadcasted_iota(jnp.int32, (tokens, devices), 1).astype(jnp.float32)
    number = home * CAP + ranks
    column = lax.broadcasted_iota(jnp.int32, (tokens, choices), 1)
    slots = jnp.zeros((tokens, choices), jnp.float32)
    for k in range(choices):
        found = jnp.sum(jnp.where(same[k], number, 0.0), axis=1, keepdims=True)
        slots = jnp.where(column == k, found, slots)
    return jnp.transpose(slots).astype(jnp.int32)


def mix_blocks(slots_ref, gates_ref, back_ref, mixed_ref):
    for t in range(mixed_ref.shape[0]):
        total = None
        for k in range(gates_ref.shape[1]):
            block = back_ref[slots_ref[0, k, t]].astype(jnp.float32) * gates_ref[0, k, t]
            total = block if total is None else total + block
        mixed_ref[t] = total


def first_kernel(
    tokens_hbm, gain_hbm, routes_hbm, place_hbm, slab_ref,
    tokens_ref, gain_ref, routes_ref, place_ref, stack_ref, sems,
):
    loads = [
        pltpu.make_async_copy(src, dst, sems.at[i])
        for i, (src, dst) in enumerate(
            (
                (routes_hbm, routes_ref),
                (place_hbm, place_ref),
                (tokens_hbm, tokens_ref),
                (gain_hbm, gain_ref),
            )
        )
    ]
    for load in loads:
        load.start()
    loads[0].wait()
    loads[1].wait()
    select, _ = slot_tables(routes_ref[0], place_ref[0:1, :], None)
    pick = jnp.transpose(select).astype(jnp.bfloat16)
    loads[2].wait()
    loads[3].wait()
    normed = normalise(tokens_ref[...].astype(jnp.float32), gain_ref[0:1, :])
    send_rows(pick, normed, stack_ref, slab_ref)


def blocks_of(stream_ref, stack_ref):
    piece = stack_ref.shape[1]
    for p in range(PIECES):
        stack_ref[p * GROUP : (p + 1) * GROUP, :] = stream_ref[:, p * piece : (p + 1) * piece]
    return jnp.dot(fold_matrix(), stack_ref[...], preferred_element_type=jnp.float32)


def middle_kernel(
    layer, first, slots_in, gates_in, back_ref, stream_ref, gain_ref, routes_ref, place_ref,
    slab_ref, out_ref, next_ref, mixed_ref, gain_rows, stack_ref, numbers_ref,
    slots_ref, gates_ref, sems,
):
    loads = [
        pltpu.make_async_copy(slots_in, slots_ref.at[0:1], sems.at[0]),
        pltpu.make_async_copy(gates_in.at[layer : layer + 1], gates_ref, sems.at[1]),
        pltpu.make_async_copy(numbers_ref, slots_ref.at[1:2], sems.at[2]),
    ]
    loads[0].start()
    loads[1].start()
    later = slice(layer + 1, layer + 2)
    numbers_ref[0] = slot_numbers(routes_ref[layer + 1], place_ref[later, :])
    loads[2].start()
    _, weight = slot_tables(routes_ref[layer + 1], place_ref[later, :], gates_in[layer + 1])
    high = weight.astype(jnp.bfloat16)
    low = (weight - high.astype(jnp.float32)).astype(jnp.bfloat16)
    next_ref[...] = jnp.concatenate([high, low], axis=0)
    slab_ref[...] = jnp.zeros(slab_ref.shape, jnp.bfloat16)
    tokens, pieces, piece = mixed_ref.shape
    if first:
        blocks = blocks_of(stream_ref, stack_ref)
    else:
        blocks = stream_ref[...].astype(jnp.float32)
    for p in range(pieces):
        gain_rows[p : p + 1, :] = gain_ref[
            layer + 1 : layer + 2, p * piece : (p + 1) * piece
        ]
    loads[0].wait()
    loads[1].wait()
    mix_blocks(slots_ref, gates_ref, back_ref, mixed_ref)
    stream = (blocks + mixed_ref[...].reshape(tokens * pieces, piece)).astype(jnp.bfloat16)
    out_ref[...] = stream
    wide = stream.astype(jnp.float32).reshape(tokens, pieces, piece)
    total = jnp.sum(jnp.sum(wide * wide, axis=2, keepdims=True), axis=1, keepdims=True)
    scale = lax.rsqrt(total / (pieces * piece) + EPS)
    mixed_ref[...] = wide * scale * gain_rows[...][None]
    loads[2].wait()
    for t in range(tokens):
        row = mixed_ref[t].astype(jnp.bfloat16)
        for k in range(slots_ref.shape[1]):
            slab_ref[slots_ref[1, k, t]] = row


def last_kernel(slab_in, blocks_ref, weight_ref, out_ref, rows_ref, stream_ref):
    unfold_rows(blocks_ref, stream_ref)
    unfold_rows(slab_in, rows_ref)
    both = jnp.dot(weight_ref[...], rows_ref[...], preferred_element_type=jnp.float32)
    tokens = weight_ref.shape[0] // 2
    mixed = both[:tokens] + both[tokens:]
    out_ref[...] = (stream_ref[...].astype(jnp.float32) + mixed).astype(jnp.bfloat16)


def block_weight(w_ref, factor, layer, first, count):
    lines = []
    for i in range(w_ref.shape[2] // QBLK):
        line = [
            (
                w_ref[layer, 0, i * QBLK : (i + 1) * QBLK, j * QBLK : (j + 1) * QBLK].astype(
                    jnp.float32
                )
                * factor(i, j)
            ).astype(jnp.bfloat16)
            for j in range(first // QBLK, (first + count) // QBLK)
        ]
        lines.append(jnp.concatenate(line, axis=1))
    return jnp.concatenate(lines, axis=0)


def expert_kernel(
    layer, in_factors, out_factors, slab_in, w_in, w_out, routes_ref, place_ref,
    slab_ref, *rest,
):
    def into(first, count):
        return block_weight(w_in, lambda i, j: in_factors[layer, j, :, i : i + 1], layer, first, count)

    def out_of(first, count):
        return block_weight(w_out, lambda i, j: out_factors[layer, i, :, j : j + 1], layer, first, count)

    x_ref, hid, stack_ref = rest[-3:]
    if len(rest) > 3:
        rest[0][0] = slot_numbers(routes_ref[layer], place_ref[layer : layer + 1, :])
    unfold_rows(slab_in, x_ref)
    ff = w_out.shape[2]
    chunk = slab_ref.shape[1]
    for n in range(ff // chunk):
        gate = jnp.dot(x_ref[...], into(n * chunk, chunk), preferred_element_type=jnp.float32)
        up = jnp.dot(x_ref[...], into(ff + n * chunk, chunk), preferred_element_type=jnp.float32)
        hid[:, n * chunk : (n + 1) * chunk] = (gate / (1.0 + jnp.exp(-gate)) * up).astype(
            jnp.bfloat16
        )
    for m in range(PIECES):
        answer = jnp.dot(
            hid[...], out_of(m * chunk, chunk), preferred_element_type=jnp.float32
        ).astype(jnp.bfloat16)
        stack_piece(stack_ref, answer, m)
    fold_rows(stack_ref, slab_ref)


VM = pl.BlockSpec(memory_space=pltpu.VMEM)
HB = pl.BlockSpec(memory_space=pltpu.HBM)


def expert(layer, slab, weights, routes_t, place):
    w_in, in_scale, w_out, out_scale = weights
    rows, piece = slab.shape
    slots = rows // PIECES
    width, ff = w_in.shape[2], w_out.shape[2]
    outs = [jax.ShapeDtypeStruct(slab.shape, jnp.bfloat16)]
    if layer + 1 < routes_t.shape[0]:
        outs.append(jax.ShapeDtypeStruct((1, *routes_t.shape[1:]), jnp.int32))
    return pl.pallas_call(
        functools.partial(expert_kernel, layer),
        in_specs=[VM] * 7,
        out_specs=[VM] * len(outs),
        out_shape=outs,
        scratch_shapes=[
            pltpu.VMEM((slots, width), jnp.bfloat16),
            pltpu.VMEM((slots, ff), jnp.bfloat16),
            pltpu.VMEM(slab.shape, jnp.bfloat16),
        ],
        compiler_params=pltpu.CompilerParams(vmem_limit_bytes=20 * MIB),
        cost_estimate=pl.CostEstimate(
            flops=6 * slots * width * ff,
            bytes_accessed=6 * width * ff + 4 * slots * width,
            transcendentals=slots * ff,
        ),
        name="expert",
    )(in_scale, out_scale, slab, w_in, w_out, routes_t, place)


def hbm(array):
    return pltpu.with_memory_space_constraint(array, pltpu.HBM)


def exchange(slab, devices):
    split = slab.reshape(devices, slab.shape[0] // devices, slab.shape[1])
    moved = lax.all_to_all(split, AXES, split_axis=0, concat_axis=0, tiled=True)
    return moved.reshape(slab.shape)


def shards(tokens, norm_gain, routes, gates, placement, w_in, in_scale, w_out, out_scale):
    count, width = tokens.shape
    layers, devices = placement.shape
    slots = devices * CAP
    piece = width // PIECES
    routes_t = jnp.swapaxes(routes, 1, 2)
    gates_t = jnp.swapaxes(gates, 1, 2)
    slab_type = jax.ShapeDtypeStruct((slots * PIECES, piece), jnp.bfloat16)
    stream_type = jax.ShapeDtypeStruct((count, width), jnp.bfloat16)
    mixed = pltpu.VMEM((count, PIECES, piece), jnp.float32)
    stack = pltpu.VMEM((slots * PIECES, piece), jnp.bfloat16)
    params = pltpu.CompilerParams(vmem_limit_bytes=12 * MIB)

    small = (
        pltpu.VMEM((count, width), jnp.bfloat16),
        pltpu.VMEM(norm_gain.shape, jnp.float32),
        pltpu.VMEM(routes_t.shape, jnp.int32),
        pltpu.VMEM(placement.shape, jnp.int32),
    )
    slab = pl.pallas_call(
        first_kernel,
        in_specs=[HB] * 4,
        out_specs=VM,
        out_shape=slab_type,
        scratch_shapes=[*small, stack, pltpu.SemaphoreType.DMA((4,))],
        compiler_params=params,
        cost_estimate=pl.CostEstimate(
            flops=8 * 10**9, bytes_accessed=8 * 10**6, transcendentals=0
        ),
        name="first",
    )(*[hbm(a) for a in (tokens, norm_gain, routes_t, placement)])
    weights = (
        w_in,
        jnp.transpose(in_scale, (0, 3, 1, 2)),
        w_out,
        jnp.transpose(out_scale, (0, 2, 1, 3)),
    )
    stream = tokens
    for layer in range(layers):
        answers, *numbers = expert(
            layer, exchange(slab, devices), weights, routes_t, placement
        )
        back = exchange(answers, devices)
        if layer + 1 < layers:
            slab, stream, weight = pl.pallas_call(
                functools.partial(middle_kernel, layer, layer == 0),
                in_specs=[VM] * 7,
                out_specs=(VM, VM, VM),
                out_shape=(
                    jax.ShapeDtypeStruct((slots, PIECES, piece), jnp.bfloat16),
                    jax.ShapeDtypeStruct((count * PIECES, piece), jnp.bfloat16),
                    jax.ShapeDtypeStruct((2 * count, slots), jnp.bfloat16),
                ),
                scratch_shapes=[
                    mixed,
                    pltpu.VMEM((PIECES, piece), jnp.float32),
                    pltpu.VMEM((count * PIECES, piece), jnp.bfloat16),
                    pltpu.VMEM(numbers[0].shape, jnp.int32),
                    pltpu.SMEM((2, *numbers[0].shape[1:]), jnp.int32),
                    pltpu.SMEM((1, *gates_t.shape[1:]), jnp.float32),
                    pltpu.SemaphoreType.DMA((3,)),
                ],
                compiler_params=params,
                name="middle",
            )(
                numbers[0], gates_t, back.reshape(slots, PIECES, piece), stream, norm_gain,
                routes_t, placement,
            )
            slab = slab.reshape(slots * PIECES, piece)
        else:
            stream = pl.pallas_call(
                last_kernel,
                in_specs=[VM] * 3,
                out_specs=VM,
                out_shape=stream_type,
                scratch_shapes=[
                    pltpu.VMEM((slots, width), jnp.bfloat16),
                    pltpu.VMEM((count, width), jnp.bfloat16),
                ],
                compiler_params=params,
                name="last",
            )(back, stream, weight)
    return stream


def solution(mesh):
    return jax.shard_map(
        shards,
        mesh=mesh,
        in_specs=(
            P(AXES, None),
            P(),
            P(None, AXES, None),
            P(None, AXES, None),
            P(),
            P(None, AXES, None, None),
            P(None, AXES, None, None),
            P(None, AXES, None, None),
            P(None, AXES, None, None),
        ),
        out_specs=P(AXES, None),
        check_vma=False,
    )
```
